32 devices in a mesh: groups: 2 (over x), tokens: 16 (over z, y, core).
Axes of the slice: x: 2, y: 2, z: 4, core: 2. Of those that a mesh axis runs over, the one named last changes fastest.
Arguments:
- update_keys: bfloat16 [16384, 2048], P(('groups', 'tokens')), parts along dimension 0, may hold values from -6 to 6
- update_values: bfloat16 [16384, 2048], P(('groups', 'tokens')), parts along dimension 0, may hold values from -6 to 6
- update_rates: float32 [16384, 4], P(('groups', 'tokens')), parts along dimension 0, may hold values from 0.05 to 1
- update_mask: int32 [16384], P(('groups', 'tokens')), parts along dimension 0, may hold values 0 or 1
- fast_weights: bfloat16 [4, 3, 512, 512], replicated, may hold values from -0.25 to 0.25
- step_sizes: float32 [4], replicated, may hold values from 0.02 to 0.08
- target_queries: bfloat16 [4096, 2048], P(('groups', 'tokens')), parts along dimension 0, may hold values from -8 to 8
- target_keys: bfloat16 [4096, 2048], P(('groups', 'tokens')), parts along dimension 0, may hold values from -8 to 8
- target_values: bfloat16 [4096, 2048], P(('groups', 'tokens')), parts along dimension 0, may hold values from -6 to 6
- target_views: int32 [4096], P(('groups', 'tokens')), parts along dimension 0, may hold values from 0 to 15, as said below
Outputs:
- mixed: bfloat16 [4096, 2048], P(('groups', 'tokens')), parts along dimension 0
The draws below stay inside these ranges and needn't reach their ends.
There are 2 independent parts, one for each index of `groups`. The reference program is written for one: setup_inputs(seed, part) draws one part's arguments, and reference() takes and returns one part's arrays. A program takes and returns all parts, laid end to end along the dimension named above; an argument that names none is the same for every part. Nothing has to cross between parts.
Inputs may be any that keep to these rules, and one draw needn't show every extreme that they name: `target_views`: every view id names exactly 128 rows. Owner o holds view o; of the 128 rows of one device, either none or exactly 16 belong to the view of one owner.
All inputs are finite; a program needn't handle non-finite values. No bound on the sum of `update_mask` on one device may be relied on, other than what follows from the above.
Results may differ from the reference program's by a relative error of at most 0.0083.
Values may be sent and summed in bfloat16 or wider, within the bound.
A program may use at most 128 MiB of HBM per device.

```python
import math
import jax
import jax.numpy as jnp
from jax import lax

HEADS = 4
DH = 512
VIEW_ROWS = 128
UPD_DEV = 512
VIEWS_DEV = 1
WIDTH = 2048
TGT_DEV = 128
CAP = 16
UPD_ROWS = 8192
TGT_ROWS = 2048
VIEWS = 16
N_TOKENS = 16


def view_layout(key):
    dev_count = TGT_ROWS // TGT_DEV
    half_count = dev_count // 2
    offsets = jax.random.permutation(jax.random.fold_in(key, 11), dev_count)[:half_count]
    source_dev = jnp.arange(dev_count, dtype=jnp.int32)[:, None]
    dest_pairs = (source_dev + offsets[None, :].astype(jnp.int32)) % dev_count
    dest_dev = jnp.repeat(dest_pairs, CAP, axis=1)
    incoming = jnp.broadcast_to(jnp.arange(TGT_DEV, dtype=jnp.int32)[None, :], (dev_count, TGT_DEV))
    arrival = jax.vmap(lambda sub_key: jax.random.permutation(sub_key, TGT_DEV))(jax.random.split(jax.random.fold_in(key, 12), dev_count))
    local_view = arrival[dest_dev, incoming].astype(jnp.int32) // VIEW_ROWS
    view_ids = dest_dev * VIEWS_DEV + local_view
    shuffle = jax.vmap(lambda sub_key: jax.random.permutation(sub_key, TGT_DEV))(jax.random.split(jax.random.fold_in(key, 13), dev_count))
    view_ids = jnp.take_along_axis(view_ids, shuffle.astype(jnp.int32), axis=1)
    return view_ids.reshape(-1).astype(jnp.int32)


def draw_target_views(key, part):
    return view_layout(key)


def drawn_pair(key):
    shape = (TGT_ROWS, WIDTH)
    queries = jnp.clip(jax.random.normal(jax.random.fold_in(key, 27), shape, jnp.float32), -4.0, 4.0)
    keys_out = jnp.clip(jax.random.normal(jax.random.fold_in(key, 28), shape, jnp.float32), -4.0, 4.0)
    return (queries, keys_out)


def draw_target_queries(key, part):
    return drawn_pair(key)[0].astype(jnp.bfloat16)


def draw_target_keys(key, part):
    return drawn_pair(key)[1].astype(jnp.bfloat16)


def touch_ends(result, stream_key, smallest, high):
    index_at = [jax.random.randint(jax.random.fold_in(stream_key, axis), (), 0, length) for axis, length in enumerate(result.shape)]
    main_axis = result.shape.index(max(result.shape))
    neighbour = index_at[:main_axis] + [(index_at[main_axis] + 1) % result.shape[main_axis]] + index_at[main_axis + 1:]
    return result.at[tuple(index_at)].set(smallest).at[tuple(neighbour)].set(high)


def raised(entries, key, source, target, shards_of, factor):
    def block_of(axis_at):
        return (jnp.arange(entries.shape[axis_at]) // (entries.shape[axis_at] // shards_of)).reshape((-1,) + (1,) * (entries.ndim - 1 - axis_at))

    near = jax.random.permutation(key, shards_of)[block_of(target)]
    far = (block_of(target) + shards_of // 2) % shards_of
    return jnp.where((block_of(source) == near) | (block_of(source) == far), factor * entries, entries)


def block_scale(key, shape, cuts, smallest, largest):
    def one(axis_at, shards_of):
        draws = jax.random.uniform(jax.random.fold_in(jax.random.fold_in(key, 6), axis_at), (shards_of,), jnp.float32, smallest / len(cuts), largest / len(cuts))
        return jnp.repeat(jnp.exp(draws), shape[axis_at] // shards_of).reshape((-1,) + (1,) * (len(shape) - axis_at - 1))

    level = one(*cuts[0])
    for cut in cuts[1:]:
        level = level * one(*cut)
    return level


def bell_draw(stream_key, dims, width, reach, pieces=(), held_as=jnp.bfloat16):
    entries = jax.random.normal(stream_key, dims, jnp.float32) * width
    if len(pieces) > 0:
        entries = block_scale(stream_key, dims, pieces, -0.22, 0.18) * entries
    return jnp.clip(entries, min=-reach, max=reach).astype(held_as)


def heavy_noise(stream_key, dims, deviation, limit, pieces, heavy, held_as=jnp.bfloat16):
    values = deviation * jax.random.normal(stream_key, dims, jnp.float32)
    if pieces:
        values = values * block_scale(stream_key, dims, pieces, -0.22, 0.18)
    return jnp.clip(raised(values, jax.random.fold_in(stream_key, 3), *heavy), -limit, limit).astype(held_as)


def setup_inputs(seed: int = 0, part: int = 0) -> dict:
    key_list = jax.random.split(jax.random.key(seed), 11)
    own_keys = jax.random.split(jax.random.fold_in(key_list[10], part), 11)
    update_keys = heavy_noise(own_keys[0], (UPD_ROWS, WIDTH), 1.0, 6.0, ((0, 16),), (0, 1, 16, 2.0))
    update_values = bell_draw(own_keys[1], (UPD_ROWS, WIDTH), 1.0, 6.0, ((0, 16),))
    update_rates = jnp.clip(jnp.exp(math.log(1.0) - 2.9957323 * jax.random.uniform(own_keys[2], (UPD_ROWS, HEADS), jnp.float32) ** block_scale(own_keys[2], (UPD_ROWS, HEADS), ((0, 16),), -0.2, 0.2)), 0.05, 1.0)
    update_mask = touch_ends((jax.random.randint(own_keys[3], (UPD_ROWS,), 0, 4) < 3).astype(jnp.int32), jax.random.fold_in(own_keys[3], 1), 0, 1)
    fast_weights = bell_draw(key_list[4], (HEADS, 3, DH, DH), DH ** -0.5, 0.25)
    step_sizes = jnp.clip(jnp.exp(jax.random.uniform(key_list[5], (HEADS,), jnp.float32, math.log(0.02), math.log(0.08))), 0.02, 0.08)
    target_queries = draw_target_queries(jax.random.fold_in(jax.random.fold_in(key_list[10], part), 71), part)
    target_keys = draw_target_keys(jax.random.fold_in(jax.random.fold_in(key_list[10], part), 71), part)
    target_values = bell_draw(own_keys[8], (TGT_ROWS, WIDTH), 1.0, 6.0, ((0, 16),))
    target_views = draw_target_views(jax.random.fold_in(jax.random.fold_in(key_list[10], part), 71), part)
    return dict(update_keys=update_keys, update_values=update_values, update_rates=update_rates, update_mask=update_mask, fast_weights=fast_weights, step_sizes=step_sizes, target_queries=target_queries, target_keys=target_keys, target_values=target_values, target_views=target_views)


epsilon = 1e-05
highest = lax.Precision.HIGHEST

def rounded(values):
    return lax.optimization_barrier(values.astype(jnp.bfloat16)).astype(jnp.float32)

def swish_parts(pre_gate):
    sigma = jax.nn.sigmoid(pre_gate)
    return (pre_gate * sigma, sigma * (1.0 + pre_gate * (1.0 - sigma)))

def row_normalize(matrix):
    return matrix * lax.rsqrt(lax.optimization_barrier(jnp.mean(matrix * matrix, axis=-1, keepdims=True)) + epsilon)

def reference(update_keys, update_values, update_rates, update_mask, fast_weights, step_sizes, target_queries, target_keys, target_values, target_views):
    weights = fast_weights.astype(jnp.float32)
    keep_rates = update_mask.astype(jnp.float32)[:, None] * update_rates

    def accumulate(block_index, grad_sum):
        first_row = (block_index * UPD_DEV).astype(jnp.int32)
        key_rows = lax.dynamic_slice_in_dim(update_keys, first_row, UPD_DEV, 0).astype(jnp.float32).reshape(UPD_DEV, HEADS, DH)
        value_rows = lax.dynamic_slice_in_dim(update_values, first_row, UPD_DEV, 0).astype(jnp.float32).reshape(UPD_DEV, HEADS, DH)
        rate_rows = lax.dynamic_slice_in_dim(keep_rates, first_row, UPD_DEV, 0)
        target_grad = rounded(-rate_rows[:, :, None] * value_rows)
        pre_gate = jnp.einsum('rhi,hij->rhj', key_rows, weights[:, 0], precision=highest)
        pre_up = jnp.einsum('rhi,hij->rhj', key_rows, weights[:, 1], precision=highest)
        activated, slope = swish_parts(pre_gate)
        hidden = rounded(activated * pre_up)
        back = jnp.einsum('rho,hjo->rhj', target_grad, weights[:, 2], precision=highest)
        grad_gate = rounded(back * pre_up * slope)
        grad_up = rounded(back * activated)
        gate_term = jnp.einsum('rhi,rhj->hij', key_rows, grad_gate, precision=highest)
        up_term = jnp.einsum('rhi,rhj->hij', key_rows, grad_up, precision=highest)
        down_term = jnp.einsum('rhj,rho->hjo', hidden, target_grad, precision=highest)
        return grad_sum + jnp.stack([gate_term, up_term, down_term], axis=1)
    gradient = lax.fori_loop(0, N_TOKENS, accumulate, jnp.zeros((HEADS, 3, DH, DH), jnp.float32))
    fresh = rounded(weights - step_sizes[:, None, None, None] * row_normalize(gradient))
    view_hit = (target_views[:, None] == jnp.arange(VIEWS, dtype=jnp.int32)[None, :]).astype(jnp.int32)
    within_view = lax.optimization_barrier(jnp.sum(view_hit * (jnp.cumsum(view_hit, axis=0) - 1), axis=1))
    position = (target_views * VIEW_ROWS + within_view).astype(jnp.int32)
    arranged = [jnp.zeros_like(source_rows).at[position].set(source_rows) for source_rows in (target_queries, target_keys, target_values)]
    query_rows = arranged[0].astype(jnp.float32).reshape(TGT_ROWS, HEADS, DH)
    pre_gate = jnp.einsum('rhi,hij->rhj', query_rows, fresh[:, 0], precision=highest)
    pre_up = jnp.einsum('rhi,hij->rhj', query_rows, fresh[:, 1], precision=highest)
    activated, slope = swish_parts(pre_gate)
    target_hidden = rounded(activated * pre_up)
    fast_out = jnp.einsum('rhj,hjo->rho', target_hidden, fresh[:, 2], precision=highest)
    normed = row_normalize(fast_out)
    view_shape = (VIEWS, VIEW_ROWS, HEADS, DH)
    view_queries = arranged[0].astype(jnp.float32).reshape(view_shape)
    view_keys = arranged[1].astype(jnp.float32).reshape(view_shape)
    view_values = arranged[2].astype(jnp.float32).reshape(view_shape)
    scores = jnp.einsum('vqhd,vkhd->vhqk', view_queries, view_keys, precision=highest) * DH ** (-0.5)
    probs = rounded(jax.nn.softmax(scores, axis=-1))
    attended = jnp.einsum('vhqk,vkhd->vqhd', probs, view_values, precision=highest).reshape(TGT_ROWS, HEADS, DH)
    return (normed + attended).reshape(TGT_ROWS, WIDTH).astype(jnp.bfloat16)
```

```python
import functools
import math

import jax
import jax.numpy as jnp
import numpy as np
from jax import lax
from jax.experimental import pallas as pl
from jax.experimental.pallas import tpu as pltpu
from jax.sharding import PartitionSpec as P

EPS = 1e-05
MESH = pl.DeviceIdType.MESH
F32 = jnp.float32
BF16 = jnp.bfloat16
LOWEST = -1e30


def remote(src, dst, send_sem, recv_sem, peer):
    return pltpu.make_async_remote_copy(
        src_ref=src,
        dst_ref=dst,
        send_sem=send_sem,
        recv_sem=recv_sem,
        device_id={"tokens": peer},
        device_id_type=MESH,
    )


def exchange_kernel(
    n,
    heads,
    keys_ref,
    values_ref,
    rates_ref,
    weights_ref,
    steps_ref,
    queries_ref,
    view_keys_ref,
    view_values_ref,
    views_ref,
    lanes_ref,
    out_ref,
    packed_ref,
    meta_ref,
    fresh_ref,
    got_ref,
    got_meta_ref,
    query_rows,
    attended,
    mixed,
    grad,
    core_out,
    core_in,
    side_out,
    side_in,
    up_out,
    up_in,
    down_out,
    down_in,
    a2a_send,
    a2a_recv,
    meta_send,
    meta_recv,
    pair_send,
    pair_recv,
    chain_send,
    chain_recv,
    spread_send,
    spread_recv,
    out_send,
    out_recv,
):
    width = weights_ref.shape[-1]
    rows = queries_ref.shape[0]
    quads = n // heads
    piece = 3 * width // quads
    slots = packed_ref.shape[1] // quads
    capacity = slots // heads
    me = lax.axis_index("tokens")
    quad = me // heads
    head = me % heads
    core = head % 2
    side = head // 2
    core_peer = me + 1 - 2 * core
    side_peer = me + 2 - 4 * side

    barrier = pltpu.get_barrier_semaphore()
    for step in range(1, n):
        pl.semaphore_signal(
            barrier, inc=1, device_id={"tokens": (me + step) % n}, device_id_type=MESH
        )

    owner = views_ref[0:1, :]
    hits = lax.broadcasted_iota(jnp.int32, (meta_ref.shape[1], rows), 0) == owner
    hits = hits.astype(F32).astype(BF16)
    earlier = (
        lax.broadcasted_iota(jnp.int32, (rows, rows), 0)
        < lax.broadcasted_iota(jnp.int32, (rows, rows), 1)
    ).astype(F32).astype(BF16)
    before = jnp.dot(hits, earlier, preferred_element_type=F32)
    rank = jnp.sum(hits.astype(F32) * before, axis=0, keepdims=True).astype(jnp.int32)
    meta_ref[...] = lax.dot_general(
        jnp.ones((meta_ref.shape[0], rows), BF16),
        hits,
        (((1,), (1,)), ((), ())),
        preferred_element_type=F32,
    )
    pick = (
        lax.broadcasted_iota(jnp.int32, (n * capacity, rows), 0) == owner * capacity + rank
    ).astype(F32).astype(BF16)
    for index, array in enumerate((queries_ref, view_keys_ref, view_values_ref)):
        packed_ref[index] = jnp.dot(pick, array[...], preferred_element_type=F32).astype(BF16)

    pl.semaphore_wait(barrier, n - 1)

    near = [step for step in range(1, n) if step % heads < 2]
    cross = [step for step in range(1, n) if step % heads >= 2]
    early = near[::-1]
    late = cross[::-1]

    def peer_of(step):
        place, total = me, 0
        unit = 1
        while unit < n:
            bit = place % 2
            total = total + unit * ((1 - bit) if (step // unit) % 2 else bit)
            place = place // 2
            unit *= 2
        return total

    def block_copy(step):
        peer = peer_of(step)
        rows = pl.ds(pl.multiple_of((peer // heads) * slots, slots), slots)
        columns = pl.ds(pl.multiple_of((peer % heads) * width, width), width)
        return remote(
            packed_ref.at[:, rows, columns],
            got_ref.at[me],
            a2a_send.at[step],
            a2a_recv.at[step],
            peer,
        )

    def meta_copy(step):
        peer = peer_of(step)
        return remote(
            meta_ref, got_meta_ref.at[me], meta_send.at[step], meta_recv.at[step], peer
        )

    for step in range(1, n):
        meta_copy(step).start()
    for step in early:
        block_copy(step).start()
    got_meta_ref[me] = meta_ref[...]
    got_ref[me] = packed_ref[
        :,
        pl.ds(pl.multiple_of(quad * slots, slots), slots),
        pl.ds(pl.multiple_of(head * width, width), width),
    ]

    def core_copy(slot):
        return remote(
            core_out.at[slot], core_in.at[slot], pair_send.at[slot], pair_recv.at[slot], core_peer
        )

    side_copy = remote(side_out, side_in, pair_send.at[2], pair_recv.at[2], side_peer)

    def one_head(turn, carry):
        on_side = jnp.where(turn < 2, 1 - side, side)
        on_core = jnp.where(turn % 2 == 0, 1 - core, core)
        now = on_side * 2 + on_core
        columns = pl.ds(pl.multiple_of(now * width, width), width)
        key_rows = keys_ref[:, columns]
        rates = rates_ref[...]
        lanes = lax.broadcasted_iota(jnp.int32, rates.shape, 1)
        rate = jnp.sum(jnp.where(lanes == now, rates, 0.0), axis=1, keepdims=True)
        target_grad = (-rate * values_ref[:, columns].astype(F32)).astype(BF16)
        pre_gate = jnp.dot(key_rows, weights_ref[now, 0], preferred_element_type=F32)
        pre_up = jnp.dot(key_rows, weights_ref[now, 1], preferred_element_type=F32)
        back = lax.dot_general(
            target_grad,
            weights_ref[now, 2],
            (((1,), (1,)), ((), ())),
            preferred_element_type=F32,
        )
        sigma = jax.nn.sigmoid(pre_gate)
        activated = pre_gate * sigma
        hidden = (activated * pre_up).astype(BF16)
        grad_gate = (back * pre_up * sigma * (1.0 + pre_gate * (1.0 - sigma))).astype(BF16)
        grad_up = (back * activated).astype(BF16)
        over_rows = (((0,), (0,)), ((), ()))
        grad[0:width] = lax.dot_general(
            key_rows, grad_gate, over_rows, preferred_element_type=F32
        )
        grad[width : 2 * width] = lax.dot_general(
            key_rows, grad_up, over_rows, preferred_element_type=F32
        )
        grad[2 * width : 3 * width] = lax.dot_general(
            hidden, target_grad, over_rows, preferred_element_type=F32
        )

        @pl.when(turn == 0)
        def _():
            core_out[0] = grad[...].astype(BF16)
            core_copy(0).start()

        @pl.when(turn == 1)
        def _():
            core_copy(0).wait_recv()
            side_out[...] = (grad[...] + core_in[0].astype(F32)).astype(BF16)
            side_copy.start()
            for step in late:
                block_copy(step).start()

        @pl.when(turn == 2)
        def _():
            core_out[1] = grad[...].astype(BF16)
            core_copy(1).start()

        return carry

    lax.fori_loop(0, 4, one_head, 0)
    core_copy(1).wait_recv()
    side_copy.wait_recv()

    def rows_of(index):
        return pl.ds(index * piece, piece)

    def own_part(rows):
        return grad[rows, :] + core_in[1, rows, :].astype(F32) + side_in[rows, :].astype(F32)

    def up_copy(index):
        return remote(
            up_out.at[index],
            up_in.at[index],
            chain_send.at[0, index],
            chain_recv.at[0, index],
            me + heads,
        )

    def down_copy(index):
        return remote(
            down_out.at[index],
            down_in.at[index],
            chain_send.at[1, index],
            chain_recv.at[1, index],
            me - heads,
        )

    def send_up(index):
        @pl.when(quad == 0)
        def _():
            up_out[index] = own_part(rows_of(index)).astype(BF16)
            up_copy(index).start()

        @pl.when((quad > 0) & (quad < index))
        def _():
            up_copy(index).wait_recv()
            up_out[index] = (own_part(rows_of(index)) + up_in[index].astype(F32)).astype(BF16)
            up_copy(index).start()

    def send_down(index):
        @pl.when(quad == quads - 1)
        def _():
            down_out[index] = own_part(rows_of(index)).astype(BF16)
            down_copy(index).start()

        @pl.when((quad < quads - 1) & (quad > index))
        def _():
            down_copy(index).wait_recv()
            down_out[index] = (own_part(rows_of(index)) + down_in[index].astype(F32)).astype(BF16)
            down_copy(index).start()

    @pl.when(2 * quad < quads)
    def _():
        for turn in range(quads - 1):
            send_up(quads - 1 - turn)
            send_down(turn)

    @pl.when(2 * quad >= quads)
    def _():
        for turn in range(quads - 1):
            send_down(turn)
            send_up(quads - 1 - turn)

    mine = pl.ds(pl.multiple_of(quad * piece, piece), piece)
    grad[mine, :] = own_part(mine)

    @pl.when(quad > 0)
    def _():
        up_copy(quad).wait_recv()
        grad[mine, :] += up_in[quad].astype(F32)

    @pl.when(quad < quads - 1)
    def _():
        down_copy(quad).wait_recv()
        grad[mine, :] += down_in[quad].astype(F32)

    total = grad[mine, :]
    scaled = total * lax.rsqrt(jnp.mean(total * total, axis=-1, keepdims=True) + EPS)
    first = quad * piece
    block = math.gcd(piece, width)
    for part in range(piece // block):
        start = first + part * block
        old = weights_ref[
            head, start // width, pl.ds(pl.multiple_of(start % width, block), block), :
        ]
        fresh_ref[quad, part * block : (part + 1) * block, :] = (
            old.astype(F32) - steps_ref[head] * scaled[part * block : (part + 1) * block, :]
        ).astype(BF16)

    def spread_copy(way, index):
        return remote(
            fresh_ref.at[index],
            fresh_ref.at[index],
            spread_send.at[way, index],
            spread_recv.at[index],
            me + heads if way == 0 else me - heads,
        )

    @pl.when(quad < quads - 1)
    def _():
        spread_copy(0, quad).start()

    @pl.when(quad > 0)
    def _():
        spread_copy(1, quad).start()

    for step in range(1, n):
        meta_copy(step).wait()
        block_copy(step).wait()
    lane_source, lane_view, lane_slot = (lanes_ref[i : i + 1, :] for i in range(3))
    lane_count = lanes_ref.shape[1]
    counts = got_meta_ref[:, 0, :].astype(BF16)
    sources = lax.broadcasted_iota(jnp.int32, (n, lane_count), 0)
    over_source = (((0,), (0,)), ((), ()))
    same = (sources == lane_source).astype(F32).astype(BF16)
    lower = (sources < lane_source).astype(F32).astype(BF16)
    owners = lax.broadcasted_iota(jnp.int32, (meta_ref.shape[1], lane_count), 0)
    wanted = owners == lane_view + quad * heads

    def lane_sum(table):
        found = lax.dot_general(counts, table, over_source, preferred_element_type=F32)
        return jnp.sum(jnp.where(wanted, found, 0.0), axis=0, keepdims=True).astype(jnp.int32)

    place_at = jnp.where(
        lane_slot < lane_sum(same), lane_view * rows + lane_sum(lower) + lane_slot, -1
    )
    place = (
        lax.broadcasted_iota(jnp.int32, (heads * rows, lane_count), 0) == place_at
    ).astype(F32).astype(BF16)
    arranged = [
        jnp.dot(
            place, got_ref[:, i].reshape(lane_count, width), preferred_element_type=F32
        ).astype(BF16)
        for i in range(3)
    ]
    for view in range(heads):
        part = slice(view * rows, (view + 1) * rows)
        scores = lax.dot_general(
            arranged[0][part], arranged[1][part], (((1,), (1,)), ((), ())),
            preferred_element_type=F32,
        ) * width ** (-0.5)
        powers = jnp.exp(scores - jnp.max(scores, axis=-1, keepdims=True))
        probs = (powers / jnp.sum(powers, axis=-1, keepdims=True)).astype(BF16)
        attended[part] = jnp.dot(probs, arranged[2][part], preferred_element_type=F32)
    query_rows[...] = arranged[0]

    for hop in range(1, quads):

        @pl.when(quad - hop >= 0)
        def _():
            index = quad - hop
            spread_copy(0, index).wait_recv()

            @pl.when(quad < quads - 1)
            def _():
                spread_copy(0, index).start()

        @pl.when(quad + hop < quads)
        def _():
            index = quad + hop
            spread_copy(1, index).wait_recv()

            @pl.when(quad > 0)
            def _():
                spread_copy(1, index).start()

    fresh = fresh_ref[...].reshape(3 * width, width)
    pre_gate = jnp.dot(query_rows[...], fresh[0:width], preferred_element_type=F32)
    pre_up = jnp.dot(query_rows[...], fresh[width : 2 * width], preferred_element_type=F32)
    target_hidden = (pre_gate * jax.nn.sigmoid(pre_gate) * pre_up).astype(BF16)
    fast_out = jnp.dot(target_hidden, fresh[2 * width :], preferred_element_type=F32)
    normed = fast_out * lax.rsqrt(jnp.mean(fast_out * fast_out, axis=-1, keepdims=True) + EPS)
    mixed[...] = (normed + attended[...]).astype(BF16).reshape(mixed.shape)
    own_columns = pl.ds(pl.multiple_of(head * width, width), width)

    def out_copy(step):
        view = (head + step) % heads
        return remote(
            mixed.at[view],
            out_ref.at[:, own_columns],
            out_send.at[step],
            out_recv.at[step],
            quad * heads + view,
        )

    for step in range(1, heads):
        out_copy(step).start()
    out_ref[:, own_columns] = mixed[head]
    for step in range(1, heads):
        out_copy(step).wait()

    core_copy(0).wait_send()
    core_copy(1).wait_send()
    side_copy.wait_send()
    for index in range(quads):

        @pl.when(quad < index)
        def _():
            up_copy(index).wait_send()

        @pl.when(quad > index)
        def _():
            down_copy(index).wait_send()

        @pl.when((index <= quad) & (quad < quads - 1))
        def _():
            spread_copy(0, index).wait_send()

        @pl.when((index >= quad) & (quad > 0))
        def _():
            spread_copy(1, index).wait_send()


def exchange(keys, values, rates, weights, steps, queries, view_keys, view_values, views):
    n = lax.axis_size("tokens")
    heads = weights.shape[0]
    width = weights.shape[-1]
    rows = queries.shape[0]
    quads = n // heads
    piece = 3 * width // quads
    capacity = 2 * rows // n
    slots = heads * capacity
    owner_lanes = -(-n // 128) * 128
    lane = np.arange(n * slots)
    lanes = np.zeros((8, n * slots), np.int32)
    lanes[0] = lane // slots
    lanes[1] = lane % slots // capacity
    lanes[2] = lane % capacity
    vmem = pl.BlockSpec(memory_space=pltpu.VMEM)
    smem = pl.BlockSpec(memory_space=pltpu.SMEM)
    dma = pltpu.SemaphoreType.DMA
    whole = (3 * width, width)
    parts = (quads, piece, width)
    return pl.pallas_call(
        functools.partial(exchange_kernel, n, heads),
        out_shape=jax.ShapeDtypeStruct((rows, heads * width), BF16),
        in_specs=[vmem, vmem, vmem, vmem, smem] + [vmem] * 5,
        out_specs=vmem,
        scratch_shapes=[
            pltpu.VMEM((3, n * capacity, heads * width), BF16),
            pltpu.VMEM((8, owner_lanes), F32),
            pltpu.VMEM(parts, BF16),
            pltpu.VMEM((n, 3, slots, width), BF16),
            pltpu.VMEM((n, 8, owner_lanes), F32),
            pltpu.VMEM((heads * rows, width), BF16),
            pltpu.VMEM((heads * rows, width), F32),
            pltpu.VMEM((heads, rows, width), BF16),
            pltpu.VMEM(whole, F32),
            pltpu.VMEM((2,) + whole, BF16),
            pltpu.VMEM((2,) + whole, BF16),
            pltpu.VMEM(whole, BF16),
            pltpu.VMEM(whole, BF16),
            pltpu.VMEM(parts, BF16),
            pltpu.VMEM(parts, BF16),
            pltpu.VMEM(parts, BF16),
            pltpu.VMEM(parts, BF16),
            dma((n,)),
            dma((n,)),
            dma((n,)),
            dma((n,)),
            dma((3,)),
            dma((3,)),
            dma((2, quads)),
            dma((2, quads)),
            dma((2, quads)),
            dma((quads,)),
            dma((heads,)),
            dma((heads,)),
        ],
        compiler_params=pltpu.CompilerParams(
            collective_id=0, has_side_effects=True, vmem_limit_bytes=63 * 1024 * 1024
        ),
    )(keys, values, rates, weights, steps, queries, view_keys, view_values, views, jnp.asarray(lanes))


def scene_kernel(
    n,
    heads,
    keys_ref,
    values_ref,
    rates_ref,
    mask_ref,
    weights_ref,
    steps_ref,
    queries_ref,
    view_keys_ref,
    view_values_ref,
    views_ref,
    out_ref,
    key_buf,
    value_buf,
    weight_buf,
    target_grad,
    hidden,
    grad_gate,
    grad_up,
    grad,
    core_out,
    core_in,
    side_out,
    side_in,
    own,
    chain_out,
    chain_in,
    fresh_ref,
    got_q,
    got_kv,
    views_out,
    got_views,
    rank_q,
    rank_kv,
    counts,
    place_q,
    place_kv,
    arranged_q,
    arranged_kv,
    attended,
    part_out,
    part_in,
    stats_out,
    stats_in,
    mixed,
    load_sem,
    local_sem,
    z_send,
    z_recv,
    y_send,
    y_recv,
    c_send,
    c_recv,
    cy_send,
    cy_recv,
    core_send,
    core_recv,
    side_send,
    side_recv,
    chain_send,
    chain_recv,
    fresh_send,
    fresh_recv,
    part_send,
    part_recv,
    out_send,
    out_recv,
):
    width = out_ref.shape[1] // heads
    rows = out_ref.shape[0]
    planes = n // heads
    piece = 3 * width // heads
    me = lax.axis_index("tokens")
    z, p = me // heads, me % heads
    y, c = p // 2, p % 2
    core_peer = me + 1 - 2 * c
    side_peer = me + 2 - 4 * y
    low = 2 * z < planes
    ahead = jnp.where(low, me + heads, me - heads)
    behind = jnp.where(low, me - heads, me + heads)
    is_end = (z == 0) | (z == planes - 1)

    def plane_of(step):
        return (z + step) % planes

    barrier = pltpu.get_barrier_semaphore()
    for peer in [core_peer, side_peer] + [
        plane_of(step) * heads + p for step in range(1, planes)
    ]:
        pl.semaphore_signal(barrier, inc=1, device_id={"tokens": peer}, device_id_type=MESH)

    def head_at(turn):
        at_mid = jnp.where(turn == 0, 3, jnp.where(turn == 1, 0, 4 - turn))
        place = jnp.where(is_end, 3 - turn, at_mid)
        return jnp.where(low, place, 3 - place)

    def columns(head):
        return pl.ds(pl.multiple_of(head * width, width), width)

    def loads(turn):
        head = head_at(turn)
        return (
            pltpu.make_async_copy(keys_ref.at[:, columns(head)], key_buf.at[turn], load_sem.at[0, turn]),
            pltpu.make_async_copy(weights_ref.at[head], weight_buf.at[turn], load_sem.at[1, turn]),
            pltpu.make_async_copy(values_ref.at[:, columns(head)], value_buf.at[turn], load_sem.at[2, turn]),
        )

    for turn in range(heads):
        for load in loads(turn):
            load.start()

    views_out[...] = jnp.broadcast_to(views_ref[...], views_out.shape)
    here = p * planes + z
    kv_here = c * planes + z
    locals_ = (
        pltpu.make_async_copy(queries_ref.at[:, columns(z)], got_q.at[here], local_sem.at[0]),
        pltpu.make_async_copy(view_keys_ref.at[:, columns(z)], got_kv.at[0, kv_here], local_sem.at[1]),
        pltpu.make_async_copy(view_values_ref.at[:, columns(z)], got_kv.at[1, kv_here], local_sem.at[2]),
    )
    for copy in locals_:
        copy.start()
    got_views[here] = views_out[...]

    pl.semaphore_wait(barrier, planes + 1)

    def z_copy(step, index):
        plane = plane_of(step)
        source, target = (
            (queries_ref.at[:, columns(plane)], got_q.at[here]),
            (view_keys_ref.at[:, columns(plane)], got_kv.at[0, kv_here]),
            (view_values_ref.at[:, columns(plane)], got_kv.at[1, kv_here]),
            (views_out, got_views.at[here]),
        )[index]
        return remote(
            source, target, z_send.at[index, step], z_recv.at[index, step], plane * heads + p
        )

    def source_plane(step):
        return (z + planes - step) % planes

    def y_copy(step, index):
        slot = p * planes + source_plane(step)
        if index == 0:
            source = queries_ref.at[:, columns(z)] if step == 0 else got_q.at[slot]
            target = got_q.at[slot]
        else:
            source = views_out if step == 0 else got_views.at[slot]
            target = got_views.at[slot]
        return remote(source, target, y_send.at[index, step], y_recv.at[index, step], side_peer)

    def c_copy(step, index):
        slot = p * planes + source_plane(step)
        kv_slot = c * planes + source_plane(step)
        target = (
            got_q.at[slot], got_kv.at[0, kv_slot], got_kv.at[1, kv_slot], got_views.at[slot]
        )[index]
        if step == 0:
            source = (
                queries_ref.at[:, columns(z)],
                view_keys_ref.at[:, columns(z)],
                view_values_ref.at[:, columns(z)],
                views_out,
            )[index]
        else:
            source = target
        return remote(source, target, c_send.at[index, step], c_recv.at[index, step], core_peer)

    def cy_copy(step, index):
        slot = (2 * (1 - y) + c) * planes + source_plane(step)
        target = got_q.at[slot] if index == 0 else got_views.at[slot]
        return remote(target, target, cy_send.at[index, step], cy_recv.at[index, step], core_peer)

    for index in (3, 0, 1, 2):
        for step in range(1, planes):
            z_copy(step, index).start()
    for index in range(2):
        y_copy(0, index).start()
    for index in range(4):
        c_copy(0, index).start()

    def core_copy(turn):
        return remote(
            core_out.at[turn], core_in.at[turn], core_send.at[turn], core_recv.at[turn], core_peer
        )

    def side_copy(turn):
        return remote(
            side_out.at[turn], side_in.at[turn], side_send.at[turn], side_recv.at[turn], side_peer
        )

    def quarter(at_y, at_c):
        return pl.ds(pl.multiple_of((2 * at_y + at_c) * piece, piece), piece)

    def take_core(turn):
        core_copy(turn).wait_recv()
        side_out[turn] = (
            grad[quarter(1 - y, c), :] + core_in[turn, 1 - y].astype(F32)
        ).astype(BF16)
        side_copy(turn).start()
        own[turn] = grad[quarter(y, c), :] + core_in[turn, y].astype(F32)

    eye = lax.broadcasted_iota(jnp.int32, (rows, rows), 0) == lax.broadcasted_iota(
        jnp.int32, (rows, rows), 1
    )

    def to_column(row):
        parts = [
            jnp.sum(jnp.where(eye, row[:, at : at + rows], 0.0), axis=1, keepdims=True)
            for at in range(0, row.shape[1], rows)
        ]
        return parts[0] if len(parts) == 1 else jnp.concatenate(parts, axis=0)

    def to_row(column):
        return jnp.sum(jnp.where(eye, column, 0.0), axis=0, keepdims=True)

    over_rows = (((0,), (0,)), ((), ()))
    over_last = (((1,), (1,)), ((), ()))

    def one_head(turn, carry):
        for load in loads(turn):
            load.wait()
        rate = to_column(rates_ref[pl.ds(head_at(turn), 1), :] * mask_ref[...].astype(F32))
        key_rows = key_buf[turn]
        target_grad[...] = (-rate * value_buf[turn].astype(F32)).astype(BF16)
        pre_gate = jnp.dot(key_rows, weight_buf[turn, 0], preferred_element_type=F32)
        pre_up = jnp.dot(key_rows, weight_buf[turn, 1], preferred_element_type=F32)
        back = lax.dot_general(
            target_grad[...], weight_buf[turn, 2], over_last, preferred_element_type=F32
        )
        sigma = jax.nn.sigmoid(pre_gate)
        activated = pre_gate * sigma
        hidden[...] = (activated * pre_up).astype(BF16)
        grad_gate[...] = (back * pre_up * sigma * (1.0 + pre_gate * (1.0 - sigma))).astype(BF16)
        grad_up[...] = (back * activated).astype(BF16)

        @pl.when(turn > 0)
        def _():
            take_core(turn - 1)

        grad[0:width] = lax.dot_general(
            key_buf[turn], grad_gate[...], over_rows, preferred_element_type=F32
        )
        grad[width : 2 * width] = lax.dot_general(
            key_buf[turn], grad_up[...], over_rows, preferred_element_type=F32
        )
        grad[2 * width : 3 * width] = lax.dot_general(
            hidden[...], target_grad[...], over_rows, preferred_element_type=F32
        )
        for at_y in range(2):
            core_out[turn, at_y] = grad[quarter(at_y, 1 - c), :].astype(BF16)
        core_copy(turn).start()

        @pl.when(turn == 2)
        def _():
            for step in range(1, planes):
                for index in (0, 3):
                    z_copy(step, index).wait_recv()
                y_copy(step, 0).start()
                y_copy(step, 1).start()
                c_copy(step, 0).start()
                c_copy(step, 3).start()

        return carry

    lax.fori_loop(0, heads, one_head, 0)
    take_core(heads - 1)

    def chain_copy(out_slot, in_slot, peer):
        return remote(
            chain_out.at[out_slot],
            chain_in.at[in_slot],
            chain_send.at[out_slot],
            chain_recv.at[in_slot],
            peer,
        )

    hops = ((0, 3, ahead), (3, 5, behind), (1, 4, ahead))

    def pass_on(turn):
        side_copy(turn).wait_recv()

        @pl.when(is_end)
        def _():
            chain_out[turn] = (own[turn] + side_in[turn].astype(F32)).astype(BF16)
            chain_copy(turn, turn, ahead).start()

        @pl.when(jnp.logical_not(is_end))
        def _():
            taken, given, peer = hops[turn]
            chain_copy(turn, taken, peer).wait_recv()
            chain_out[turn] = (
                own[turn] + side_in[turn].astype(F32) + chain_in[taken].astype(F32)
            ).astype(BF16)
            chain_copy(turn, given, peer).start()

    pass_on(0)

    for step in range(planes):
        for index in range(2):
            y_copy(step, index).wait_recv()
            cy_copy(step, index).start()

    pass_on(1)

    locals_[0].wait()
    for step in range(planes):
        for index in range(2):
            cy_copy(step, index).wait_recv()
        c_copy(step, 0).wait_recv()
        c_copy(step, 3).wait_recv()

    views = 2 * planes
    square = (n * views, n * views)
    low_axis = lax.broadcasted_iota(jnp.int32, square, 0)
    high_axis = lax.broadcasted_iota(jnp.int32, square, 1)

    def order(index):
        slot = index // views
        return slot % planes * heads + slot // planes

    def ones(where):
        return where.astype(F32).astype(BF16)

    listed = low_axis % views
    side_of = jnp.where(listed < planes, y, 1 - y)
    wanted = listed % planes * heads + 2 * side_of + c
    is_hit = got_views[...].reshape(n * views, rows) == wanted[:, :rows]
    hits = ones(is_hit)
    within = jnp.dot(
        hits,
        ones(
            lax.broadcasted_iota(jnp.int32, (rows, rows), 0)
            < lax.broadcasted_iota(jnp.int32, (rows, rows), 1)
        ),
        preferred_element_type=F32,
    )
    before = (low_axis % views == high_axis % views) & (order(high_axis) < order(low_axis))
    in_column = high_axis // (views * n // 2) == y

    def earlier(table):
        found = jnp.dot(ones(table), hits, preferred_element_type=F32)
        return jnp.sum(found, axis=1, keepdims=True)

    rank_q[...] = jnp.where(is_hit, earlier(before) + within, -1.0).reshape(rank_q.shape)
    rank_kv[...] = jnp.where(is_hit, earlier(before & in_column) + within, -1.0).reshape(
        rank_kv.shape
    )
    counts[...] = jnp.broadcast_to(
        earlier(((low_axis % views == high_axis % views) & in_column)[0:views]), counts.shape
    )

    def spots(ranks, first, sources, view):
        row = jnp.concatenate(
            [ranks[first + source, view : view + 1, :] for source in range(sources)], axis=1
        )
        at = lax.broadcasted_iota(jnp.int32, (rows, sources * rows), 0).astype(F32)
        return ones(at == row)

    def arrange_q(group):
        for view in range(planes):
            place_q[view * rows : (view + 1) * rows] = spots(rank_q, 0, n, group * planes + view)
        arranged_q[group] = jnp.dot(
            place_q[...], got_q[...].reshape(n * rows, width), preferred_element_type=F32
        ).astype(BF16)

    def arrange_kv(group):
        for view in range(planes):
            place_kv[view * rows : (view + 1) * rows] = spots(
                rank_kv, y * (n // 2), n // 2, group * planes + view
            )
        for index in range(2):
            arranged_kv[index] = jnp.dot(
                place_kv[...],
                got_kv[index].reshape(n // 2 * rows, width),
                preferred_element_type=F32,
            ).astype(BF16)

    def attend(group, view):
        part = slice(view * rows, (view + 1) * rows)
        scores = lax.dot_general(
            arranged_q[group, part], arranged_kv[0, part], over_last, preferred_element_type=F32
        ) * width ** (-0.5)
        at = group * planes + view
        real = lax.broadcasted_iota(jnp.int32, (rows, rows), 1).astype(F32) < counts[at : at + 1, :]
        top = jnp.max(jnp.where(real, scores, LOWEST), axis=-1, keepdims=True)
        powers = jnp.where(real, jnp.exp(jnp.where(real, scores - top, 0.0)), 0.0)
        total = jnp.sum(powers, axis=-1, keepdims=True)
        result = jnp.dot(powers.astype(BF16), arranged_kv[1, part], preferred_element_type=F32)
        return top, total, result

    arrange_q(1)
    arrange_q(0)

    pass_on(2)

    for step in range(1, planes):
        for index in (1, 2):
            z_copy(step, index).wait_recv()
            c_copy(step, index).start()
    locals_[1].wait()
    locals_[2].wait()
    for step in range(planes):
        for index in (1, 2):
            c_copy(step, index).wait_recv()

    arrange_kv(1)
    for view in range(planes):
        top, total, result = attend(1, view)
        part_out[view] = result.astype(BF16)
        stats_out[view : view + 1, :] = to_row(top)
        stats_out[planes + view : planes + view + 1, :] = to_row(total)

    part_copy = remote(part_out, part_in, part_send.at[0], part_recv.at[0], side_peer)
    stats_copy = remote(stats_out, stats_in, part_send.at[1], part_recv.at[1], side_peer)
    part_copy.start()
    stats_copy.start()

    last = heads - 1
    side_copy(last).wait_recv()
    own[last] += side_in[last].astype(F32)

    @pl.when(is_end)
    def _():
        chain_copy(0, 5, ahead).wait_recv()
        own[last] += chain_in[5].astype(F32)

    @pl.when(jnp.logical_not(is_end))
    def _():
        for slot in (2, 4):
            chain_copy(0, slot, ahead).wait_recv()
            own[last] += chain_in[slot].astype(F32)

    gradient = own[last]
    scaled = gradient * lax.rsqrt(jnp.mean(gradient * gradient, axis=-1, keepdims=True) + EPS)
    block = math.gcd(piece, width)
    for part in range(piece // block):
        start = p * piece + part * block
        old = weight_buf[
            last, start // width, pl.ds(pl.multiple_of(start % width, block), block), :
        ]
        fresh_ref[p, part * block : (part + 1) * block, :] = (
            old.astype(F32) - steps_ref[z] * scaled[part * block : (part + 1) * block, :]
        ).astype(BF16)

    def fresh_copy(index):
        slot = 2 * (1 - y) + c if index == 2 else p
        return remote(
            fresh_ref.at[slot],
            fresh_ref.at[slot],
            fresh_send.at[index],
            fresh_recv.at[index],
            side_peer if index == 0 else core_peer,
        )

    fresh_copy(0).start()
    fresh_copy(1).start()

    arrange_kv(0)
    tops, totals = [], []
    for view in range(planes):
        top, total, result = attend(0, view)
        tops.append(top)
        totals.append(total)
        attended[view] = result

    fresh_copy(0).wait_recv()
    fresh_copy(2).start()
    fresh_copy(1).wait_recv()
    fresh_copy(2).wait_recv()

    fresh = fresh_ref[...].reshape(3 * width, width)
    query_rows = arranged_q[0]
    pre_gate = jnp.dot(query_rows, fresh[0:width], preferred_element_type=F32)
    pre_up = jnp.dot(query_rows, fresh[width : 2 * width], preferred_element_type=F32)
    target_hidden = (pre_gate * jax.nn.sigmoid(pre_gate) * pre_up).astype(BF16)
    fast_out = jnp.dot(target_hidden, fresh[2 * width :], preferred_element_type=F32)
    normed = fast_out * lax.rsqrt(jnp.mean(fast_out * fast_out, axis=-1, keepdims=True) + EPS)

    part_copy.wait_recv()
    stats_copy.wait_recv()
    for view in range(planes):
        other_top = to_column(stats_in[view : view + 1, :])
        other_total = to_column(stats_in[planes + view : planes + view + 1, :])
        top = jnp.maximum(tops[view], other_top)
        scale, other_scale = jnp.exp(tops[view] - top), jnp.exp(other_top - top)
        weight = 1.0 / (scale * totals[view] + other_scale * other_total)
        mixed[view] = (
            normed[view * rows : (view + 1) * rows]
            + attended[view] * (scale * weight)
            + part_in[view].astype(F32) * (other_scale * weight)
        ).astype(BF16)

    def out_copy(step):
        plane = plane_of(step)
        return remote(
            mixed.at[plane],
            out_ref.at[:, columns(z)],
            out_send.at[step],
            out_recv.at[step],
            plane * heads + p,
        )

    for step in range(1, planes):
        out_copy(step).start()
    out_ref[:, columns(z)] = mixed[z]
    for step in range(1, planes):
        out_copy(step).wait()

    part_copy.wait_send()
    stats_copy.wait_send()
    for index in range(3):
        fresh_copy(index).wait_send()
        chain_copy(index, 0, ahead).wait_send()
    for turn in range(heads):
        core_copy(turn).wait_send()
        side_copy(turn).wait_send()
    for step in range(planes):
        for index in range(4):
            c_copy(step, index).wait_send()
            if step > 0:
                z_copy(step, index).wait_send()
        for index in range(2):
            y_copy(step, index).wait_send()
            cy_copy(step, index).wait_send()


def scene(keys, values, rates, mask, weights, steps, queries, view_keys, view_values, views):
    n = lax.axis_size("tokens")
    heads, _, _, width = weights.shape
    rows = queries.shape[0]
    depth = keys.shape[0]
    planes = n // heads
    piece = 3 * width // heads
    slots = 2 * planes
    vmem = pl.BlockSpec(memory_space=pltpu.VMEM)
    smem = pl.BlockSpec(memory_space=pltpu.SMEM)
    hbm = pl.BlockSpec(memory_space=pl.ANY)
    dma = pltpu.SemaphoreType.DMA

    def half(*shape):
        return pltpu.VMEM(shape, BF16)

    def single(*shape):
        return pltpu.VMEM(shape, F32)

    return pl.pallas_call(
        functools.partial(scene_kernel, n, heads),
        out_shape=jax.ShapeDtypeStruct((rows, heads * width), BF16),
        in_specs=[hbm, hbm, vmem, vmem, hbm, smem, hbm, hbm, hbm, vmem],
        out_specs=vmem,
        scratch_shapes=[
            half(heads, depth, width),
            half(heads, depth, width),
            half(heads, 3, width, width),
            half(depth, width),
            half(depth, width),
            half(depth, width),
            half(depth, width),
            single(3 * width, width),
            half(heads, 2, piece, width),
            half(heads, 2, piece, width),
            half(heads, piece, width),
            half(heads, piece, width),
            single(heads, piece, width),
            half(3, piece, width),
            half(6, piece, width),
            half(heads, piece, width),
            half(n, rows, width),
            half(2, n // 2, rows, width),
            pltpu.VMEM((slots, rows), jnp.int32),
            pltpu.VMEM((n, slots, rows), jnp.int32),
            single(n, slots, rows),
            single(n, slots, rows),
            single(slots, rows),
            half(planes * rows, n * rows),
            half(planes * rows, n // 2 * rows),
            half(2, planes * rows, width),
            half(2, planes * rows, width),
            single(planes, rows, width),
            half(planes, rows, width),
            half(planes, rows, width),
            single(slots, rows),
            single(slots, rows),
            half(planes, rows, width),
            dma((3, heads)),
            dma((3,)),
            dma((4, planes)),
            dma((4, planes)),
            dma((2, planes)),
            dma((2, planes)),
            dma((4, planes)),
            dma((4, planes)),
            dma((2, planes)),
            dma((2, planes)),
            dma((heads,)),
            dma((heads,)),
            dma((heads,)),
            dma((heads,)),
            dma((3,)),
            dma((6,)),
            dma((3,)),
            dma((3,)),
            dma((2,)),
            dma((2,)),
            dma((planes,)),
            dma((planes,)),
        ],
        compiler_params=pltpu.CompilerParams(
            collective_id=1, has_side_effects=True, vmem_limit_bytes=63 * 1024 * 1024
        ),
    )(keys, values, rates, mask, weights, steps, queries, view_keys, view_values, views)


def on_device(
    update_keys,
    update_values,
    update_rates,
    update_mask,
    fast_weights,
    step_sizes,
    target_queries,
    target_keys,
    target_values,
    target_views,
):
    n = lax.axis_size("tokens")
    heads = fast_weights.shape[0]
    if heads == 4 and n == heads * heads:
        return scene(
            update_keys,
            update_values,
            update_rates.T,
            update_mask[None, :],
            fast_weights,
            step_sizes,
            target_queries,
            target_keys,
            target_values,
            target_views[None, :],
        )
    rates = update_rates * update_mask.astype(F32)[:, None]
    return exchange(
        update_keys,
        update_values,
        rates,
        fast_weights,
        step_sizes,
        target_queries,
        target_keys,
        target_values,
        target_views[None, :],
    )


def solution(mesh):
    rows = P(("groups", "tokens"), None)
    flat = P(("groups", "tokens"))
    return jax.shard_map(
        on_device,
        mesh=mesh,
        in_specs=(rows, rows, rows, flat, P(), P(), rows, rows, rows, flat),
        out_specs=rows,
        check_vma=False,
    )
```

```python
import functools
import math

import jax
import jax.numpy as jnp
import numpy as np
from jax import lax
from jax.experimental import pallas as pl
from jax.experimental.pallas import tpu as pltpu
from jax.sharding import PartitionSpec as P

EPS = 1e-05
MESH = pl.DeviceIdType.MESH
F32 = jnp.float32
BF16 = jnp.bfloat16
LOWEST = -1e30


def remote(src, dst, send_sem, recv_sem, peer):
    return pltpu.make_async_remote_copy(
        src_ref=src,
        dst_ref=dst,
        send_sem=send_sem,
        recv_sem=recv_sem,
        device_id={"tokens": peer},
        device_id_type=MESH,
    )


def exchange_kernel(
    n,
    heads,
    keys_ref,
    values_ref,
    rates_ref,
    weights_ref,
    steps_ref,
    queries_ref,
    view_keys_ref,
    view_values_ref,
    views_ref,
    lanes_ref,
    out_ref,
    packed_ref,
    meta_ref,
    fresh_ref,
    got_ref,
    got_meta_ref,
    query_rows,
    attended,
    mixed,
    grad,
    core_out,
    core_in,
    side_out,
    side_in,
    up_out,
    up_in,
    down_out,
    down_in,
    a2a_send,
    a2a_recv,
    meta_send,
    meta_recv,
    pair_send,
    pair_recv,
    chain_send,
    chain_recv,
    spread_send,
    spread_recv,
    out_send,
    out_recv,
):
    width = weights_ref.shape[-1]
    rows = queries_ref.shape[0]
    quads = n // heads
    piece = 3 * width // quads
    slots = packed_ref.shape[1] // quads
    capacity = slots // heads
    me = lax.axis_index("tokens")
    quad = me // heads
    head = me % heads
    core = head % 2
    side = head // 2
    core_peer = me + 1 - 2 * core
    side_peer = me + 2 - 4 * side

    barrier = pltpu.get_barrier_semaphore()
    for step in range(1, n):
        pl.semaphore_signal(
            barrier, inc=1, device_id={"tokens": (me + step) % n}, device_id_type=MESH
        )

    owner = views_ref[0:1, :]
    hits = lax.broadcasted_iota(jnp.int32, (meta_ref.shape[1], rows), 0) == owner
    hits = hits.astype(F32).astype(BF16)
    earlier = (
        lax.broadcasted_iota(jnp.int32, (rows, rows), 0)
        < lax.broadcasted_iota(jnp.int32, (rows, rows), 1)
    ).astype(F32).astype(BF16)
    before = jnp.dot(hits, earlier, preferred_element_type=F32)
    rank = jnp.sum(hits.astype(F32) * before, axis=0, keepdims=True).astype(jnp.int32)
    meta_ref[...] = lax.dot_general(
        jnp.ones((meta_ref.shape[0], rows), BF16),
        hits,
        (((1,), (1,)), ((), ())),
        preferred_element_type=F32,
    )
    pick = (
        lax.broadcasted_iota(jnp.int32, (n * capacity, rows), 0) == owner * capacity + rank
    ).astype(F32).astype(BF16)
    for index, array in enumerate((queries_ref, view_keys_ref, view_values_ref)):
        packed_ref[index] = jnp.dot(pick, array[...], preferred_element_type=F32).astype(BF16)

    pl.semaphore_wait(barrier, n - 1)

    near = [step for step in range(1, n) if step % heads < 2]
    cross = [step for step in range(1, n) if step % heads >= 2]
    early = near[::-1]
    late = cross[::-1]

    def peer_of(step):
        place, total = me, 0
        unit = 1
        while unit < n:
            bit = place % 2
            total = total + unit * ((1 - bit) if (step // unit) % 2 else bit)
            place = place // 2
            unit *= 2
        return total

    def block_copy(step):
        peer = peer_of(step)
        rows = pl.ds(pl.multiple_of((peer // heads) * slots, slots), slots)
        columns = pl.ds(pl.multiple_of((peer % heads) * width, width), width)
        return remote(
            packed_ref.at[:, rows, columns],
            got_ref.at[me],
            a2a_send.at[step],
            a2a_recv.at[step],
            peer,
        )

    def meta_copy(step):
        peer = peer_of(step)
        return remote(
            meta_ref, got_meta_ref.at[me], meta_send.at[step], meta_recv.at[step], peer
        )

    for step in range(1, n):
        meta_copy(step).start()
    for step in early:
        block_copy(step).start()
    got_meta_ref[me] = meta_ref[...]
    got_ref[me] = packed_ref[
        :,
        pl.ds(pl.multiple_of(quad * slots, slots), slots),
        pl.ds(pl.multiple_of(head * width, width), width),
    ]

    def core_copy(slot):
        return remote(
            core_out.at[slot], core_in.at[slot], pair_send.at[slot], pair_recv.at[slot], core_peer
        )

    side_copy = remote(side_out, side_in, pair_send.at[2], pair_recv.at[2], side_peer)

    def one_head(turn, carry):
        on_side = jnp.where(turn < 2, 1 - side, side)
        on_core = jnp.where(turn % 2 == 0, 1 - core, core)
        now = on_side * 2 + on_core
        columns = pl.ds(pl.multiple_of(now * width, width), width)
        key_rows = keys_ref[:, columns]
        rates = rates_ref[...]
        lanes = lax.broadcasted_iota(jnp.int32, rates.shape, 1)
        rate = jnp.sum(jnp.where(lanes == now, rates, 0.0), axis=1, keepdims=True)
        target_grad = (-rate * values_ref[:, columns].astype(F32)).astype(BF16)
        pre_gate = jnp.dot(key_rows, weights_ref[now, 0], preferred_element_type=F32)
        pre_up = jnp.dot(key_rows, weights_ref[now, 1], preferred_element_type=F32)
        back = lax.dot_general(
            target_grad,
            weights_ref[now, 2],
            (((1,), (1,)), ((), ())),
            preferred_element_type=F32,
        )
        sigma = jax.nn.sigmoid(pre_gate)
        activated = pre_gate * sigma
        hidden = (activated * pre_up).astype(BF16)
        grad_gate = (back * pre_up * sigma * (1.0 + pre_gate * (1.0 - sigma))).astype(BF16)
        grad_up = (back * activated).astype(BF16)
        over_rows = (((0,), (0,)), ((), ()))
        grad[0:width] = lax.dot_general(
            key_rows, grad_gate, over_rows, preferred_element_type=F32
        )
        grad[width : 2 * width] = lax.dot_general(
            key_rows, grad_up, over_rows, preferred_element_type=F32
        )
        grad[2 * width : 3 * width] = lax.dot_general(
            hidden, target_grad, over_rows, preferred_element_type=F32
        )

        @pl.when(turn == 0)
        def _():
            core_out[0] = grad[...].astype(BF16)
            core_copy(0).start()

        @pl.when(turn == 1)
        def _():
            core_copy(0).wait_recv()
            side_out[...] = (grad[...] + core_in[0].astype(F32)).astype(BF16)
            side_copy.start()
            for step in late:
                block_copy(step).start()

        @pl.when(turn == 2)
        def _():
            core_out[1] = grad[...].astype(BF16)
            core_copy(1).start()

        return carry

    lax.fori_loop(0, 4, one_head, 0)
    core_copy(1).wait_recv()
    side_copy.wait_recv()

    def rows_of(index):
        return pl.ds(index * piece, piece)

    def own_part(rows):
        return grad[rows, :] + core_in[1, rows, :].astype(F32) + side_in[rows, :].astype(F32)

    def up_copy(index):
        return remote(
            up_out.at[index],
            up_in.at[index],
            chain_send.at[0, index],
            chain_recv.at[0, index],
            me + heads,
        )

    def down_copy(index):
        return remote(
            down_out.at[index],
            down_in.at[index],
            chain_send.at[1, index],
            chain_recv.at[1, index],
            me - heads,
        )

    def send_up(index):
        @pl.when(quad == 0)
        def _():
            up_out[index] = own_part(rows_of(index)).astype(BF16)
            up_copy(index).start()

        @pl.when((quad > 0) & (quad < index))
        def _():
            up_copy(index).wait_recv()
            up_out[index] = (own_part(rows_of(index)) + up_in[index].astype(F32)).astype(BF16)
            up_copy(index).start()

    def send_down(index):
        @pl.when(quad == quads - 1)
        def _():
            down_out[index] = own_part(rows_of(index)).astype(BF16)
            down_copy(index).start()

        @pl.when((quad < quads - 1) & (quad > index))
        def _():
            down_copy(index).wait_recv()
            down_out[index] = (own_part(rows_of(index)) + down_in[index].astype(F32)).astype(BF16)
            down_copy(index).start()

    @pl.when(2 * quad < quads)
    def _():
        for turn in range(quads - 1):
            send_up(quads - 1 - turn)
            send_down(turn)

    @pl.when(2 * quad >= quads)
    def _():
        for turn in range(quads - 1):
            send_down(turn)
            send_up(quads - 1 - turn)

    mine = pl.ds(pl.multiple_of(quad * piece, piece), piece)
    grad[mine, :] = own_part(mine)

    @pl.when(quad > 0)
    def _():
        up_copy(quad).wait_recv()
        grad[mine, :] += up_in[quad].astype(F32)

    @pl.when(quad < quads - 1)
    def _():
        down_copy(quad).wait_recv()
        grad[mine, :] += down_in[quad].astype(F32)

    total = grad[mine, :]
    scaled = total * lax.rsqrt(jnp.mean(total * total, axis=-1, keepdims=True) + EPS)
    first = quad * piece
    block = math.gcd(piece, width)
    for part in range(piece // block):
        start = first + part * block
        old = weights_ref[
            head, start // width, pl.ds(pl.multiple_of(start % width, block), block), :
        ]
        fresh_ref[quad, part * block : (part + 1) * block, :] = (
            old.astype(F32) - steps_ref[head] * scaled[part * block : (part + 1) * block, :]
        ).astype(BF16)

    def spread_copy(way, index):
        return remote(
            fresh_ref.at[index],
            fresh_ref.at[index],
            spread_send.at[way, index],
            spread_recv.at[index],
            me + heads if way == 0 else me - heads,
        )

    @pl.when(quad < quads - 1)
    def _():
        spread_copy(0, quad).start()

    @pl.when(quad > 0)
    def _():
        spread_copy(1, quad).start()

    for step in range(1, n):
        meta_copy(step).wait()
        block_copy(step).wait()
    lane_source, lane_view, lane_slot = (lanes_ref[i : i + 1, :] for i in range(3))
    lane_count = lanes_ref.shape[1]
    counts = got_meta_ref[:, 0, :].astype(BF16)
    sources = lax.broadcasted_iota(jnp.int32, (n, lane_count), 0)
    over_source = (((0,), (0,)), ((), ()))
    same = (sources == lane_source).astype(F32).astype(BF16)
    lower = (sources < lane_source).astype(F32).astype(BF16)
    owners = lax.broadcasted_iota(jnp.int32, (meta_ref.shape[1], lane_count), 0)
    wanted = owners == lane_view + quad * heads

    def lane_sum(table):
        found = lax.dot_general(counts, table, over_source, preferred_element_type=F32)
        return jnp.sum(jnp.where(wanted, found, 0.0), axis=0, keepdims=True).astype(jnp.int32)

    place_at = jnp.where(
        lane_slot < lane_sum(same), lane_view * rows + lane_sum(lower) + lane_slot, -1
    )
    place = (
        lax.broadcasted_iota(jnp.int32, (heads * rows, lane_count), 0) == place_at
    ).astype(F32).astype(BF16)
    arranged = [
        jnp.dot(
            place, got_ref[:, i].reshape(lane_count, width), preferred_element_type=F32
        ).astype(BF16)
        for i in range(3)
    ]
    for view in range(heads):
        part = slice(view * rows, (view + 1) * rows)
        scores = lax.dot_general(
            arranged[0][part], arranged[1][part], (((1,), (1,)), ((), ())),
            preferred_element_type=F32,
        ) * width ** (-0.5)
        powers = jnp.exp(scores - jnp.max(scores, axis=-1, keepdims=True))
        probs = (powers / jnp.sum(powers, axis=-1, keepdims=True)).astype(BF16)
        attended[part] = jnp.dot(probs, arranged[2][part], preferred_element_type=F32)
    query_rows[...] = arranged[0]

    for hop in range(1, quads):

        @pl.when(quad - hop >= 0)
        def _():
            index = quad - hop
            spread_copy(0, index).wait_recv()

            @pl.when(quad < quads - 1)
            def _():
                spread_copy(0, index).start()

        @pl.when(quad + hop < quads)
        def _():
            index = quad + hop
            spread_copy(1, index).wait_recv()

            @pl.when(quad > 0)
            def _():
                spread_copy(1, index).start()

    fresh = fresh_ref[...].reshape(3 * width, width)
    pre_gate = jnp.dot(query_rows[...], fresh[0:width], preferred_element_type=F32)
    pre_up = jnp.dot(query_rows[...], fresh[width : 2 * width], preferred_element_type=F32)
    target_hidden = (pre_gate * jax.nn.sigmoid(pre_gate) * pre_up).astype(BF16)
    fast_out = jnp.dot(target_hidden, fresh[2 * width :], preferred_element_type=F32)
    normed = fast_out * lax.rsqrt(jnp.mean(fast_out * fast_out, axis=-1, keepdims=True) + EPS)
    mixed[...] = (normed + attended[...]).astype(BF16).reshape(mixed.shape)
    own_columns = pl.ds(pl.multiple_of(head * width, width), width)

    def out_copy(step):
        view = (head + step) % heads
        return remote(
            mixed.at[view],
            out_ref.at[:, own_columns],
            out_send.at[step],
            out_recv.at[step],
            quad * heads + view,
        )

    for step in range(1, heads):
        out_copy(step).start()
    out_ref[:, own_columns] = mixed[head]
    for step in range(1, heads):
        out_copy(step).wait()

    core_copy(0).wait_send()
    core_copy(1).wait_send()
    side_copy.wait_send()
    for index in range(quads):

        @pl.when(quad < index)
        def _():
            up_copy(index).wait_send()

        @pl.when(quad > index)
        def _():
            down_copy(index).wait_send()

        @pl.when((index <= quad) & (quad < quads - 1))
        def _():
            spread_copy(0, index).wait_send()

        @pl.when((index >= quad) & (quad > 0))
        def _():
            spread_copy(1, index).wait_send()


def exchange(keys, values, rates, weights, steps, queries, view_keys, view_values, views):
    n = lax.axis_size("tokens")
    heads = weights.shape[0]
    width = weights.shape[-1]
    rows = queries.shape[0]
    quads = n // heads
    piece = 3 * width // quads
    capacity = 2 * rows // n
    slots = heads * capacity
    owner_lanes = -(-n // 128) * 128
    lane = np.arange(n * slots)
    lanes = np.zeros((8, n * slots), np.int32)
    lanes[0] = lane // slots
    lanes[1] = lane % slots // capacity
    lanes[2] = lane % capacity
    vmem = pl.BlockSpec(memory_space=pltpu.VMEM)
    smem = pl.BlockSpec(memory_space=pltpu.SMEM)
    dma = pltpu.SemaphoreType.DMA
    whole = (3 * width, width)
    parts = (quads, piece, width)
    return pl.pallas_call(
        functools.partial(exchange_kernel, n, heads),
        out_shape=jax.ShapeDtypeStruct((rows, heads * width), BF16),
        in_specs=[vmem, vmem, vmem, vmem, smem] + [vmem] * 5,
        out_specs=vmem,
        scratch_shapes=[
            pltpu.VMEM((3, n * capacity, heads * width), BF16),
            pltpu.VMEM((8, owner_lanes), F32),
            pltpu.VMEM(parts, BF16),
            pltpu.VMEM((n, 3, slots, width), BF16),
            pltpu.VMEM((n, 8, owner_lanes), F32),
            pltpu.VMEM((heads * rows, width), BF16),
            pltpu.VMEM((heads * rows, width), F32),
            pltpu.VMEM((heads, rows, width), BF16),
            pltpu.VMEM(whole, F32),
            pltpu.VMEM((2,) + whole, BF16),
            pltpu.VMEM((2,) + whole, BF16),
            pltpu.VMEM(whole, BF16),
            pltpu.VMEM(whole, BF16),
            pltpu.VMEM(parts, BF16),
            pltpu.VMEM(parts, BF16),
            pltpu.VMEM(parts, BF16),
            pltpu.VMEM(parts, BF16),
            dma((n,)),
            dma((n,)),
            dma((n,)),
            dma((n,)),
            dma((3,)),
            dma((3,)),
            dma((2, quads)),
            dma((2, quads)),
            dma((2, quads)),
            dma((quads,)),
            dma((heads,)),
            dma((heads,)),
        ],
        compiler_params=pltpu.CompilerParams(
            collective_id=0, has_side_effects=True, vmem_limit_bytes=63 * 1024 * 1024
        ),
    )(keys, values, rates, weights, steps, queries, view_keys, view_values, views, jnp.asarray(lanes))


def scene_kernel(
    n,
    heads,
    keys_ref,
    values_ref,
    rates_ref,
    mask_ref,
    weights_ref,
    steps_ref,
    queries_ref,
    view_keys_ref,
    view_values_ref,
    views_ref,
    out_ref,
    key_buf,
    value_buf,
    weight_buf,
    target_grad,
    hidden,
    grad_gate,
    grad_up,
    grad,
    core_out,
    core_in,
    side_out,
    side_in,
    own,
    chain_out,
    chain_in,
    fresh_ref,
    got_q,
    got_kv,
    views_out,
    got_views,
    rank_q,
    rank_kv,
    counts,
    place_q,
    place_kv,
    arranged_q,
    arranged_kv,
    powers,
    attended,
    part_out,
    part_in,
    stats_out,
    stats_in,
    mixed,
    normed,
    load_sem,
    local_sem,
    z_send,
    z_recv,
    y_send,
    y_recv,
    c_send,
    c_recv,
    cy_send,
    cy_recv,
    core_send,
    core_recv,
    side_send,
    side_recv,
    chain_send,
    chain_recv,
    fresh_send,
    fresh_recv,
    part_send,
    part_recv,
    out_send,
    out_recv,
):
    width = out_ref.shape[1] // heads
    rows = out_ref.shape[0]
    planes = n // heads
    piece = 3 * width // heads
    me = lax.axis_index("tokens")
    z, p = me // heads, me % heads
    y, c = p // 2, p % 2
    core_peer = me + 1 - 2 * c
    side_peer = me + 2 - 4 * y
    low = 2 * z < planes
    ahead = jnp.where(low, me + heads, me - heads)
    behind = jnp.where(low, me - heads, me + heads)
    is_end = (z == 0) | (z == planes - 1)

    def plane_of(step):
        return (z + step) % planes

    barrier = pltpu.get_barrier_semaphore()
    for peer in [core_peer, side_peer] + [
        plane_of(step) * heads + p for step in range(1, planes)
    ]:
        pl.semaphore_signal(barrier, inc=1, device_id={"tokens": peer}, device_id_type=MESH)

    def head_at(turn):
        at_mid = jnp.where(turn == 0, 3, jnp.where(turn == 1, 0, 4 - turn))
        place = jnp.where(is_end, 3 - turn, at_mid)
        return jnp.where(low, place, 3 - place)

    def columns(head):
        return pl.ds(pl.multiple_of(head * width, width), width)

    def loads(turn):
        head = head_at(turn)
        return (
            pltpu.make_async_copy(keys_ref.at[:, columns(head)], key_buf.at[turn], load_sem.at[0, turn]),
            pltpu.make_async_copy(weights_ref.at[head], weight_buf.at[turn], load_sem.at[1, turn]),
            pltpu.make_async_copy(values_ref.at[:, columns(head)], value_buf.at[turn], load_sem.at[2, turn]),
        )

    for turn in range(heads):
        for load in loads(turn):
            load.start()

    views_out[...] = jnp.broadcast_to(views_ref[...], views_out.shape)
    here = p * planes + z
    kv_here = c * planes + z
    locals_ = (
        pltpu.make_async_copy(queries_ref.at[:, columns(z)], got_q.at[here], local_sem.at[0]),
        pltpu.make_async_copy(view_keys_ref.at[:, columns(z)], got_kv.at[0, kv_here], local_sem.at[1]),
        pltpu.make_async_copy(view_values_ref.at[:, columns(z)], got_kv.at[1, kv_here], local_sem.at[2]),
    )
    for copy in locals_:
        copy.start()
    got_views[here] = views_out[...]

    pl.semaphore_wait(barrier, planes + 1)

    def z_copy(turn, index):
        plane = head_at(turn)
        source, target = (
            (queries_ref.at[:, columns(plane)], got_q.at[here]),
            (view_keys_ref.at[:, columns(plane)], got_kv.at[0, kv_here]),
            (view_values_ref.at[:, columns(plane)], got_kv.at[1, kv_here]),
            (views_out, got_views.at[here]),
        )[index]
        return remote(
            source, target, z_send.at[index, turn], z_recv.at[index, z], plane * heads + p
        )

    def z_arrived(step, index):
        source, target = ((queries_ref.at[:, columns(z)], got_q.at[here]), (views_out, got_views.at[here]))[
            index == 3
        ]
        remote(
            source, target, z_send.at[index, 0], z_recv.at[index, plane_of(step)], core_peer
        ).wait_recv()

    def y_copy(step, index):
        slot = p * planes + plane_of(step)
        if index == 0:
            source = queries_ref.at[:, columns(z)] if step == 0 else got_q.at[slot]
            target = got_q.at[slot]
        else:
            source = views_out if step == 0 else got_views.at[slot]
            target = got_views.at[slot]
        return remote(source, target, y_send.at[index, step], y_recv.at[index, step], side_peer)

    def c_copy(step, index):
        slot = p * planes + plane_of(step)
        kv_slot = c * planes + plane_of(step)
        target = (
            got_q.at[slot], got_kv.at[0, kv_slot], got_kv.at[1, kv_slot], got_views.at[slot]
        )[index]
        if step == 0:
            source = (
                queries_ref.at[:, columns(z)],
                view_keys_ref.at[:, columns(z)],
                view_values_ref.at[:, columns(z)],
                views_out,
            )[index]
        else:
            source = target
        return remote(source, target, c_send.at[index, step], c_recv.at[index, step], core_peer)

    def cy_copy(step, index):
        slot = (2 * (1 - y) + c) * planes + plane_of(step)
        target = got_q.at[slot] if index == 0 else got_views.at[slot]
        return remote(target, target, cy_send.at[index, step], cy_recv.at[index, step], core_peer)

    for index in (3, 0, 1):
        for turn in range(heads - 1):
            z_copy(turn, index).start()

    @pl.when(jnp.logical_not(is_end))
    def _():
        for turn in range(heads - 1):
            z_copy(turn, 2).start()

    for index in (1, 0):
        y_copy(0, index).start()
    for index in (3, 0, 1, 2):
        c_copy(0, index).start()

    def core_copy(turn):
        return remote(
            core_out.at[turn], core_in.at[turn], core_send.at[turn], core_recv.at[turn], core_peer
        )

    chunk = math.gcd(piece, width)
    chunks = piece // chunk

    def chunk_rows(index):
        return slice(index * chunk, (index + 1) * chunk)

    def side_copy(turn, index):
        at = chunk_rows(index)
        return remote(
            side_out.at[turn, at],
            side_in.at[turn, at],
            side_send.at[turn, index],
            side_recv.at[turn, index],
            side_peer,
        )

    def quarter(at_y, at_c):
        return pl.ds(pl.multiple_of((2 * at_y + at_c) * piece, piece), piece)

    def take_core(turn):
        core_copy(turn).wait_recv()
        side_out[turn] = (
            grad[quarter(1 - y, c), :] + core_in[turn, 1 - y].astype(F32)
        ).astype(BF16)
        for index in range(chunks):
            side_copy(turn, index).start()
        own[turn] = grad[quarter(y, c), :] + core_in[turn, y].astype(F32)

    eye = lax.broadcasted_iota(jnp.int32, (rows, rows), 0) == lax.broadcasted_iota(
        jnp.int32, (rows, rows), 1
    )

    def to_column(row):
        parts = [
            jnp.sum(jnp.where(eye, row[:, at : at + rows], 0.0), axis=1, keepdims=True)
            for at in range(0, row.shape[1], rows)
        ]
        return parts[0] if len(parts) == 1 else jnp.concatenate(parts, axis=0)

    def to_row(column):
        return jnp.sum(jnp.where(eye, column, 0.0), axis=0, keepdims=True)

    over_rows = (((0,), (0,)), ((), ()))
    over_last = (((1,), (1,)), ((), ()))

    def one_head(turn, carry):
        for load in loads(turn):
            load.wait()
        rate = to_column(rates_ref[pl.ds(head_at(turn), 1), :] * mask_ref[...].astype(F32))
        key_rows = key_buf[turn]
        target_grad[...] = (-rate * value_buf[turn].astype(F32)).astype(BF16)
        pre_gate = jnp.dot(key_rows, weight_buf[turn, 0], preferred_element_type=F32)
        pre_up = jnp.dot(key_rows, weight_buf[turn, 1], preferred_element_type=F32)
        back = lax.dot_general(
            target_grad[...], weight_buf[turn, 2], over_last, preferred_element_type=F32
        )
        sigma = jax.nn.sigmoid(pre_gate)
        activated = pre_gate * sigma
        hidden[...] = (activated * pre_up).astype(BF16)
        grad_gate[...] = (back * pre_up * sigma * (1.0 + pre_gate * (1.0 - sigma))).astype(BF16)
        grad_up[...] = (back * activated).astype(BF16)

        @pl.when(turn > 0)
        def _():
            take_core(turn - 1)

        grad[0:width] = lax.dot_general(
            key_buf[turn], grad_gate[...], over_rows, preferred_element_type=F32
        )
        grad[width : 2 * width] = lax.dot_general(
            key_buf[turn], grad_up[...], over_rows, preferred_element_type=F32
        )
        grad[2 * width : 3 * width] = lax.dot_general(
            hidden[...], target_grad[...], over_rows, preferred_element_type=F32
        )
        for at_y in range(2):
            core_out[turn, at_y] = grad[quarter(at_y, 1 - c), :].astype(BF16)
        core_copy(turn).start()

        @pl.when(turn == 1)
        def _():
            for step in range(1, planes):
                z_arrived(step, 3)
                y_copy(step, 1).start()
                c_copy(step, 3).start()

        return carry

    lax.fori_loop(0, heads, one_head, 0)
    take_core(heads - 1)

    for step in range(1, planes):
        z_arrived(step, 0)
        y_copy(step, 0).start()
        c_copy(step, 0).start()

    def chain_copy(out_slot, in_slot, index, peer):
        at = chunk_rows(index)
        return remote(
            chain_out.at[out_slot, at],
            chain_in.at[in_slot, at],
            chain_send.at[out_slot, index],
            chain_recv.at[in_slot, index],
            peer,
        )

    hops = ((0, 3, ahead), (3, 5, behind), (1, 4, ahead))

    def pass_on(turn, index):
        side_copy(turn, index).wait_recv()
        at = chunk_rows(index)

        @pl.when(is_end)
        def _():
            chain_out[turn, at] = (own[turn, at] + side_in[turn, at].astype(F32)).astype(BF16)
            chain_copy(turn, turn, index, ahead).start()

        @pl.when(jnp.logical_not(is_end))
        def _():
            taken, given, peer = hops[turn]
            chain_copy(turn, taken, index, peer).wait_recv()
            chain_out[turn, at] = (
                own[turn, at] + side_in[turn, at].astype(F32) + chain_in[taken, at].astype(F32)
            ).astype(BF16)
            chain_copy(turn, given, index, peer).start()

    views = 2 * planes
    def ones(where):
        return where.astype(F32).astype(BF16)

    def rank_rows():
        square = (n * views, n * views)
        low_axis = lax.broadcasted_iota(jnp.int32, square, 0)
        high_axis = lax.broadcasted_iota(jnp.int32, square, 1)

        def order(index):
            slot = index // views
            return slot % planes * heads + slot // planes

        listed = low_axis % views
        side_of = jnp.where(listed < planes, y, 1 - y)
        wanted = listed % planes * heads + 2 * side_of + c
        is_hit = got_views[...].reshape(n * views, rows) == wanted[:, :rows]
        hits = ones(is_hit)
        within = jnp.dot(
            hits,
            ones(
                lax.broadcasted_iota(jnp.int32, (rows, rows), 0)
                < lax.broadcasted_iota(jnp.int32, (rows, rows), 1)
            ),
            preferred_element_type=F32,
        )
        before = (low_axis % views == high_axis % views) & (order(high_axis) < order(low_axis))
        in_column = high_axis // (views * n // 2) == y

        def earlier(table):
            found = jnp.dot(ones(table), hits, preferred_element_type=F32)
            return jnp.sum(found, axis=1, keepdims=True)

        rank_q[...] = jnp.where(is_hit, earlier(before) + within, -1.0).reshape(rank_q.shape)
        rank_kv[...] = jnp.where(is_hit, earlier(before & in_column) + within, -1.0).reshape(
            rank_kv.shape
        )
        counts[...] = jnp.broadcast_to(
            earlier(((low_axis % views == high_axis % views) & in_column)[0:views]), counts.shape
        )

    def spots(ranks, first, sources, view):
        row = jnp.concatenate(
            [ranks[first + source, view : view + 1, :] for source in range(sources)], axis=1
        )
        at = lax.broadcasted_iota(jnp.int32, (rows, sources * rows), 0).astype(F32)
        return ones(at == row)

    def spot_q(group):
        for view in range(planes):
            place_q[group, view * rows : (view + 1) * rows] = spots(
                rank_q, 0, n, group * planes + view
            )

    def arrange_q(group):
        arranged_q[group] = jnp.dot(
            place_q[group], got_q[...].reshape(n * rows, width), preferred_element_type=F32
        ).astype(BF16)

    def spot_kv(group):
        for view in range(planes):
            place_kv[group, view * rows : (view + 1) * rows] = spots(
                rank_kv, y * (n // 2), n // 2, group * planes + view
            )

    def arrange_kv(group, index):
        arranged_kv[group, index] = jnp.dot(
            place_kv[group],
            got_kv[index].reshape(n // 2 * rows, width),
            preferred_element_type=F32,
        ).astype(BF16)

    def view_rows(view):
        return pl.ds(pl.multiple_of(view * rows, rows), rows)

    def weigh(group, turn):
        view = head_at(turn)
        part = view_rows(view)
        scores = lax.dot_general(
            arranged_q[group, part], arranged_kv[group, 0, part], over_last, preferred_element_type=F32
        ) * width ** (-0.5)
        at = group * planes + view
        real = lax.broadcasted_iota(jnp.int32, (rows, rows), 1).astype(F32) < counts[pl.ds(at, 1), :]
        top = jnp.max(jnp.where(real, scores, LOWEST), axis=-1, keepdims=True)
        exps = jnp.where(real, jnp.exp(jnp.where(real, scores - top, 0.0)), 0.0)
        powers[group, turn] = exps.astype(BF16)
        return top, jnp.sum(exps, axis=-1, keepdims=True)

    def attend(group, turn):
        return jnp.dot(
            powers[group, turn],
            arranged_kv[group, 1, view_rows(head_at(turn))],
            preferred_element_type=F32,
        )

    def part_copy(turn, index):
        view = head_at(turn)
        source, target = ((part_out, part_in), (stats_out, stats_in))[index]
        return remote(
            source.at[view],
            target.at[view],
            part_send.at[index, turn],
            part_recv.at[index, turn],
            side_peer,
        )

    pass_on(0, 0)
    for step in range(planes):
        y_copy(step, 1).wait_recv()
        cy_copy(step, 1).start()
    pass_on(0, 1)
    for step in range(planes):
        cy_copy(step, 1).wait_recv()
        c_copy(step, 3).wait_recv()
    rank_rows()
    pass_on(0, 2)
    spot_q(1)
    pass_on(1, 0)
    spot_q(0)
    pass_on(1, 1)
    spot_kv(1)
    pass_on(1, 2)
    spot_kv(0)
    for index in range(chunks):
        pass_on(2, index)

    @pl.when(is_end)
    def _():
        for turn in range(heads - 1):
            z_copy(turn, 2).start()

    for step in range(1, planes):
        z_arrived(step, 1)
        c_copy(step, 1).start()

    last = heads - 1

    def fresh_copy(way, index):
        slot = 2 * (1 - y) + c if way == 2 else p
        at = chunk_rows(index)
        return remote(
            fresh_ref.at[slot, at],
            fresh_ref.at[slot, at],
            fresh_send.at[way, index],
            fresh_recv.at[way, index],
            side_peer if way == 0 else core_peer,
        )

    for index in range(chunks):
        at = chunk_rows(index)
        side_copy(last, index).wait_recv()
        own[last, at] += side_in[last, at].astype(F32)

        @pl.when(is_end)
        def _():
            chain_copy(0, 5, index, ahead).wait_recv()
            own[last, at] += chain_in[5, at].astype(F32)

        @pl.when(jnp.logical_not(is_end))
        def _():
            for slot in (2, 4):
                chain_copy(0, slot, index, ahead).wait_recv()
            own[last, at] += chain_in[2, at].astype(F32) + chain_in[4, at].astype(F32)

        gradient = own[last, at]
        scaled = gradient * lax.rsqrt(jnp.mean(gradient * gradient, axis=-1, keepdims=True) + EPS)
        start = p * piece + index * chunk
        old = weight_buf[
            last, start // width, pl.ds(pl.multiple_of(start % width, chunk), chunk), :
        ]
        fresh_ref[p, at, :] = (old.astype(F32) - steps_ref[z] * scaled).astype(BF16)
        fresh_copy(0, index).start()
        fresh_copy(1, index).start()

    for step in range(planes):
        y_copy(step, 0).wait_recv()
        cy_copy(step, 0).start()
    locals_[0].wait()
    locals_[1].wait()
    for step in range(planes):
        c_copy(step, 1).wait_recv()
    arrange_kv(1, 0)
    arrange_kv(0, 0)
    for step in range(planes):
        cy_copy(step, 0).wait_recv()
        c_copy(step, 0).wait_recv()
    arrange_q(1)
    for turn in range(heads):
        view = head_at(turn)
        top, total = weigh(1, turn)
        stats_out[view, 0:1, :] = to_row(top)
        stats_out[view, 1:2, :] = to_row(total)
        part_copy(turn, 1).start()
    arrange_q(0)
    tops, totals = [], []
    for turn in range(heads):
        top, total = weigh(0, turn)
        tops.append(top)
        totals.append(total)

    for step in range(1, planes):
        z_arrived(step, 2)
        c_copy(step, 2).start()
    locals_[2].wait()
    for step in range(planes):
        c_copy(step, 2).wait_recv()
    arrange_kv(1, 1)
    for turn in range(heads):
        part_out[head_at(turn)] = attend(1, turn).astype(BF16)
        part_copy(turn, 0).start()
    arrange_kv(0, 1)
    for turn in range(heads):
        attended[turn] = attend(0, turn)

    for index in range(chunks):
        fresh_copy(0, index).wait_recv()
        fresh_copy(2, index).start()
    for index in range(chunks):
        fresh_copy(1, index).wait_recv()
        fresh_copy(2, index).wait_recv()

    fresh = fresh_ref[...].reshape(3 * width, width)
    query_rows = arranged_q[0]
    pre_gate = jnp.dot(query_rows, fresh[0:width], preferred_element_type=F32)
    pre_up = jnp.dot(query_rows, fresh[width : 2 * width], preferred_element_type=F32)
    target_hidden = (pre_gate * jax.nn.sigmoid(pre_gate) * pre_up).astype(BF16)
    fast_out = jnp.dot(target_hidden, fresh[2 * width :], preferred_element_type=F32)
    normed[...] = fast_out * lax.rsqrt(
        jnp.mean(fast_out * fast_out, axis=-1, keepdims=True) + EPS
    )

    def out_copy(turn, plane, source):
        return remote(
            mixed.at[turn],
            out_ref.at[:, columns(source)],
            out_send.at[turn],
            out_recv.at[source],
            plane * heads + p,
        )

    for turn in range(heads):
        view = head_at(turn)
        for index in range(2):
            part_copy(turn, index).wait_recv()
        other_top = to_column(stats_in[view, 0:1, :])
        other_total = to_column(stats_in[view, 1:2, :])
        top = jnp.maximum(tops[turn], other_top)
        scale, other_scale = jnp.exp(tops[turn] - top), jnp.exp(other_top - top)
        weight = 1.0 / (scale * totals[turn] + other_scale * other_total)
        result = (
            normed[pl.ds(pl.multiple_of(view * rows, rows), rows)]
            + attended[turn] * (scale * weight)
            + part_in[view].astype(F32) * (other_scale * weight)
        ).astype(BF16)
        if turn < last:
            mixed[turn] = result
            out_copy(turn, view, z).start()
        else:
            out_ref[:, columns(z)] = result

    for step in range(1, planes):
        out_copy(0, z, plane_of(step)).wait_recv()
    for turn in range(last):
        out_copy(turn, z, z).wait_send()
        for index in range(chunks):
            chain_copy(turn, 0, index, ahead).wait_send()
            fresh_copy(turn, index).wait_send()
    for turn in range(heads):
        core_copy(turn).wait_send()
        for index in range(2):
            part_copy(turn, index).wait_send()
        for index in range(chunks):
            side_copy(turn, index).wait_send()
    for step in range(planes):
        for index in range(4):
            c_copy(step, index).wait_send()
            if step < last:
                z_copy(step, index).wait_send()
        for index in range(2):
            y_copy(step, index).wait_send()
            cy_copy(step, index).wait_send()


def scene(keys, values, rates, mask, weights, steps, queries, view_keys, view_values, views):
    n = lax.axis_size("tokens")
    heads, _, _, width = weights.shape
    rows = queries.shape[0]
    depth = keys.shape[0]
    planes = n // heads
    piece = 3 * width // heads
    chunks = piece // math.gcd(piece, width)
    slots = 2 * planes
    vmem = pl.BlockSpec(memory_space=pltpu.VMEM)
    smem = pl.BlockSpec(memory_space=pltpu.SMEM)
    hbm = pl.BlockSpec(memory_space=pl.ANY)
    dma = pltpu.SemaphoreType.DMA

    def half(*shape):
        return pltpu.VMEM(shape, BF16)

    def single(*shape):
        return pltpu.VMEM(shape, F32)

    return pl.pallas_call(
        functools.partial(scene_kernel, n, heads),
        out_shape=jax.ShapeDtypeStruct((rows, heads * width), BF16),
        in_specs=[hbm, hbm, vmem, vmem, hbm, smem, hbm, hbm, hbm, vmem],
        out_specs=vmem,
        scratch_shapes=[
            half(heads, depth, width),
            half(heads, depth, width),
            half(heads, 3, width, width),
            half(depth, width),
            half(depth, width),
            half(depth, width),
            half(depth, width),
            single(3 * width, width),
            half(heads, 2, piece, width),
            half(heads, 2, piece, width),
            half(heads, piece, width),
            half(heads, piece, width),
            single(heads, piece, width),
            half(3, piece, width),
            half(6, piece, width),
            half(heads, piece, width),
            half(n, rows, width),
            half(2, n // 2, rows, width),
            pltpu.VMEM((slots, rows), jnp.int32),
            pltpu.VMEM((n, slots, rows), jnp.int32),
            single(n, slots, rows),
            single(n, slots, rows),
            single(slots, rows),
            half(2, planes * rows, n * rows),
            half(2, planes * rows, n // 2 * rows),
            half(2, planes * rows, width),
            half(2, 2, planes * rows, width),
            half(2, heads, rows, rows),
            single(planes, rows, width),
            half(planes, rows, width),
            half(planes, rows, width),
            single(planes, 8, rows),
            single(planes, 8, rows),
            half(planes - 1, rows, width),
            single(planes * rows, width),
            dma((3, heads)),
            dma((3,)),
            dma((4, planes)),
            dma((4, planes)),
            dma((2, planes)),
            dma((2, planes)),
            dma((4, planes)),
            dma((4, planes)),
            dma((2, planes)),
            dma((2, planes)),
            dma((heads,)),
            dma((heads,)),
            dma((heads, chunks)),
            dma((heads, chunks)),
            dma((3, chunks)),
            dma((6, chunks)),
            dma((3, chunks)),
            dma((3, chunks)),
            dma((2, heads)),
            dma((2, heads)),
            dma((planes - 1,)),
            dma((planes,)),
        ],
        compiler_params=pltpu.CompilerParams(
            collective_id=1, has_side_effects=True, vmem_limit_bytes=63 * 1024 * 1024
        ),
    )(keys, values, rates, mask, weights, steps, queries, view_keys, view_values, views)


def on_device(
    update_keys,
    update_values,
    update_rates,
    update_mask,
    fast_weights,
    step_sizes,
    target_queries,
    target_keys,
    target_values,
    target_views,
):
    n = lax.axis_size("tokens")
    heads = fast_weights.shape[0]
    if heads == 4 and n == heads * heads:
        return scene(
            update_keys,
            update_values,
            update_rates.T,
            update_mask[None, :],
            fast_weights,
            step_sizes,
            target_queries,
            target_keys,
            target_values,
            target_views[None, :],
        )
    rates = update_rates * update_mask.astype(F32)[:, None]
    return exchange(
        update_keys,
        update_values,
        rates,
        fast_weights,
        step_sizes,
        target_queries,
        target_keys,
        target_values,
        target_views[None, :],
    )


def solution(mesh):
    rows = P(("groups", "tokens"), None)
    flat = P(("groups", "tokens"))
    return jax.shard_map(
        on_device,
        mesh=mesh,
        in_specs=(rows, rows, rows, flat, P(), P(), rows, rows, rows, flat),
        out_specs=rows,
        check_vma=False,
    )
```

```python
import functools
import math

import jax
import jax.numpy as jnp
import numpy as np
from jax import lax
from jax.experimental import pallas as pl
from jax.experimental.pallas import tpu as pltpu
from jax.sharding import PartitionSpec as P

EPS = 1e-05
MESH = pl.DeviceIdType.MESH
F32 = jnp.float32
BF16 = jnp.bfloat16
LOWEST = -1e30


def remote(src, dst, send_sem, recv_sem, peer):
    return pltpu.make_async_remote_copy(
        src_ref=src,
        dst_ref=dst,
        send_sem=send_sem,
        recv_sem=recv_sem,
        device_id={"tokens": peer},
        device_id_type=MESH,
    )


def exchange_kernel(
    n,
    heads,
    keys_ref,
    values_ref,
    rates_ref,
    weights_ref,
    steps_ref,
    queries_ref,
    view_keys_ref,
    view_values_ref,
    views_ref,
    lanes_ref,
    out_ref,
    packed_ref,
    meta_ref,
    fresh_ref,
    got_ref,
    got_meta_ref,
    query_rows,
    attended,
    mixed,
    grad,
    core_out,
    core_in,
    side_out,
    side_in,
    up_out,
    up_in,
    down_out,
    down_in,
    a2a_send,
    a2a_recv,
    meta_send,
    meta_recv,
    pair_send,
    pair_recv,
    chain_send,
    chain_recv,
    spread_send,
    spread_recv,
    out_send,
    out_recv,
):
    width = weights_ref.shape[-1]
    rows = queries_ref.shape[0]
    quads = n // heads
    piece = 3 * width // quads
    slots = packed_ref.shape[1] // quads
    capacity = slots // heads
    me = lax.axis_index("tokens")
    quad = me // heads
    head = me % heads
    core = head % 2
    side = head // 2
    core_peer = me + 1 - 2 * core
    side_peer = me + 2 - 4 * side

    barrier = pltpu.get_barrier_semaphore()
    for step in range(1, n):
        pl.semaphore_signal(
            barrier, inc=1, device_id={"tokens": (me + step) % n}, device_id_type=MESH
        )

    owner = views_ref[0:1, :]
    hits = lax.broadcasted_iota(jnp.int32, (meta_ref.shape[1], rows), 0) == owner
    hits = hits.astype(F32).astype(BF16)
    earlier = (
        lax.broadcasted_iota(jnp.int32, (rows, rows), 0)
        < lax.broadcasted_iota(jnp.int32, (rows, rows), 1)
    ).astype(F32).astype(BF16)
    before = jnp.dot(hits, earlier, preferred_element_type=F32)
    rank = jnp.sum(hits.astype(F32) * before, axis=0, keepdims=True).astype(jnp.int32)
    meta_ref[...] = lax.dot_general(
        jnp.ones((meta_ref.shape[0], rows), BF16),
        hits,
        (((1,), (1,)), ((), ())),
        preferred_element_type=F32,
    )
    pick = (
        lax.broadcasted_iota(jnp.int32, (n * capacity, rows), 0) == owner * capacity + rank
    ).astype(F32).astype(BF16)
    for index, array in enumerate((queries_ref, view_keys_ref, view_values_ref)):
        packed_ref[index] = jnp.dot(pick, array[...], preferred_element_type=F32).astype(BF16)

    pl.semaphore_wait(barrier, n - 1)

    near = [step for step in range(1, n) if step % heads < 2]
    cross = [step for step in range(1, n) if step % heads >= 2]
    early = near[::-1]
    late = cross[::-1]

    def peer_of(step):
        place, total = me, 0
        unit = 1
        while unit < n:
            bit = place % 2
            total = total + unit * ((1 - bit) if (step // unit) % 2 else bit)
            place = place // 2
            unit *= 2
        return total

    def block_copy(step):
        peer = peer_of(step)
        rows = pl.ds(pl.multiple_of((peer // heads) * slots, slots), slots)
        columns = pl.ds(pl.multiple_of((peer % heads) * width, width), width)
        return remote(
            packed_ref.at[:, rows, columns],
            got_ref.at[me],
            a2a_send.at[step],
            a2a_recv.at[step],
            peer,
        )

    def meta_copy(step):
        peer = peer_of(step)
        return remote(
            meta_ref, got_meta_ref.at[me], meta_send.at[step], meta_recv.at[step], peer
        )

    for step in range(1, n):
        meta_copy(step).start()
    for step in early:
        block_copy(step).start()
    got_meta_ref[me] = meta_ref[...]
    got_ref[me] = packed_ref[
        :,
        pl.ds(pl.multiple_of(quad * slots, slots), slots),
        pl.ds(pl.multiple_of(head * width, width), width),
    ]

    def core_copy(slot):
        return remote(
            core_out.at[slot], core_in.at[slot], pair_send.at[slot], pair_recv.at[slot], core_peer
        )

    side_copy = remote(side_out, side_in, pair_send.at[2], pair_recv.at[2], side_peer)

    def one_head(turn, carry):
        on_side = jnp.where(turn < 2, 1 - side, side)
        on_core = jnp.where(turn % 2 == 0, 1 - core, core)
        now = on_side * 2 + on_core
        columns = pl.ds(pl.multiple_of(now * width, width), width)
        key_rows = keys_ref[:, columns]
        rates = rates_ref[...]
        lanes = lax.broadcasted_iota(jnp.int32, rates.shape, 1)
        rate = jnp.sum(jnp.where(lanes == now, rates, 0.0), axis=1, keepdims=True)
        target_grad = (-rate * values_ref[:, columns].astype(F32)).astype(BF16)
        pre_gate = jnp.dot(key_rows, weights_ref[now, 0], preferred_element_type=F32)
        pre_up = jnp.dot(key_rows, weights_ref[now, 1], preferred_element_type=F32)
        back = lax.dot_general(
            target_grad,
            weights_ref[now, 2],
            (((1,), (1,)), ((), ())),
            preferred_element_type=F32,
        )
        sigma = jax.nn.sigmoid(pre_gate)
        activated = pre_gate * sigma
        hidden = (activated * pre_up).astype(BF16)
        grad_gate = (back * pre_up * sigma * (1.0 + pre_gate * (1.0 - sigma))).astype(BF16)
        grad_up = (back * activated).astype(BF16)
        over_rows = (((0,), (0,)), ((), ()))
        grad[0:width] = lax.dot_general(
            key_rows, grad_gate, over_rows, preferred_element_type=F32
        )
        grad[width : 2 * width] = lax.dot_general(
            key_rows, grad_up, over_rows, preferred_element_type=F32
        )
        grad[2 * width : 3 * width] = lax.dot_general(
            hidden, target_grad, over_rows, preferred_element_type=F32
        )

        @pl.when(turn == 0)
        def _():
            core_out[0] = grad[...].astype(BF16)
            core_copy(0).start()

        @pl.when(turn == 1)
        def _():
            core_copy(0).wait_recv()
            side_out[...] = (grad[...] + core_in[0].astype(F32)).astype(BF16)
            side_copy.start()
            for step in late:
                block_copy(step).start()

        @pl.when(turn == 2)
        def _():
            core_out[1] = grad[...].astype(BF16)
            core_copy(1).start()

        return carry

    lax.fori_loop(0, 4, one_head, 0)
    core_copy(1).wait_recv()
    side_copy.wait_recv()

    def rows_of(index):
        return pl.ds(index * piece, piece)

    def own_part(rows):
        return grad[rows, :] + core_in[1, rows, :].astype(F32) + side_in[rows, :].astype(F32)

    def up_copy(index):
        return remote(
            up_out.at[index],
            up_in.at[index],
            chain_send.at[0, index],
            chain_recv.at[0, index],
            me + heads,
        )

    def down_copy(index):
        return remote(
            down_out.at[index],
            down_in.at[index],
            chain_send.at[1, index],
            chain_recv.at[1, index],
            me - heads,
        )

    def send_up(index):
        @pl.when(quad == 0)
        def _():
            up_out[index] = own_part(rows_of(index)).astype(BF16)
            up_copy(index).start()

        @pl.when((quad > 0) & (quad < index))
        def _():
            up_copy(index).wait_recv()
            up_out[index] = (own_part(rows_of(index)) + up_in[index].astype(F32)).astype(BF16)
            up_copy(index).start()

    def send_down(index):
        @pl.when(quad == quads - 1)
        def _():
            down_out[index] = own_part(rows_of(index)).astype(BF16)
            down_copy(index).start()

        @pl.when((quad < quads - 1) & (quad > index))
        def _():
            down_copy(index).wait_recv()
            down_out[index] = (own_part(rows_of(index)) + down_in[index].astype(F32)).astype(BF16)
            down_copy(index).start()

    @pl.when(2 * quad < quads)
    def _():
        for turn in range(quads - 1):
            send_up(quads - 1 - turn)
            send_down(turn)

    @pl.when(2 * quad >= quads)
    def _():
        for turn in range(quads - 1):
            send_down(turn)
            send_up(quads - 1 - turn)

    mine = pl.ds(pl.multiple_of(quad * piece, piece), piece)
    grad[mine, :] = own_part(mine)

    @pl.when(quad > 0)
    def _():
        up_copy(quad).wait_recv()
        grad[mine, :] += up_in[quad].astype(F32)

    @pl.when(quad < quads - 1)
    def _():
        down_copy(quad).wait_recv()
        grad[mine, :] += down_in[quad].astype(F32)

    total = grad[mine, :]
    scaled = total * lax.rsqrt(jnp.mean(total * total, axis=-1, keepdims=True) + EPS)
    first = quad * piece
    block = math.gcd(piece, width)
    for part in range(piece // block):
        start = first + part * block
        old = weights_ref[
            head, start // width, pl.ds(pl.multiple_of(start % width, block), block), :
        ]
        fresh_ref[quad, part * block : (part + 1) * block, :] = (
            old.astype(F32) - steps_ref[head] * scaled[part * block : (part + 1) * block, :]
        ).astype(BF16)

    def spread_copy(way, index):
        return remote(
            fresh_ref.at[index],
            fresh_ref.at[index],
            spread_send.at[way, index],
            spread_recv.at[index],
            me + heads if way == 0 else me - heads,
        )

    @pl.when(quad < quads - 1)
    def _():
        spread_copy(0, quad).start()

    @pl.when(quad > 0)
    def _():
        spread_copy(1, quad).start()

    for step in range(1, n):
        meta_copy(step).wait()
        block_copy(step).wait()
    lane_source, lane_view, lane_slot = (lanes_ref[i : i + 1, :] for i in range(3))
    lane_count = lanes_ref.shape[1]
    counts = got_meta_ref[:, 0, :].astype(BF16)
    sources = lax.broadcasted_iota(jnp.int32, (n, lane_count), 0)
    over_source = (((0,), (0,)), ((), ()))
    same = (sources == lane_source).astype(F32).astype(BF16)
    lower = (sources < lane_source).astype(F32).astype(BF16)
    owners = lax.broadcasted_iota(jnp.int32, (meta_ref.shape[1], lane_count), 0)
    wanted = owners == lane_view + quad * heads

    def lane_sum(table):
        found = lax.dot_general(counts, table, over_source, preferred_element_type=F32)
        return jnp.sum(jnp.where(wanted, found, 0.0), axis=0, keepdims=True).astype(jnp.int32)

    place_at = jnp.where(
        lane_slot < lane_sum(same), lane_view * rows + lane_sum(lower) + lane_slot, -1
    )
    place = (
        lax.broadcasted_iota(jnp.int32, (heads * rows, lane_count), 0) == place_at
    ).astype(F32).astype(BF16)
    arranged = [
        jnp.dot(
            place, got_ref[:, i].reshape(lane_count, width), preferred_element_type=F32
        ).astype(BF16)
        for i in range(3)
    ]
    for view in range(heads):
        part = slice(view * rows, (view + 1) * rows)
        scores = lax.dot_general(
            arranged[0][part], arranged[1][part], (((1,), (1,)), ((), ())),
            preferred_element_type=F32,
        ) * width ** (-0.5)
        powers = jnp.exp(scores - jnp.max(scores, axis=-1, keepdims=True))
        probs = (powers / jnp.sum(powers, axis=-1, keepdims=True)).astype(BF16)
        attended[part] = jnp.dot(probs, arranged[2][part], preferred_element_type=F32)
    query_rows[...] = arranged[0]

    for hop in range(1, quads):

        @pl.when(quad - hop >= 0)
        def _():
            index = quad - hop
            spread_copy(0, index).wait_recv()

            @pl.when(quad < quads - 1)
            def _():
                spread_copy(0, index).start()

        @pl.when(quad + hop < quads)
        def _():
            index = quad + hop
            spread_copy(1, index).wait_recv()

            @pl.when(quad > 0)
            def _():
                spread_copy(1, index).start()

    fresh = fresh_ref[...].reshape(3 * width, width)
    pre_gate = jnp.dot(query_rows[...], fresh[0:width], preferred_element_type=F32)
    pre_up = jnp.dot(query_rows[...], fresh[width : 2 * width], preferred_element_type=F32)
    target_hidden = (pre_gate * jax.nn.sigmoid(pre_gate) * pre_up).astype(BF16)
    fast_out = jnp.dot(target_hidden, fresh[2 * width :], preferred_element_type=F32)
    normed = fast_out * lax.rsqrt(jnp.mean(fast_out * fast_out, axis=-1, keepdims=True) + EPS)
    mixed[...] = (normed + attended[...]).astype(BF16).reshape(mixed.shape)
    own_columns = pl.ds(pl.multiple_of(head * width, width), width)

    def out_copy(step):
        view = (head + step) % heads
        return remote(
            mixed.at[view],
            out_ref.at[:, own_columns],
            out_send.at[step],
            out_recv.at[step],
            quad * heads + view,
        )

    for step in range(1, heads):
        out_copy(step).start()
    out_ref[:, own_columns] = mixed[head]
    for step in range(1, heads):
        out_copy(step).wait()

    core_copy(0).wait_send()
    core_copy(1).wait_send()
    side_copy.wait_send()
    for index in range(quads):

        @pl.when(quad < index)
        def _():
            up_copy(index).wait_send()

        @pl.when(quad > index)
        def _():
            down_copy(index).wait_send()

        @pl.when((index <= quad) & (quad < quads - 1))
        def _():
            spread_copy(0, index).wait_send()

        @pl.when((index >= quad) & (quad > 0))
        def _():
            spread_copy(1, index).wait_send()


def exchange(keys, values, rates, weights, steps, queries, view_keys, view_values, views):
    n = lax.axis_size("tokens")
    heads = weights.shape[0]
    width = weights.shape[-1]
    rows = queries.shape[0]
    quads = n // heads
    piece = 3 * width // quads
    capacity = 2 * rows // n
    slots = heads * capacity
    owner_lanes = -(-n // 128) * 128
    lane = np.arange(n * slots)
    lanes = np.zeros((8, n * slots), np.int32)
    lanes[0] = lane // slots
    lanes[1] = lane % slots // capacity
    lanes[2] = lane % capacity
    vmem = pl.BlockSpec(memory_space=pltpu.VMEM)
    smem = pl.BlockSpec(memory_space=pltpu.SMEM)
    dma = pltpu.SemaphoreType.DMA
    whole = (3 * width, width)
    parts = (quads, piece, width)
    return pl.pallas_call(
        functools.partial(exchange_kernel, n, heads),
        out_shape=jax.ShapeDtypeStruct((rows, heads * width), BF16),
        in_specs=[vmem, vmem, vmem, vmem, smem] + [vmem] * 5,
        out_specs=vmem,
        scratch_shapes=[
            pltpu.VMEM((3, n * capacity, heads * width), BF16),
            pltpu.VMEM((8, owner_lanes), F32),
            pltpu.VMEM(parts, BF16),
            pltpu.VMEM((n, 3, slots, width), BF16),
            pltpu.VMEM((n, 8, owner_lanes), F32),
            pltpu.VMEM((heads * rows, width), BF16),
            pltpu.VMEM((heads * rows, width), F32),
            pltpu.VMEM((heads, rows, width), BF16),
            pltpu.VMEM(whole, F32),
            pltpu.VMEM((2,) + whole, BF16),
            pltpu.VMEM((2,) + whole, BF16),
            pltpu.VMEM(whole, BF16),
            pltpu.VMEM(whole, BF16),
            pltpu.VMEM(parts, BF16),
            pltpu.VMEM(parts, BF16),
            pltpu.VMEM(parts, BF16),
            pltpu.VMEM(parts, BF16),
            dma((n,)),
            dma((n,)),
            dma((n,)),
            dma((n,)),
            dma((3,)),
            dma((3,)),
            dma((2, quads)),
            dma((2, quads)),
            dma((2, quads)),
            dma((quads,)),
            dma((heads,)),
            dma((heads,)),
        ],
        compiler_params=pltpu.CompilerParams(
            collective_id=0, has_side_effects=True, vmem_limit_bytes=63 * 1024 * 1024
        ),
    )(keys, values, rates, weights, steps, queries, view_keys, view_values, views, jnp.asarray(lanes))


def scene_kernel(
    n,
    heads,
    keys_ref,
    values_ref,
    rates_ref,
    mask_ref,
    weights_ref,
    steps_ref,
    queries_ref,
    view_keys_ref,
    view_values_ref,
    views_ref,
    out_ref,
    key_buf,
    value_buf,
    weight_buf,
    target_grad,
    hidden,
    grad_gate,
    grad_up,
    grad,
    core_out,
    core_in,
    side_out,
    side_in,
    own,
    chain_out,
    chain_in,
    fresh_ref,
    got_q,
    got_kv,
    views_out,
    got_views,
    rank_q,
    rank_kv,
    counts,
    place_q,
    place_kv,
    arranged_q,
    arranged_kv,
    powers,
    attended,
    part_out,
    part_in,
    stats_out,
    stats_in,
    mixed,
    normed,
    load_sem,
    local_sem,
    z_send,
    z_recv,
    y_send,
    y_recv,
    c_send,
    c_recv,
    cy_send,
    cy_recv,
    core_send,
    core_recv,
    side_send,
    side_recv,
    chain_send,
    chain_recv,
    fresh_send,
    fresh_recv,
    part_send,
    part_recv,
    out_send,
    out_recv,
):
    width = out_ref.shape[1] // heads
    rows = out_ref.shape[0]
    planes = n // heads
    piece = 3 * width // heads
    me = lax.axis_index("tokens")
    z, p = me // heads, me % heads
    y, c = p // 2, p % 2
    core_peer = me + 1 - 2 * c
    side_peer = me + 2 - 4 * y
    low = 2 * z < planes
    ahead = jnp.where(low, me + heads, me - heads)
    behind = jnp.where(low, me - heads, me + heads)
    is_end = (z == 0) | (z == planes - 1)

    def plane_of(step):
        return (z + step) % planes

    barrier = pltpu.get_barrier_semaphore()
    for peer in [core_peer, side_peer] + [
        plane_of(step) * heads + p for step in range(1, planes)
    ]:
        pl.semaphore_signal(barrier, inc=1, device_id={"tokens": peer}, device_id_type=MESH)

    def head_at(turn):
        at_mid = jnp.where(turn == 0, 3, jnp.where(turn == 1, 0, 4 - turn))
        place = jnp.where(is_end, 3 - turn, at_mid)
        return jnp.where(low, place, 3 - place)

    def columns(head):
        return pl.ds(pl.multiple_of(head * width, width), width)

    def loads(turn):
        head = head_at(turn)
        return (
            pltpu.make_async_copy(keys_ref.at[:, columns(head)], key_buf.at[turn], load_sem.at[0, turn]),
            pltpu.make_async_copy(weights_ref.at[head], weight_buf.at[turn], load_sem.at[1, turn]),
            pltpu.make_async_copy(values_ref.at[:, columns(head)], value_buf.at[turn], load_sem.at[2, turn]),
        )

    for turn in range(heads):
        for load in loads(turn):
            load.start()

    views_out[...] = jnp.broadcast_to(views_ref[...], views_out.shape)
    here = p * planes + z
    kv_here = c * planes + z
    locals_ = (
        pltpu.make_async_copy(queries_ref.at[:, columns(z)], got_q.at[here], local_sem.at[0]),
        pltpu.make_async_copy(view_keys_ref.at[:, columns(z)], got_kv.at[0, kv_here], local_sem.at[1]),
        pltpu.make_async_copy(view_values_ref.at[:, columns(z)], got_kv.at[1, kv_here], local_sem.at[2]),
    )
    for copy in locals_:
        copy.start()
    got_views[here] = views_out[...]

    pl.semaphore_wait(barrier, planes + 1)

    def z_copy(turn, index):
        plane = head_at(turn)
        source, target = (
            (queries_ref.at[:, columns(plane)], got_q.at[here]),
            (view_keys_ref.at[:, columns(plane)], got_kv.at[0, kv_here]),
            (view_values_ref.at[:, columns(plane)], got_kv.at[1, kv_here]),
            (views_out, got_views.at[here]),
        )[index]
        return remote(
            source, target, z_send.at[index, turn], z_recv.at[index, z], plane * heads + p
        )

    def z_arrived(step, index):
        source, target = ((queries_ref.at[:, columns(z)], got_q.at[here]), (views_out, got_views.at[here]))[
            index == 3
        ]
        remote(
            source, target, z_send.at[index, 0], z_recv.at[index, plane_of(step)], core_peer
        ).wait_recv()

    def y_copy(step, index):
        slot = p * planes + plane_of(step)
        if index == 0:
            source = queries_ref.at[:, columns(z)] if step == 0 else got_q.at[slot]
            target = got_q.at[slot]
        else:
            source = views_out if step == 0 else got_views.at[slot]
            target = got_views.at[slot]
        return remote(source, target, y_send.at[index, step], y_recv.at[index, step], side_peer)

    def c_copy(step, index):
        slot = p * planes + plane_of(step)
        kv_slot = c * planes + plane_of(step)
        target = (
            got_q.at[slot], got_kv.at[0, kv_slot], got_kv.at[1, kv_slot], got_views.at[slot]
        )[index]
        if step == 0:
            source = (
                queries_ref.at[:, columns(z)],
                view_keys_ref.at[:, columns(z)],
                view_values_ref.at[:, columns(z)],
                views_out,
            )[index]
        else:
            source = target
        return remote(source, target, c_send.at[index, step], c_recv.at[index, step], core_peer)

    def cy_copy(step, index):
        slot = (2 * (1 - y) + c) * planes + plane_of(step)
        target = got_q.at[slot] if index == 0 else got_views.at[slot]
        return remote(target, target, cy_send.at[index, step], cy_recv.at[index, step], core_peer)

    for index in (3, 0, 1):
        for turn in range(heads - 1):
            z_copy(turn, index).start()

    @pl.when(jnp.logical_not(is_end))
    def _():
        for turn in range(heads - 1):
            z_copy(turn, 2).start()

    for index in (1, 0):
        y_copy(0, index).start()
    for index in (3, 0, 1, 2):
        c_copy(0, index).start()

    def core_copy(turn):
        return remote(
            core_out.at[turn], core_in.at[turn], core_send.at[turn], core_recv.at[turn], core_peer
        )

    chunk = math.gcd(piece, width)
    chunks = piece // chunk

    def chunk_rows(index):
        return slice(index * chunk, (index + 1) * chunk)

    def side_copy(turn, index):
        at = chunk_rows(index)
        return remote(
            side_out.at[turn, at],
            side_in.at[turn, at],
            side_send.at[turn, index],
            side_recv.at[turn, index],
            side_peer,
        )

    def quarter(at_y, at_c):
        return pl.ds(pl.multiple_of((2 * at_y + at_c) * piece, piece), piece)

    def take_core(turn):
        core_copy(turn).wait_recv()
        side_out[turn] = (
            grad[quarter(1 - y, c), :] + core_in[turn, 1 - y].astype(F32)
        ).astype(BF16)
        for index in range(chunks):
            side_copy(turn, index).start()
        own[turn] = grad[quarter(y, c), :] + core_in[turn, y].astype(F32)

    eye = lax.broadcasted_iota(jnp.int32, (rows, rows), 0) == lax.broadcasted_iota(
        jnp.int32, (rows, rows), 1
    )

    def to_column(row):
        parts = [
            jnp.sum(jnp.where(eye, row[:, at : at + rows], 0.0), axis=1, keepdims=True)
            for at in range(0, row.shape[1], rows)
        ]
        return parts[0] if len(parts) == 1 else jnp.concatenate(parts, axis=0)

    def to_row(column):
        return jnp.sum(jnp.where(eye, column, 0.0), axis=0, keepdims=True)

    over_rows = (((0,), (0,)), ((), ()))
    over_last = (((1,), (1,)), ((), ()))

    def one_head(turn, carry):
        for load in loads(turn):
            load.wait()
        rate = to_column(rates_ref[pl.ds(head_at(turn), 1), :] * mask_ref[...].astype(F32))
        key_rows = key_buf[turn]
        target_grad[...] = (-rate * value_buf[turn].astype(F32)).astype(BF16)
        pre_gate = jnp.dot(key_rows, weight_buf[turn, 0], preferred_element_type=F32)
        pre_up = jnp.dot(key_rows, weight_buf[turn, 1], preferred_element_type=F32)
        back = lax.dot_general(
            target_grad[...], weight_buf[turn, 2], over_last, preferred_element_type=F32
        )
        sigma = jax.nn.sigmoid(pre_gate)
        activated = pre_gate * sigma
        hidden[...] = (activated * pre_up).astype(BF16)
        grad_gate[...] = (back * pre_up * sigma * (1.0 + pre_gate * (1.0 - sigma))).astype(BF16)
        grad_up[...] = (back * activated).astype(BF16)

        @pl.when(turn > 0)
        def _():
            take_core(turn - 1)

        grad[0:width] = lax.dot_general(
            key_buf[turn], grad_gate[...], over_rows, preferred_element_type=F32
        )
        grad[width : 2 * width] = lax.dot_general(
            key_buf[turn], grad_up[...], over_rows, preferred_element_type=F32
        )
        grad[2 * width : 3 * width] = lax.dot_general(
            hidden[...], target_grad[...], over_rows, preferred_element_type=F32
        )
        for at_y in range(2):
            core_out[turn, at_y] = grad[quarter(at_y, 1 - c), :].astype(BF16)
        core_copy(turn).start()

        @pl.when(turn == 1)
        def _():
            for step in range(1, planes):
                z_arrived(step, 3)
                y_copy(step, 1).start()
                c_copy(step, 3).start()

        @pl.when(turn == 2)
        def _():
            for step in range(1, planes):
                z_arrived(step, 0)
                y_copy(step, 0).start()
                c_copy(step, 0).start()

        return carry

    lax.fori_loop(0, heads, one_head, 0)
    take_core(heads - 1)

    def chain_copy(out_slot, in_slot, index, peer):
        at = chunk_rows(index)
        return remote(
            chain_out.at[out_slot, at],
            chain_in.at[in_slot, at],
            chain_send.at[out_slot, index],
            chain_recv.at[in_slot, index],
            peer,
        )

    hops = ((0, 3, ahead), (3, 5, behind), (1, 4, ahead))

    def pass_on(turn, index):
        side_copy(turn, index).wait_recv()
        at = chunk_rows(index)

        @pl.when(is_end)
        def _():
            chain_out[turn, at] = (own[turn, at] + side_in[turn, at].astype(F32)).astype(BF16)
            chain_copy(turn, turn, index, ahead).start()

        @pl.when(jnp.logical_not(is_end))
        def _():
            taken, given, peer = hops[turn]
            chain_copy(turn, taken, index, peer).wait_recv()
            chain_out[turn, at] = (
                own[turn, at] + side_in[turn, at].astype(F32) + chain_in[taken, at].astype(F32)
            ).astype(BF16)
            chain_copy(turn, given, index, peer).start()

    views = 2 * planes
    def ones(where):
        return where.astype(F32).astype(BF16)

    def rank_rows():
        square = (n * views, n * views)
        low_axis = lax.broadcasted_iota(jnp.int32, square, 0)
        high_axis = lax.broadcasted_iota(jnp.int32, square, 1)

        def order(index):
            slot = index // views
            return slot % planes * heads + slot // planes

        listed = low_axis % views
        side_of = jnp.where(listed < planes, y, 1 - y)
        wanted = listed % planes * heads + 2 * side_of + c
        is_hit = got_views[...].reshape(n * views, rows) == wanted[:, :rows]
        hits = ones(is_hit)
        within = jnp.dot(
            hits,
            ones(
                lax.broadcasted_iota(jnp.int32, (rows, rows), 0)
                < lax.broadcasted_iota(jnp.int32, (rows, rows), 1)
            ),
            preferred_element_type=F32,
        )
        before = (low_axis % views == high_axis % views) & (order(high_axis) < order(low_axis))
        in_column = high_axis // (views * n // 2) == y

        def earlier(table):
            found = jnp.dot(ones(table), hits, preferred_element_type=F32)
            return jnp.sum(found, axis=1, keepdims=True)

        rank_q[...] = jnp.where(is_hit, earlier(before) + within, -1.0).reshape(rank_q.shape)
        rank_kv[...] = jnp.where(is_hit, earlier(before & in_column) + within, -1.0).reshape(
            rank_kv.shape
        )
        counts[...] = jnp.broadcast_to(
            earlier(((low_axis % views == high_axis % views) & in_column)[0:views]), counts.shape
        )

    def spots(ranks, first, sources, view):
        row = jnp.concatenate(
            [ranks[first + source, view : view + 1, :] for source in range(sources)], axis=1
        )
        at = lax.broadcasted_iota(jnp.int32, (rows, sources * rows), 0).astype(F32)
        return ones(at == row)

    def spot_q(group):
        for view in range(planes):
            place_q[group, view * rows : (view + 1) * rows] = spots(
                rank_q, 0, n, group * planes + view
            )

    def arrange_q(group):
        arranged_q[group] = jnp.dot(
            place_q[group], got_q[...].reshape(n * rows, width), preferred_element_type=F32
        ).astype(BF16)

    def spot_kv(group):
        for view in range(planes):
            place_kv[group, view * rows : (view + 1) * rows] = spots(
                rank_kv, y * (n // 2), n // 2, group * planes + view
            )

    def arrange_kv(group, index):
        arranged_kv[group, index] = jnp.dot(
            place_kv[group],
            got_kv[index].reshape(n // 2 * rows, width),
            preferred_element_type=F32,
        ).astype(BF16)

    def view_rows(view):
        return pl.ds(pl.multiple_of(view * rows, rows), rows)

    def weigh(group, turn):
        view = head_at(turn)
        part = view_rows(view)
        scores = lax.dot_general(
            arranged_q[group, part], arranged_kv[group, 0, part], over_last, preferred_element_type=F32
        ) * width ** (-0.5)
        at = group * planes + view
        real = lax.broadcasted_iota(jnp.int32, (rows, rows), 1).astype(F32) < counts[pl.ds(at, 1), :]
        top = jnp.max(jnp.where(real, scores, LOWEST), axis=-1, keepdims=True)
        exps = jnp.where(real, jnp.exp(jnp.where(real, scores - top, 0.0)), 0.0)
        powers[group, turn] = exps.astype(BF16)
        return top, jnp.sum(exps, axis=-1, keepdims=True)

    def attend(group, turn):
        return jnp.dot(
            powers[group, turn],
            arranged_kv[group, 1, view_rows(head_at(turn))],
            preferred_element_type=F32,
        )

    def part_copy(turn, index):
        view = head_at(turn)
        source, target = ((part_out, part_in), (stats_out, stats_in))[index]
        return remote(
            source.at[view],
            target.at[view],
            part_send.at[index, turn],
            part_recv.at[index, turn],
            side_peer,
        )

    for index in range(chunks):
        pass_on(0, index)
    for step in range(planes):
        y_copy(step, 1).wait_recv()
        cy_copy(step, 1).start()
    for step in range(planes):
        cy_copy(step, 1).wait_recv()
        c_copy(step, 3).wait_recv()
    rank_rows()
    spot_q(1)
    pass_on(1, 0)
    spot_q(0)
    pass_on(1, 1)
    spot_kv(1)
    pass_on(1, 2)
    spot_kv(0)
    for copy in locals_:
        copy.wait()
    for step in range(1, planes):
        z_arrived(step, 1)
        c_copy(step, 1).start()
    for step in range(planes):
        y_copy(step, 0).wait_recv()
        cy_copy(step, 0).start()
    for step in range(planes):
        c_copy(step, 1).wait_recv()
    arrange_kv(1, 0)
    pass_on(2, 0)
    arrange_kv(0, 0)
    for step in range(planes):
        cy_copy(step, 0).wait_recv()
        c_copy(step, 0).wait_recv()
    arrange_q(1)
    pass_on(2, 1)
    arrange_q(0)
    pass_on(2, 2)

    @pl.when(is_end)
    def _():
        for turn in range(heads - 1):
            z_copy(turn, 2).start()

    for turn in range(heads):
        view = head_at(turn)
        top, total = weigh(1, turn)
        stats_out[view, 0:1, :] = to_row(top)
        stats_out[view, 1:2, :] = to_row(total)
        part_copy(turn, 1).start()

    last = heads - 1

    def fresh_copy(way, index):
        slot = 2 * (1 - y) + c if way == 2 else p
        at = chunk_rows(index)
        return remote(
            fresh_ref.at[slot, at],
            fresh_ref.at[slot, at],
            fresh_send.at[way, index],
            fresh_recv.at[way, index],
            side_peer if way == 0 else core_peer,
        )

    for index in range(chunks):
        at = chunk_rows(index)
        side_copy(last, index).wait_recv()
        own[last, at] += side_in[last, at].astype(F32)

        @pl.when(is_end)
        def _():
            chain_copy(0, 5, index, ahead).wait_recv()
            own[last, at] += chain_in[5, at].astype(F32)

        @pl.when(jnp.logical_not(is_end))
        def _():
            for slot in (2, 4):
                chain_copy(0, slot, index, ahead).wait_recv()
            own[last, at] += chain_in[2, at].astype(F32) + chain_in[4, at].astype(F32)

        gradient = own[last, at]
        scaled = gradient * lax.rsqrt(jnp.mean(gradient * gradient, axis=-1, keepdims=True) + EPS)
        start = p * piece + index * chunk
        old = weight_buf[
            last, start // width, pl.ds(pl.multiple_of(start % width, chunk), chunk), :
        ]
        fresh_ref[p, at, :] = (old.astype(F32) - steps_ref[z] * scaled).astype(BF16)
        fresh_copy(0, index).start()
        fresh_copy(1, index).start()

    tops, totals = [], []
    for turn in range(heads):
        top, total = weigh(0, turn)
        tops.append(top)
        totals.append(total)

    for step in range(1, planes):
        z_arrived(step, 2)
        c_copy(step, 2).start()
    for step in range(planes):
        c_copy(step, 2).wait_recv()
    arrange_kv(1, 1)
    for turn in range(heads):
        part_out[head_at(turn)] = attend(1, turn).astype(BF16)
        part_copy(turn, 0).start()
    arrange_kv(0, 1)
    for turn in range(heads):
        attended[turn] = attend(0, turn)

    for index in range(chunks):
        fresh_copy(0, index).wait_recv()
        fresh_copy(2, index).start()
    for index in range(chunks):
        fresh_copy(1, index).wait_recv()
        fresh_copy(2, index).wait_recv()

    fresh = fresh_ref[...].reshape(3 * width, width)
    query_rows = arranged_q[0]
    pre_gate = jnp.dot(query_rows, fresh[0:width], preferred_element_type=F32)
    pre_up = jnp.dot(query_rows, fresh[width : 2 * width], preferred_element_type=F32)
    target_hidden = (pre_gate * jax.nn.sigmoid(pre_gate) * pre_up).astype(BF16)
    fast_out = jnp.dot(target_hidden, fresh[2 * width :], preferred_element_type=F32)
    normed[...] = fast_out * lax.rsqrt(
        jnp.mean(fast_out * fast_out, axis=-1, keepdims=True) + EPS
    )

    def out_copy(turn, plane, source):
        return remote(
            mixed.at[turn],
            out_ref.at[:, columns(source)],
            out_send.at[turn],
            out_recv.at[source],
            plane * heads + p,
        )

    for turn in range(heads):
        view = head_at(turn)
        for index in range(2):
            part_copy(turn, index).wait_recv()
        other_top = to_column(stats_in[view, 0:1, :])
        other_total = to_column(stats_in[view, 1:2, :])
        top = jnp.maximum(tops[turn], other_top)
        scale, other_scale = jnp.exp(tops[turn] - top), jnp.exp(other_top - top)
        weight = 1.0 / (scale * totals[turn] + other_scale * other_total)
        result = (
            normed[pl.ds(pl.multiple_of(view * rows, rows), rows)]
            + attended[turn] * (scale * weight)
            + part_in[view].astype(F32) * (other_scale * weight)
        ).astype(BF16)
        if turn < last:
            mixed[turn] = result
            out_copy(turn, view, z).start()
        else:
            out_ref[:, columns(z)] = result

    for step in range(1, planes):
        out_copy(0, z, plane_of(step)).wait_recv()
    for turn in range(last):
        out_copy(turn, z, z).wait_send()
        for index in range(chunks):
            chain_copy(turn, 0, index, ahead).wait_send()
            fresh_copy(turn, index).wait_send()
    for turn in range(heads):
        core_copy(turn).wait_send()
        for index in range(2):
            part_copy(turn, index).wait_send()
        for index in range(chunks):
            side_copy(turn, index).wait_send()
    for step in range(planes):
        for index in range(4):
            c_copy(step, index).wait_send()
            if step < last:
                z_copy(step, index).wait_send()
        for index in range(2):
            y_copy(step, index).wait_send()
            cy_copy(step, index).wait_send()


def scene(keys, values, rates, mask, weights, steps, queries, view_keys, view_values, views):
    n = lax.axis_size("tokens")
    heads, _, _, width = weights.shape
    rows = queries.shape[0]
    depth = keys.shape[0]
    planes = n // heads
    piece = 3 * width // heads
    chunks = piece // math.gcd(piece, width)
    slots = 2 * planes
    vmem = pl.BlockSpec(memory_space=pltpu.VMEM)
    smem = pl.BlockSpec(memory_space=pltpu.SMEM)
    hbm = pl.BlockSpec(memory_space=pl.ANY)
    dma = pltpu.SemaphoreType.DMA

    def half(*shape):
        return pltpu.VMEM(shape, BF16)

    def single(*shape):
        return pltpu.VMEM(shape, F32)

    return pl.pallas_call(
        functools.partial(scene_kernel, n, heads),
        out_shape=jax.ShapeDtypeStruct((rows, heads * width), BF16),
        in_specs=[hbm, hbm, vmem, vmem, hbm, smem, hbm, hbm, hbm, vmem],
        out_specs=vmem,
        scratch_shapes=[
            half(heads, depth, width),
            half(heads, depth, width),
            half(heads, 3, width, width),
            half(depth, width),
            half(depth, width),
            half(depth, width),
            half(depth, width),
            single(3 * width, width),
            half(heads, 2, piece, width),
            half(heads, 2, piece, width),
            half(heads, piece, width),
            half(heads, piece, width),
            single(heads, piece, width),
            half(3, piece, width),
            half(6, piece, width),
            half(heads, piece, width),
            half(n, rows, width),
            half(2, n // 2, rows, width),
            pltpu.VMEM((slots, rows), jnp.int32),
            pltpu.VMEM((n, slots, rows), jnp.int32),
            single(n, slots, rows),
            single(n, slots, rows),
            single(slots, rows),
            half(2, planes * rows, n * rows),
            half(2, planes * rows, n // 2 * rows),
            half(2, planes * rows, width),
            half(2, 2, planes * rows, width),
            half(2, heads, rows, rows),
            single(planes, rows, width),
            half(planes, rows, width),
            half(planes, rows, width),
            single(planes, 8, rows),
            single(planes, 8, rows),
            half(planes - 1, rows, width),
            single(planes * rows, width),
            dma((3, heads)),
            dma((3,)),
            dma((4, planes)),
            dma((4, planes)),
            dma((2, planes)),
            dma((2, planes)),
            dma((4, planes)),
            dma((4, planes)),
            dma((2, planes)),
            dma((2, planes)),
            dma((heads,)),
            dma((heads,)),
            dma((heads, chunks)),
            dma((heads, chunks)),
            dma((3, chunks)),
            dma((6, chunks)),
            dma((3, chunks)),
            dma((3, chunks)),
            dma((2, heads)),
            dma((2, heads)),
            dma((planes - 1,)),
            dma((planes,)),
        ],
        compiler_params=pltpu.CompilerParams(
            collective_id=1, has_side_effects=True, vmem_limit_bytes=63 * 1024 * 1024
        ),
    )(keys, values, rates, mask, weights, steps, queries, view_keys, view_values, views)


def on_device(
    update_keys,
    update_values,
    update_rates,
    update_mask,
    fast_weights,
    step_sizes,
    target_queries,
    target_keys,
    target_values,
    target_views,
):
    n = lax.axis_size("tokens")
    heads = fast_weights.shape[0]
    if heads == 4 and n == heads * heads:
        return scene(
            update_keys,
            update_values,
            update_rates.T,
            update_mask[None, :],
            fast_weights,
            step_sizes,
            target_queries,
            target_keys,
            target_values,
            target_views[None, :],
        )
    rates = update_rates * update_mask.astype(F32)[:, None]
    return exchange(
        update_keys,
        update_values,
        rates,
        fast_weights,
        step_sizes,
        target_queries,
        target_keys,
        target_values,
        target_views[None, :],
    )


def solution(mesh):
    rows = P(("groups", "tokens"), None)
    flat = P(("groups", "tokens"))
    return jax.shard_map(
        on_device,
        mesh=mesh,
        in_specs=(rows, rows, rows, flat, P(), P(), rows, rows, rows, flat),
        out_specs=rows,
        check_vma=False,
    )
```

```python
import functools
import math

import jax
import jax.numpy as jnp
import numpy as np
from jax import lax
from jax.experimental import pallas as pl
from jax.experimental.pallas import tpu as pltpu
from jax.sharding import PartitionSpec as P

EPS = 1e-05
MESH = pl.DeviceIdType.MESH
F32 = jnp.float32
BF16 = jnp.bfloat16
LOWEST = -1e30


def remote(src, dst, send_sem, recv_sem, peer):
    return pltpu.make_async_remote_copy(
        src_ref=src,
        dst_ref=dst,
        send_sem=send_sem,
        recv_sem=recv_sem,
        device_id={"tokens": peer},
        device_id_type=MESH,
    )


def exchange_kernel(
    n,
    heads,
    keys_ref,
    values_ref,
    rates_ref,
    weights_ref,
    steps_ref,
    queries_ref,
    view_keys_ref,
    view_values_ref,
    views_ref,
    lanes_ref,
    out_ref,
    packed_ref,
    meta_ref,
    fresh_ref,
    got_ref,
    got_meta_ref,
    query_rows,
    attended,
    mixed,
    grad,
    core_out,
    core_in,
    side_out,
    side_in,
    up_out,
    up_in,
    down_out,
    down_in,
    a2a_send,
    a2a_recv,
    meta_send,
    meta_recv,
    pair_send,
    pair_recv,
    chain_send,
    chain_recv,
    spread_send,
    spread_recv,
    out_send,
    out_recv,
):
    width = weights_ref.shape[-1]
    rows = queries_ref.shape[0]
    quads = n // heads
    piece = 3 * width // quads
    slots = packed_ref.shape[1] // quads
    capacity = slots // heads
    me = lax.axis_index("tokens")
    quad = me // heads
    head = me % heads
    core = head % 2
    side = head // 2
    core_peer = me + 1 - 2 * core
    side_peer = me + 2 - 4 * side

    barrier = pltpu.get_barrier_semaphore()
    for step in range(1, n):
        pl.semaphore_signal(
            barrier, inc=1, device_id={"tokens": (me + step) % n}, device_id_type=MESH
        )

    owner = views_ref[0:1, :]
    hits = lax.broadcasted_iota(jnp.int32, (meta_ref.shape[1], rows), 0) == owner
    hits = hits.astype(F32).astype(BF16)
    earlier = (
        lax.broadcasted_iota(jnp.int32, (rows, rows), 0)
        < lax.broadcasted_iota(jnp.int32, (rows, rows), 1)
    ).astype(F32).astype(BF16)
    before = jnp.dot(hits, earlier, preferred_element_type=F32)
    rank = jnp.sum(hits.astype(F32) * before, axis=0, keepdims=True).astype(jnp.int32)
    meta_ref[...] = lax.dot_general(
        jnp.ones((meta_ref.shape[0], rows), BF16),
        hits,
        (((1,), (1,)), ((), ())),
        preferred_element_type=F32,
    )
    pick = (
        lax.broadcasted_iota(jnp.int32, (n * capacity, rows), 0) == owner * capacity + rank
    ).astype(F32).astype(BF16)
    for index, array in enumerate((queries_ref, view_keys_ref, view_values_ref)):
        packed_ref[index] = jnp.dot(pick, array[...], preferred_element_type=F32).astype(BF16)

    pl.semaphore_wait(barrier, n - 1)

    near = [step for step in range(1, n) if step % heads < 2]
    cross = [step for step in range(1, n) if step % heads >= 2]
    early = near[::-1]
    late = cross[::-1]

    def peer_of(step):
        place, total = me, 0
        unit = 1
        while unit < n:
            bit = place % 2
            total = total + unit * ((1 - bit) if (step // unit) % 2 else bit)
            place = place // 2
            unit *= 2
        return total

    def block_copy(step):
        peer = peer_of(step)
        rows = pl.ds(pl.multiple_of((peer // heads) * slots, slots), slots)
        columns = pl.ds(pl.multiple_of((peer % heads) * width, width), width)
        return remote(
            packed_ref.at[:, rows, columns],
            got_ref.at[me],
            a2a_send.at[step],
            a2a_recv.at[step],
            peer,
        )

    def meta_copy(step):
        peer = peer_of(step)
        return remote(
            meta_ref, got_meta_ref.at[me], meta_send.at[step], meta_recv.at[step], peer
        )

    for step in range(1, n):
        meta_copy(step).start()
    for step in early:
        block_copy(step).start()
    got_meta_ref[me] = meta_ref[...]
    got_ref[me] = packed_ref[
        :,
        pl.ds(pl.multiple_of(quad * slots, slots), slots),
        pl.ds(pl.multiple_of(head * width, width), width),
    ]

    def core_copy(slot):
        return remote(
            core_out.at[slot], core_in.at[slot], pair_send.at[slot], pair_recv.at[slot], core_peer
        )

    side_copy = remote(side_out, side_in, pair_send.at[2], pair_recv.at[2], side_peer)

    def one_head(turn, carry):
        on_side = jnp.where(turn < 2, 1 - side, side)
        on_core = jnp.where(turn % 2 == 0, 1 - core, core)
        now = on_side * 2 + on_core
        columns = pl.ds(pl.multiple_of(now * width, width), width)
        key_rows = keys_ref[:, columns]
        rates = rates_ref[...]
        lanes = lax.broadcasted_iota(jnp.int32, rates.shape, 1)
        rate = jnp.sum(jnp.where(lanes == now, rates, 0.0), axis=1, keepdims=True)
        target_grad = (-rate * values_ref[:, columns].astype(F32)).astype(BF16)
        pre_gate = jnp.dot(key_rows, weights_ref[now, 0], preferred_element_type=F32)
        pre_up = jnp.dot(key_rows, weights_ref[now, 1], preferred_element_type=F32)
        back = lax.dot_general(
            target_grad,
            weights_ref[now, 2],
            (((1,), (1,)), ((), ())),
            preferred_element_type=F32,
        )
        sigma = jax.nn.sigmoid(pre_gate)
        activated = pre_gate * sigma
        hidden = (activated * pre_up).astype(BF16)
        grad_gate = (back * pre_up * sigma * (1.0 + pre_gate * (1.0 - sigma))).astype(BF16)
        grad_up = (back * activated).astype(BF16)
        over_rows = (((0,), (0,)), ((), ()))
        grad[0:width] = lax.dot_general(
            key_rows, grad_gate, over_rows, preferred_element_type=F32
        )
        grad[width : 2 * width] = lax.dot_general(
            key_rows, grad_up, over_rows, preferred_element_type=F32
        )
        grad[2 * width : 3 * width] = lax.dot_general(
            hidden, target_grad, over_rows, preferred_element_type=F32
        )

        @pl.when(turn == 0)
        def _():
            core_out[0] = grad[...].astype(BF16)
            core_copy(0).start()

        @pl.when(turn == 1)
        def _():
            core_copy(0).wait_recv()
            side_out[...] = (grad[...] + core_in[0].astype(F32)).astype(BF16)
            side_copy.start()
            for step in late:
                block_copy(step).start()

        @pl.when(turn == 2)
        def _():
            core_out[1] = grad[...].astype(BF16)
            core_copy(1).start()

        return carry

    lax.fori_loop(0, 4, one_head, 0)
    core_copy(1).wait_recv()
    side_copy.wait_recv()

    def rows_of(index):
        return pl.ds(index * piece, piece)

    def own_part(rows):
        return grad[rows, :] + core_in[1, rows, :].astype(F32) + side_in[rows, :].astype(F32)

    def up_copy(index):
        return remote(
            up_out.at[index],
            up_in.at[index],
            chain_send.at[0, index],
            chain_recv.at[0, index],
            me + heads,
        )

    def down_copy(index):
        return remote(
            down_out.at[index],
            down_in.at[index],
            chain_send.at[1, index],
            chain_recv.at[1, index],
            me - heads,
        )

    def send_up(index):
        @pl.when(quad == 0)
        def _():
            up_out[index] = own_part(rows_of(index)).astype(BF16)
            up_copy(index).start()

        @pl.when((quad > 0) & (quad < index))
        def _():
            up_copy(index).wait_recv()
            up_out[index] = (own_part(rows_of(index)) + up_in[index].astype(F32)).astype(BF16)
            up_copy(index).start()

    def send_down(index):
        @pl.when(quad == quads - 1)
        def _():
            down_out[index] = own_part(rows_of(index)).astype(BF16)
            down_copy(index).start()

        @pl.when((quad < quads - 1) & (quad > index))
        def _():
            down_copy(index).wait_recv()
            down_out[index] = (own_part(rows_of(index)) + down_in[index].astype(F32)).astype(BF16)
            down_copy(index).start()

    @pl.when(2 * quad < quads)
    def _():
        for turn in range(quads - 1):
            send_up(quads - 1 - turn)
            send_down(turn)

    @pl.when(2 * quad >= quads)
    def _():
        for turn in range(quads - 1):
            send_down(turn)
            send_up(quads - 1 - turn)

    mine = pl.ds(pl.multiple_of(quad * piece, piece), piece)
    grad[mine, :] = own_part(mine)

    @pl.when(quad > 0)
    def _():
        up_copy(quad).wait_recv()
        grad[mine, :] += up_in[quad].astype(F32)

    @pl.when(quad < quads - 1)
    def _():
        down_copy(quad).wait_recv()
        grad[mine, :] += down_in[quad].astype(F32)

    total = grad[mine, :]
    scaled = total * lax.rsqrt(jnp.mean(total * total, axis=-1, keepdims=True) + EPS)
    first = quad * piece
    block = math.gcd(piece, width)
    for part in range(piece // block):
        start = first + part * block
        old = weights_ref[
            head, start // width, pl.ds(pl.multiple_of(start % width, block), block), :
        ]
        fresh_ref[quad, part * block : (part + 1) * block, :] = (
            old.astype(F32) - steps_ref[head] * scaled[part * block : (part + 1) * block, :]
        ).astype(BF16)

    def spread_copy(way, index):
        return remote(
            fresh_ref.at[index],
            fresh_ref.at[index],
            spread_send.at[way, index],
            spread_recv.at[index],
            me + heads if way == 0 else me - heads,
        )

    @pl.when(quad < quads - 1)
    def _():
        spread_copy(0, quad).start()

    @pl.when(quad > 0)
    def _():
        spread_copy(1, quad).start()

    for step in range(1, n):
        meta_copy(step).wait()
        block_copy(step).wait()
    lane_source, lane_view, lane_slot = (lanes_ref[i : i + 1, :] for i in range(3))
    lane_count = lanes_ref.shape[1]
    counts = got_meta_ref[:, 0, :].astype(BF16)
    sources = lax.broadcasted_iota(jnp.int32, (n, lane_count), 0)
    over_source = (((0,), (0,)), ((), ()))
    same = (sources == lane_source).astype(F32).astype(BF16)
    lower = (sources < lane_source).astype(F32).astype(BF16)
    owners = lax.broadcasted_iota(jnp.int32, (meta_ref.shape[1], lane_count), 0)
    wanted = owners == lane_view + quad * heads

    def lane_sum(table):
        found = lax.dot_general(counts, table, over_source, preferred_element_type=F32)
        return jnp.sum(jnp.where(wanted, found, 0.0), axis=0, keepdims=True).astype(jnp.int32)

    place_at = jnp.where(
        lane_slot < lane_sum(same), lane_view * rows + lane_sum(lower) + lane_slot, -1
    )
    place = (
        lax.broadcasted_iota(jnp.int32, (heads * rows, lane_count), 0) == place_at
    ).astype(F32).astype(BF16)
    arranged = [
        jnp.dot(
            place, got_ref[:, i].reshape(lane_count, width), preferred_element_type=F32
        ).astype(BF16)
        for i in range(3)
    ]
    for view in range(heads):
        part = slice(view * rows, (view + 1) * rows)
        scores = lax.dot_general(
            arranged[0][part], arranged[1][part], (((1,), (1,)), ((), ())),
            preferred_element_type=F32,
        ) * width ** (-0.5)
        powers = jnp.exp(scores - jnp.max(scores, axis=-1, keepdims=True))
        probs = (powers / jnp.sum(powers, axis=-1, keepdims=True)).astype(BF16)
        attended[part] = jnp.dot(probs, arranged[2][part], preferred_element_type=F32)
    query_rows[...] = arranged[0]

    for hop in range(1, quads):

        @pl.when(quad - hop >= 0)
        def _():
            index = quad - hop
            spread_copy(0, index).wait_recv()

            @pl.when(quad < quads - 1)
            def _():
                spread_copy(0, index).start()

        @pl.when(quad + hop < quads)
        def _():
            index = quad + hop
            spread_copy(1, index).wait_recv()

            @pl.when(quad > 0)
            def _():
                spread_copy(1, index).start()

    fresh = fresh_ref[...].reshape(3 * width, width)
    pre_gate = jnp.dot(query_rows[...], fresh[0:width], preferred_element_type=F32)
    pre_up = jnp.dot(query_rows[...], fresh[width : 2 * width], preferred_element_type=F32)
    target_hidden = (pre_gate * jax.nn.sigmoid(pre_gate) * pre_up).astype(BF16)
    fast_out = jnp.dot(target_hidden, fresh[2 * width :], preferred_element_type=F32)
    normed = fast_out * lax.rsqrt(jnp.mean(fast_out * fast_out, axis=-1, keepdims=True) + EPS)
    mixed[...] = (normed + attended[...]).astype(BF16).reshape(mixed.shape)
    own_columns = pl.ds(pl.multiple_of(head * width, width), width)

    def out_copy(step):
        view = (head + step) % heads
        return remote(
            mixed.at[view],
            out_ref.at[:, own_columns],
            out_send.at[step],
            out_recv.at[step],
            quad * heads + view,
        )

    for step in range(1, heads):
        out_copy(step).start()
    out_ref[:, own_columns] = mixed[head]
    for step in range(1, heads):
        out_copy(step).wait()

    core_copy(0).wait_send()
    core_copy(1).wait_send()
    side_copy.wait_send()
    for index in range(quads):

        @pl.when(quad < index)
        def _():
            up_copy(index).wait_send()

        @pl.when(quad > index)
        def _():
            down_copy(index).wait_send()

        @pl.when((index <= quad) & (quad < quads - 1))
        def _():
            spread_copy(0, index).wait_send()

        @pl.when((index >= quad) & (quad > 0))
        def _():
            spread_copy(1, index).wait_send()


def exchange(keys, values, rates, weights, steps, queries, view_keys, view_values, views):
    n = lax.axis_size("tokens")
    heads = weights.shape[0]
    width = weights.shape[-1]
    rows = queries.shape[0]
    quads = n // heads
    piece = 3 * width // quads
    capacity = 2 * rows // n
    slots = heads * capacity
    owner_lanes = -(-n // 128) * 128
    lane = np.arange(n * slots)
    lanes = np.zeros((8, n * slots), np.int32)
    lanes[0] = lane // slots
    lanes[1] = lane % slots // capacity
    lanes[2] = lane % capacity
    vmem = pl.BlockSpec(memory_space=pltpu.VMEM)
    smem = pl.BlockSpec(memory_space=pltpu.SMEM)
    dma = pltpu.SemaphoreType.DMA
    whole = (3 * width, width)
    parts = (quads, piece, width)
    return pl.pallas_call(
        functools.partial(exchange_kernel, n, heads),
        out_shape=jax.ShapeDtypeStruct((rows, heads * width), BF16),
        in_specs=[vmem, vmem, vmem, vmem, smem] + [vmem] * 5,
        out_specs=vmem,
        scratch_shapes=[
            pltpu.VMEM((3, n * capacity, heads * width), BF16),
            pltpu.VMEM((8, owner_lanes), F32),
            pltpu.VMEM(parts, BF16),
            pltpu.VMEM((n, 3, slots, width), BF16),
            pltpu.VMEM((n, 8, owner_lanes), F32),
            pltpu.VMEM((heads * rows, width), BF16),
            pltpu.VMEM((heads * rows, width), F32),
            pltpu.VMEM((heads, rows, width), BF16),
            pltpu.VMEM(whole, F32),
            pltpu.VMEM((2,) + whole, BF16),
            pltpu.VMEM((2,) + whole, BF16),
            pltpu.VMEM(whole, BF16),
            pltpu.VMEM(whole, BF16),
            pltpu.VMEM(parts, BF16),
            pltpu.VMEM(parts, BF16),
            pltpu.VMEM(parts, BF16),
            pltpu.VMEM(parts, BF16),
            dma((n,)),
            dma((n,)),
            dma((n,)),
            dma((n,)),
            dma((3,)),
            dma((3,)),
            dma((2, quads)),
            dma((2, quads)),
            dma((2, quads)),
            dma((quads,)),
            dma((heads,)),
            dma((heads,)),
        ],
        compiler_params=pltpu.CompilerParams(
            collective_id=0, has_side_effects=True, vmem_limit_bytes=63 * 1024 * 1024
        ),
    )(keys, values, rates, weights, steps, queries, view_keys, view_values, views, jnp.asarray(lanes))


def scene_kernel(
    n,
    heads,
    keys_ref,
    values_ref,
    rates_ref,
    mask_ref,
    weights_ref,
    steps_ref,
    queries_ref,
    view_keys_ref,
    view_values_ref,
    views_ref,
    out_ref,
    key_buf,
    value_buf,
    weight_buf,
    target_grad,
    hidden,
    grad_gate,
    grad_up,
    grad,
    core_out,
    core_in,
    side_out,
    side_in,
    own,
    chain_out,
    chain_in,
    fresh_ref,
    got_q,
    got_kv,
    views_out,
    got_views,
    rank_q,
    rank_kv,
    counts,
    place_q,
    place_kv,
    arranged_q,
    arranged_kv,
    powers,
    attended,
    part_out,
    part_in,
    stats_out,
    stats_in,
    mixed,
    normed,
    load_sem,
    local_sem,
    z_send,
    z_recv,
    y_send,
    y_recv,
    c_send,
    c_recv,
    cy_send,
    cy_recv,
    core_send,
    core_recv,
    side_send,
    side_recv,
    chain_send,
    chain_recv,
    fresh_send,
    fresh_recv,
    part_send,
    part_recv,
    out_send,
    out_recv,
):
    width = out_ref.shape[1] // heads
    rows = out_ref.shape[0]
    planes = n // heads
    piece = 3 * width // heads
    me = lax.axis_index("tokens")
    z, p = me // heads, me % heads
    y, c = p // 2, p % 2
    core_peer = me + 1 - 2 * c
    side_peer = me + 2 - 4 * y
    low = 2 * z < planes
    ahead = jnp.where(low, me + heads, me - heads)
    behind = jnp.where(low, me - heads, me + heads)
    is_end = (z == 0) | (z == planes - 1)

    def plane_of(step):
        return (z + step) % planes

    barrier = pltpu.get_barrier_semaphore()
    for peer in [core_peer, side_peer] + [
        plane_of(step) * heads + p for step in range(1, planes)
    ]:
        pl.semaphore_signal(barrier, inc=1, device_id={"tokens": peer}, device_id_type=MESH)

    def head_at(turn):
        at_mid = jnp.where(turn == 0, 3, jnp.where(turn == 1, 0, 4 - turn))
        place = jnp.where(is_end, 3 - turn, at_mid)
        return jnp.where(low, place, 3 - place)

    def columns(head):
        return pl.ds(pl.multiple_of(head * width, width), width)

    def loads(turn):
        head = head_at(turn)
        return (
            pltpu.make_async_copy(keys_ref.at[:, columns(head)], key_buf.at[turn], load_sem.at[0, turn]),
            pltpu.make_async_copy(weights_ref.at[head], weight_buf.at[turn], load_sem.at[1, turn]),
            pltpu.make_async_copy(values_ref.at[:, columns(head)], value_buf.at[turn], load_sem.at[2, turn]),
        )

    for turn in range(heads):
        for load in loads(turn):
            load.start()

    views_out[...] = jnp.broadcast_to(views_ref[...], views_out.shape)
    here = p * planes + z
    kv_here = c * planes + z
    locals_ = (
        pltpu.make_async_copy(queries_ref.at[:, columns(z)], got_q.at[here], local_sem.at[0]),
        pltpu.make_async_copy(view_keys_ref.at[:, columns(z)], got_kv.at[0, kv_here], local_sem.at[1]),
        pltpu.make_async_copy(view_values_ref.at[:, columns(z)], got_kv.at[1, kv_here], local_sem.at[2]),
    )
    for copy in locals_:
        copy.start()
    got_views[here] = views_out[...]

    pl.semaphore_wait(barrier, planes + 1)

    def z_copy(turn, index):
        plane = head_at(turn)
        source, target = (
            (queries_ref.at[:, columns(plane)], got_q.at[here]),
            (view_keys_ref.at[:, columns(plane)], got_kv.at[0, kv_here]),
            (view_values_ref.at[:, columns(plane)], got_kv.at[1, kv_here]),
            (views_out, got_views.at[here]),
        )[index]
        return remote(
            source, target, z_send.at[index, turn], z_recv.at[index, z], plane * heads + p
        )

    def z_arrived(step, index):
        source, target = ((queries_ref.at[:, columns(z)], got_q.at[here]), (views_out, got_views.at[here]))[
            index == 3
        ]
        remote(
            source, target, z_send.at[index, 0], z_recv.at[index, plane_of(step)], core_peer
        ).wait_recv()

    def y_copy(step, index):
        slot = p * planes + plane_of(step)
        if index == 0:
            source = queries_ref.at[:, columns(z)] if step == 0 else got_q.at[slot]
            target = got_q.at[slot]
        else:
            source = views_out if step == 0 else got_views.at[slot]
            target = got_views.at[slot]
        return remote(source, target, y_send.at[index, step], y_recv.at[index, step], side_peer)

    def c_copy(step, index):
        slot = p * planes + plane_of(step)
        kv_slot = c * planes + plane_of(step)
        target = (
            got_q.at[slot], got_kv.at[0, kv_slot], got_kv.at[1, kv_slot], got_views.at[slot]
        )[index]
        if step == 0:
            source = (
                queries_ref.at[:, columns(z)],
                view_keys_ref.at[:, columns(z)],
                view_values_ref.at[:, columns(z)],
                views_out,
            )[index]
        else:
            source = target
        return remote(source, target, c_send.at[index, step], c_recv.at[index, step], core_peer)

    def cy_copy(step, index):
        slot = (2 * (1 - y) + c) * planes + plane_of(step)
        target = got_q.at[slot] if index == 0 else got_views.at[slot]
        return remote(target, target, cy_send.at[index, step], cy_recv.at[index, step], core_peer)

    for index in (3, 0, 1):
        for turn in (1, 0, 2):
            z_copy(turn, index).start()

    @pl.when(jnp.logical_not(is_end))
    def _():
        for turn in (2, 0, 1):
            z_copy(turn, 2).start()

    for index in (1, 0):
        y_copy(0, index).start()
    for index in (3, 0, 1, 2):
        c_copy(0, index).start()

    def core_copy(turn):
        return remote(
            core_out.at[turn], core_in.at[turn], core_send.at[turn], core_recv.at[turn], core_peer
        )

    chunk = math.gcd(piece, width)
    chunks = piece // chunk

    def chunk_rows(index):
        return slice(index * chunk, (index + 1) * chunk)

    def side_copy(turn, index):
        at = chunk_rows(index)
        return remote(
            side_out.at[turn, at],
            side_in.at[turn, at],
            side_send.at[turn, index],
            side_recv.at[turn, index],
            side_peer,
        )

    def quarter(at_y, at_c):
        return pl.ds(pl.multiple_of((2 * at_y + at_c) * piece, piece), piece)

    def take_core(turn):
        core_copy(turn).wait_recv()
        side_out[turn] = (
            grad[quarter(1 - y, c), :] + core_in[turn, 1 - y].astype(F32)
        ).astype(BF16)
        for index in range(chunks):
            side_copy(turn, index).start()
        own[turn] = grad[quarter(y, c), :] + core_in[turn, y].astype(F32)

    eye = lax.broadcasted_iota(jnp.int32, (rows, rows), 0) == lax.broadcasted_iota(
        jnp.int32, (rows, rows), 1
    )

    def to_column(row):
        parts = [
            jnp.sum(jnp.where(eye, row[:, at : at + rows], 0.0), axis=1, keepdims=True)
            for at in range(0, row.shape[1], rows)
        ]
        return parts[0] if len(parts) == 1 else jnp.concatenate(parts, axis=0)

    def to_row(column):
        return jnp.sum(jnp.where(eye, column, 0.0), axis=0, keepdims=True)

    over_rows = (((0,), (0,)), ((), ()))
    over_last = (((1,), (1,)), ((), ()))

    def is_early(step):
        return is_end & (plane_of(step) * heads + p == ahead)

    def hand_on(step):
        z_arrived(step, 0)
        y_copy(step, 0).start()
        c_copy(step, 0).start()

    def one_head(turn, carry):
        for load in loads(turn):
            load.wait()
        rate = to_column(rates_ref[pl.ds(head_at(turn), 1), :] * mask_ref[...].astype(F32))
        key_rows = key_buf[turn]
        target_grad[...] = (-rate * value_buf[turn].astype(F32)).astype(BF16)
        pre_gate = jnp.dot(key_rows, weight_buf[turn, 0], preferred_element_type=F32)
        pre_up = jnp.dot(key_rows, weight_buf[turn, 1], preferred_element_type=F32)
        back = lax.dot_general(
            target_grad[...], weight_buf[turn, 2], over_last, preferred_element_type=F32
        )
        sigma = jax.nn.sigmoid(pre_gate)
        activated = pre_gate * sigma
        hidden[...] = (activated * pre_up).astype(BF16)
        grad_gate[...] = (back * pre_up * sigma * (1.0 + pre_gate * (1.0 - sigma))).astype(BF16)
        grad_up[...] = (back * activated).astype(BF16)

        for step in (1, planes - 1):

            @pl.when((turn == 1) & is_early(step))
            def _():
                hand_on(step)

        @pl.when(turn > 0)
        def _():
            take_core(turn - 1)

        grad[0:width] = lax.dot_general(
            key_buf[turn], grad_gate[...], over_rows, preferred_element_type=F32
        )
        grad[width : 2 * width] = lax.dot_general(
            key_buf[turn], grad_up[...], over_rows, preferred_element_type=F32
        )
        grad[2 * width : 3 * width] = lax.dot_general(
            hidden[...], target_grad[...], over_rows, preferred_element_type=F32
        )
        for at_y in range(2):
            core_out[turn, at_y] = grad[quarter(at_y, 1 - c), :].astype(BF16)
        core_copy(turn).start()

        @pl.when(turn == 1)
        def _():
            for step in range(1, planes):
                z_arrived(step, 3)
                y_copy(step, 1).start()
                c_copy(step, 3).start()

        @pl.when(turn == 2)
        def _():
            for step in range(1, planes):

                @pl.when(jnp.logical_not(is_early(step)))
                def _():
                    hand_on(step)

        return carry

    lax.fori_loop(0, heads, one_head, 0)
    take_core(heads - 1)

    def chain_copy(out_slot, in_slot, index, peer):
        at = chunk_rows(index)
        return remote(
            chain_out.at[out_slot, at],
            chain_in.at[in_slot, at],
            chain_send.at[out_slot, index],
            chain_recv.at[in_slot, index],
            peer,
        )

    hops = ((0, 3, ahead), (3, 5, behind), (1, 4, ahead))

    def pass_on(turn, index):
        side_copy(turn, index).wait_recv()
        at = chunk_rows(index)

        @pl.when(is_end)
        def _():
            chain_out[turn, at] = (own[turn, at] + side_in[turn, at].astype(F32)).astype(BF16)
            chain_copy(turn, turn, index, ahead).start()

        @pl.when(jnp.logical_not(is_end))
        def _():
            taken, given, peer = hops[turn]
            chain_copy(turn, taken, index, peer).wait_recv()
            chain_out[turn, at] = (
                own[turn, at] + side_in[turn, at].astype(F32) + chain_in[taken, at].astype(F32)
            ).astype(BF16)
            chain_copy(turn, given, index, peer).start()

    views = 2 * planes
    def ones(where):
        return where.astype(F32).astype(BF16)

    def rank_rows():
        square = (n * views, n * views)
        low_axis = lax.broadcasted_iota(jnp.int32, square, 0)
        high_axis = lax.broadcasted_iota(jnp.int32, square, 1)

        def order(index):
            slot = index // views
            return slot % planes * heads + slot // planes

        listed = low_axis % views
        side_of = jnp.where(listed < planes, y, 1 - y)
        wanted = listed % planes * heads + 2 * side_of + c
        is_hit = got_views[...].reshape(n * views, rows) == wanted[:, :rows]
        hits = ones(is_hit)
        within = jnp.dot(
            hits,
            ones(
                lax.broadcasted_iota(jnp.int32, (rows, rows), 0)
                < lax.broadcasted_iota(jnp.int32, (rows, rows), 1)
            ),
            preferred_element_type=F32,
        )
        before = (low_axis % views == high_axis % views) & (order(high_axis) < order(low_axis))
        in_column = high_axis // (views * n // 2) == y

        def earlier(table):
            found = jnp.dot(ones(table), hits, preferred_element_type=F32)
            return jnp.sum(found, axis=1, keepdims=True)

        rank_q[...] = jnp.where(is_hit, earlier(before) + within, -1.0).reshape(rank_q.shape)
        rank_kv[...] = jnp.where(is_hit, earlier(before & in_column) + within, -1.0).reshape(
            rank_kv.shape
        )
        counts[...] = jnp.broadcast_to(
            earlier(((low_axis % views == high_axis % views) & in_column)[0:views]), counts.shape
        )

    def spots(ranks, first, sources, view):
        row = jnp.concatenate(
            [ranks[first + source, view : view + 1, :] for source in range(sources)], axis=1
        )
        at = lax.broadcasted_iota(jnp.int32, (rows, sources * rows), 0).astype(F32)
        return ones(at == row)

    def spot_q(group):
        for view in range(planes):
            place_q[group, view * rows : (view + 1) * rows] = spots(
                rank_q, 0, n, group * planes + view
            )

    def arrange_q(group):
        arranged_q[group] = jnp.dot(
            place_q[group], got_q[...].reshape(n * rows, width), preferred_element_type=F32
        ).astype(BF16)

    def spot_kv(group):
        for view in range(planes):
            place_kv[group, view * rows : (view + 1) * rows] = spots(
                rank_kv, y * (n // 2), n // 2, group * planes + view
            )

    def arrange_kv(group, index):
        arranged_kv[group, index] = jnp.dot(
            place_kv[group],
            got_kv[index].reshape(n // 2 * rows, width),
            preferred_element_type=F32,
        ).astype(BF16)

    def view_rows(view):
        return pl.ds(pl.multiple_of(view * rows, rows), rows)

    def weigh(group, turn):
        view = head_at(turn)
        part = view_rows(view)
        scores = lax.dot_general(
            arranged_q[group, part], arranged_kv[group, 0, part], over_last, preferred_element_type=F32
        ) * width ** (-0.5)
        at = group * planes + view
        real = lax.broadcasted_iota(jnp.int32, (rows, rows), 1).astype(F32) < counts[pl.ds(at, 1), :]
        top = jnp.max(jnp.where(real, scores, LOWEST), axis=-1, keepdims=True)
        exps = jnp.where(real, jnp.exp(jnp.where(real, scores - top, 0.0)), 0.0)
        powers[group, turn] = exps.astype(BF16)
        return top, jnp.sum(exps, axis=-1, keepdims=True)

    def attend(group, turn):
        return jnp.dot(
            powers[group, turn],
            arranged_kv[group, 1, view_rows(head_at(turn))],
            preferred_element_type=F32,
        )

    def part_copy(turn, index):
        view = head_at(turn)
        source, target = ((part_out, part_in), (stats_out, stats_in))[index]
        return remote(
            source.at[view],
            target.at[view],
            part_send.at[index, turn],
            part_recv.at[index, turn],
            side_peer,
        )

    for index in range(chunks):
        pass_on(0, index)
    for step in range(planes):
        y_copy(step, 1).wait_recv()
        cy_copy(step, 1).start()
    for step in range(planes):
        cy_copy(step, 1).wait_recv()
        c_copy(step, 3).wait_recv()
    rank_rows()
    spot_q(1)
    pass_on(1, 0)
    spot_q(0)
    pass_on(1, 1)
    spot_kv(1)
    pass_on(1, 2)

    @pl.when(is_end)
    def _():
        for turn in (1, 2):
            z_copy(turn, 2).start()

    spot_kv(0)
    for copy in locals_:
        copy.wait()
    for step in range(1, planes):
        z_arrived(step, 1)
        c_copy(step, 1).start()
    for step in range(planes):
        y_copy(step, 0).wait_recv()
        cy_copy(step, 0).start()
    for step in range(planes):
        c_copy(step, 1).wait_recv()
    arrange_kv(1, 0)
    pass_on(2, 0)
    arrange_kv(0, 0)
    for step in range(planes):
        cy_copy(step, 0).wait_recv()
        c_copy(step, 0).wait_recv()
    arrange_q(1)
    pass_on(2, 1)
    arrange_q(0)
    pass_on(2, 2)

    @pl.when(is_end)
    def _():
        for turn in (0,):
            z_copy(turn, 2).start()

    for turn in range(heads):
        view = head_at(turn)
        top, total = weigh(1, turn)
        stats_out[view, 0:1, :] = to_row(top)
        stats_out[view, 1:2, :] = to_row(total)
        part_copy(turn, 1).start()

    last = heads - 1

    def fresh_copy(way, index):
        slot = 2 * (1 - y) + c if way == 2 else p
        at = chunk_rows(index)
        return remote(
            fresh_ref.at[slot, at],
            fresh_ref.at[slot, at],
            fresh_send.at[way, index],
            fresh_recv.at[way, index],
            side_peer if way == 0 else core_peer,
        )

    for index in range(chunks):
        at = chunk_rows(index)
        side_copy(last, index).wait_recv()
        own[last, at] += side_in[last, at].astype(F32)

        @pl.when(is_end)
        def _():
            chain_copy(0, 5, index, ahead).wait_recv()
            own[last, at] += chain_in[5, at].astype(F32)

        @pl.when(jnp.logical_not(is_end))
        def _():
            for slot in (2, 4):
                chain_copy(0, slot, index, ahead).wait_recv()
            own[last, at] += chain_in[2, at].astype(F32) + chain_in[4, at].astype(F32)

        gradient = own[last, at]
        scaled = gradient * lax.rsqrt(jnp.mean(gradient * gradient, axis=-1, keepdims=True) + EPS)
        start = p * piece + index * chunk
        old = weight_buf[
            last, start // width, pl.ds(pl.multiple_of(start % width, chunk), chunk), :
        ]
        fresh_ref[p, at, :] = (old.astype(F32) - steps_ref[z] * scaled).astype(BF16)
        fresh_copy(0, index).start()
        fresh_copy(1, index).start()

    tops, totals = [], []
    for turn in range(heads):
        top, total = weigh(0, turn)
        tops.append(top)
        totals.append(total)

    for step in range(1, planes):
        z_arrived(step, 2)
        c_copy(step, 2).start()
    for step in range(planes):
        c_copy(step, 2).wait_recv()
    arrange_kv(1, 1)
    for turn in range(heads):
        part_out[head_at(turn)] = attend(1, turn).astype(BF16)
        part_copy(turn, 0).start()
    for index in range(chunks):
        fresh_copy(0, index).wait_recv()
        fresh_copy(2, index).start()
    arrange_kv(0, 1)
    for turn in range(heads):
        attended[turn] = attend(0, turn)

    for index in range(chunks):
        fresh_copy(1, index).wait_recv()
        fresh_copy(2, index).wait_recv()

    fresh = fresh_ref[...].reshape(3 * width, width)
    query_rows = arranged_q[0]
    pre_gate = jnp.dot(query_rows, fresh[0:width], preferred_element_type=F32)
    pre_up = jnp.dot(query_rows, fresh[width : 2 * width], preferred_element_type=F32)
    target_hidden = (pre_gate * jax.nn.sigmoid(pre_gate) * pre_up).astype(BF16)
    fast_out = jnp.dot(target_hidden, fresh[2 * width :], preferred_element_type=F32)
    normed[...] = fast_out * lax.rsqrt(
        jnp.mean(fast_out * fast_out, axis=-1, keepdims=True) + EPS
    )

    def out_copy(turn, plane, source):
        return remote(
            mixed.at[turn],
            out_ref.at[:, columns(source)],
            out_send.at[turn],
            out_recv.at[source],
            plane * heads + p,
        )

    for turn in range(heads):
        view = head_at(turn)
        for index in range(2):
            part_copy(turn, index).wait_recv()
        other_top = to_column(stats_in[view, 0:1, :])
        other_total = to_column(stats_in[view, 1:2, :])
        top = jnp.maximum(tops[turn], other_top)
        scale, other_scale = jnp.exp(tops[turn] - top), jnp.exp(other_top - top)
        weight = 1.0 / (scale * totals[turn] + other_scale * other_total)
        result = (
            normed[pl.ds(pl.multiple_of(view * rows, rows), rows)]
            + attended[turn] * (scale * weight)
            + part_in[view].astype(F32) * (other_scale * weight)
        ).astype(BF16)
        if turn < last:
            mixed[turn] = result
            out_copy(turn, view, z).start()
        else:
            out_ref[:, columns(z)] = result

    for step in range(1, planes):
        out_copy(0, z, plane_of(step)).wait_recv()
    for turn in range(last):
        out_copy(turn, z, z).wait_send()
        for index in range(chunks):
            chain_copy(turn, 0, index, ahead).wait_send()
            fresh_copy(turn, index).wait_send()
    for turn in range(heads):
        core_copy(turn).wait_send()
        for index in range(2):
            part_copy(turn, index).wait_send()
        for index in range(chunks):
            side_copy(turn, index).wait_send()
    for step in range(planes):
        for index in range(4):
            c_copy(step, index).wait_send()
            if step < last:
                z_copy(step, index).wait_send()
        for index in range(2):
            y_copy(step, index).wait_send()
            cy_copy(step, index).wait_send()


def scene(keys, values, rates, mask, weights, steps, queries, view_keys, view_values, views):
    n = lax.axis_size("tokens")
    heads, _, _, width = weights.shape
    rows = queries.shape[0]
    depth = keys.shape[0]
    planes = n // heads
    piece = 3 * width // heads
    chunks = piece // math.gcd(piece, width)
    slots = 2 * planes
    vmem = pl.BlockSpec(memory_space=pltpu.VMEM)
    smem = pl.BlockSpec(memory_space=pltpu.SMEM)
    hbm = pl.BlockSpec(memory_space=pl.ANY)
    dma = pltpu.SemaphoreType.DMA

    def half(*shape):
        return pltpu.VMEM(shape, BF16)

    def single(*shape):
        return pltpu.VMEM(shape, F32)

    return pl.pallas_call(
        functools.partial(scene_kernel, n, heads),
        out_shape=jax.ShapeDtypeStruct((rows, heads * width), BF16),
        in_specs=[hbm, hbm, vmem, vmem, hbm, smem, hbm, hbm, hbm, vmem],
        out_specs=vmem,
        scratch_shapes=[
            half(heads, depth, width),
            half(heads, depth, width),
            half(heads, 3, width, width),
            half(depth, width),
            half(depth, width),
            half(depth, width),
            half(depth, width),
            single(3 * width, width),
            half(heads, 2, piece, width),
            half(heads, 2, piece, width),
            half(heads, piece, width),
            half(heads, piece, width),
            single(heads, piece, width),
            half(3, piece, width),
            half(6, piece, width),
            half(heads, piece, width),
            half(n, rows, width),
            half(2, n // 2, rows, width),
            pltpu.VMEM((slots, rows), jnp.int32),
            pltpu.VMEM((n, slots, rows), jnp.int32),
            single(n, slots, rows),
            single(n, slots, rows),
            single(slots, rows),
            half(2, planes * rows, n * rows),
            half(2, planes * rows, n // 2 * rows),
            half(2, planes * rows, width),
            half(2, 2, planes * rows, width),
            half(2, heads, rows, rows),
            single(planes, rows, width),
            half(planes, rows, width),
            half(planes, rows, width),
            single(planes, 8, rows),
            single(planes, 8, rows),
            half(planes - 1, rows, width),
            single(planes * rows, width),
            dma((3, heads)),
            dma((3,)),
            dma((4, planes)),
            dma((4, planes)),
            dma((2, planes)),
            dma((2, planes)),
            dma((4, planes)),
            dma((4, planes)),
            dma((2, planes)),
            dma((2, planes)),
            dma((heads,)),
            dma((heads,)),
            dma((heads, chunks)),
            dma((heads, chunks)),
            dma((3, chunks)),
            dma((6, chunks)),
            dma((3, chunks)),
            dma((3, chunks)),
            dma((2, heads)),
            dma((2, heads)),
            dma((planes - 1,)),
            dma((planes,)),
        ],
        compiler_params=pltpu.CompilerParams(
            collective_id=1, has_side_effects=True, vmem_limit_bytes=63 * 1024 * 1024
        ),
    )(keys, values, rates, mask, weights, steps, queries, view_keys, view_values, views)


def on_device(
    update_keys,
    update_values,
    update_rates,
    update_mask,
    fast_weights,
    step_sizes,
    target_queries,
    target_keys,
    target_values,
    target_views,
):
    n = lax.axis_size("tokens")
    heads = fast_weights.shape[0]
    if heads == 4 and n == heads * heads:
        return scene(
            update_keys,
            update_values,
            update_rates.T,
            update_mask[None, :],
            fast_weights,
            step_sizes,
            target_queries,
            target_keys,
            target_values,
            target_views[None, :],
        )
    rates = update_rates * update_mask.astype(F32)[:, None]
    return exchange(
        update_keys,
        update_values,
        rates,
        fast_weights,
        step_sizes,
        target_queries,
        target_keys,
        target_values,
        target_views[None, :],
    )


def solution(mesh):
    rows = P(("groups", "tokens"), None)
    flat = P(("groups", "tokens"))
    return jax.shard_map(
        on_device,
        mesh=mesh,
        in_specs=(rows, rows, rows, flat, P(), P(), rows, rows, rows, flat),
        out_specs=rows,
        check_vma=False,
    )
```

```python
import functools
import math

import jax
import jax.numpy as jnp
import numpy as np
from jax import lax
from jax.experimental import pallas as pl
from jax.experimental.pallas import tpu as pltpu
from jax.sharding import PartitionSpec as P

EPS = 1e-05
MESH = pl.DeviceIdType.MESH
F32 = jnp.float32
BF16 = jnp.bfloat16
LOWEST = -1e30


def remote(src, dst, send_sem, recv_sem, peer):
    return pltpu.make_async_remote_copy(
        src_ref=src,
        dst_ref=dst,
        send_sem=send_sem,
        recv_sem=recv_sem,
        device_id={"tokens": peer},
        device_id_type=MESH,
    )


def exchange_kernel(
    n,
    heads,
    keys_ref,
    values_ref,
    rates_ref,
    weights_ref,
    steps_ref,
    queries_ref,
    view_keys_ref,
    view_values_ref,
    views_ref,
    lanes_ref,
    out_ref,
    packed_ref,
    meta_ref,
    fresh_ref,
    got_ref,
    got_meta_ref,
    query_rows,
    attended,
    mixed,
    grad,
    core_out,
    core_in,
    side_out,
    side_in,
    up_out,
    up_in,
    down_out,
    down_in,
    a2a_send,
    a2a_recv,
    meta_send,
    meta_recv,
    pair_send,
    pair_recv,
    chain_send,
    chain_recv,
    spread_send,
    spread_recv,
    out_send,
    out_recv,
):
    width = weights_ref.shape[-1]
    rows = queries_ref.shape[0]
    quads = n // heads
    piece = 3 * width // quads
    slots = packed_ref.shape[1] // quads
    capacity = slots // heads
    me = lax.axis_index("tokens")
    quad = me // heads
    head = me % heads
    core = head % 2
    side = head // 2
    core_peer = me + 1 - 2 * core
    side_peer = me + 2 - 4 * side

    barrier = pltpu.get_barrier_semaphore()
    for step in range(1, n):
        pl.semaphore_signal(
            barrier, inc=1, device_id={"tokens": (me + step) % n}, device_id_type=MESH
        )

    owner = views_ref[0:1, :]
    hits = lax.broadcasted_iota(jnp.int32, (meta_ref.shape[1], rows), 0) == owner
    hits = hits.astype(F32).astype(BF16)
    earlier = (
        lax.broadcasted_iota(jnp.int32, (rows, rows), 0)
        < lax.broadcasted_iota(jnp.int32, (rows, rows), 1)
    ).astype(F32).astype(BF16)
    before = jnp.dot(hits, earlier, preferred_element_type=F32)
    rank = jnp.sum(hits.astype(F32) * before, axis=0, keepdims=True).astype(jnp.int32)
    meta_ref[...] = lax.dot_general(
        jnp.ones((meta_ref.shape[0], rows), BF16),
        hits,
        (((1,), (1,)), ((), ())),
        preferred_element_type=F32,
    )
    pick = (
        lax.broadcasted_iota(jnp.int32, (n * capacity, rows), 0) == owner * capacity + rank
    ).astype(F32).astype(BF16)
    for index, array in enumerate((queries_ref, view_keys_ref, view_values_ref)):
        packed_ref[index] = jnp.dot(pick, array[...], preferred_element_type=F32).astype(BF16)

    pl.semaphore_wait(barrier, n - 1)

    near = [step for step in range(1, n) if step % heads < 2]
    cross = [step for step in range(1, n) if step % heads >= 2]
    early = near[::-1]
    late = cross[::-1]

    def peer_of(step):
        place, total = me, 0
        unit = 1
        while unit < n:
            bit = place % 2
            total = total + unit * ((1 - bit) if (step // unit) % 2 else bit)
            place = place // 2
            unit *= 2
        return total

    def block_copy(step):
        peer = peer_of(step)
        rows = pl.ds(pl.multiple_of((peer // heads) * slots, slots), slots)
        columns = pl.ds(pl.multiple_of((peer % heads) * width, width), width)
        return remote(
            packed_ref.at[:, rows, columns],
            got_ref.at[me],
            a2a_send.at[step],
            a2a_recv.at[step],
            peer,
        )

    def meta_copy(step):
        peer = peer_of(step)
        return remote(
            meta_ref, got_meta_ref.at[me], meta_send.at[step], meta_recv.at[step], peer
        )

    for step in range(1, n):
        meta_copy(step).start()
    for step in early:
        block_copy(step).start()
    got_meta_ref[me] = meta_ref[...]
    got_ref[me] = packed_ref[
        :,
        pl.ds(pl.multiple_of(quad * slots, slots), slots),
        pl.ds(pl.multiple_of(head * width, width), width),
    ]

    def core_copy(slot):
        return remote(
            core_out.at[slot], core_in.at[slot], pair_send.at[slot], pair_recv.at[slot], core_peer
        )

    side_copy = remote(side_out, side_in, pair_send.at[2], pair_recv.at[2], side_peer)

    def one_head(turn, carry):
        on_side = jnp.where(turn < 2, 1 - side, side)
        on_core = jnp.where(turn % 2 == 0, 1 - core, core)
        now = on_side * 2 + on_core
        columns = pl.ds(pl.multiple_of(now * width, width), width)
        key_rows = keys_ref[:, columns]
        rates = rates_ref[...]
        lanes = lax.broadcasted_iota(jnp.int32, rates.shape, 1)
        rate = jnp.sum(jnp.where(lanes == now, rates, 0.0), axis=1, keepdims=True)
        target_grad = (-rate * values_ref[:, columns].astype(F32)).astype(BF16)
        pre_gate = jnp.dot(key_rows, weights_ref[now, 0], preferred_element_type=F32)
        pre_up = jnp.dot(key_rows, weights_ref[now, 1], preferred_element_type=F32)
        back = lax.dot_general(
            target_grad,
            weights_ref[now, 2],
            (((1,), (1,)), ((), ())),
            preferred_element_type=F32,
        )
        sigma = jax.nn.sigmoid(pre_gate)
        activated = pre_gate * sigma
        hidden = (activated * pre_up).astype(BF16)
        grad_gate = (back * pre_up * sigma * (1.0 + pre_gate * (1.0 - sigma))).astype(BF16)
        grad_up = (back * activated).astype(BF16)
        over_rows = (((0,), (0,)), ((), ()))
        grad[0:width] = lax.dot_general(
            key_rows, grad_gate, over_rows, preferred_element_type=F32
        )
        grad[width : 2 * width] = lax.dot_general(
            key_rows, grad_up, over_rows, preferred_element_type=F32
        )
        grad[2 * width : 3 * width] = lax.dot_general(
            hidden, target_grad, over_rows, preferred_element_type=F32
        )

        @pl.when(turn == 0)
        def _():
            core_out[0] = grad[...].astype(BF16)
            core_copy(0).start()

        @pl.when(turn == 1)
        def _():
            core_copy(0).wait_recv()
            side_out[...] = (grad[...] + core_in[0].astype(F32)).astype(BF16)
            side_copy.start()
            for step in late:
                block_copy(step).start()

        @pl.when(turn == 2)
        def _():
            core_out[1] = grad[...].astype(BF16)
            core_copy(1).start()

        return carry

    lax.fori_loop(0, 4, one_head, 0)
    core_copy(1).wait_recv()
    side_copy.wait_recv()

    def rows_of(index):
        return pl.ds(index * piece, piece)

    def own_part(rows):
        return grad[rows, :] + core_in[1, rows, :].astype(F32) + side_in[rows, :].astype(F32)

    def up_copy(index):
        return remote(
            up_out.at[index],
            up_in.at[index],
            chain_send.at[0, index],
            chain_recv.at[0, index],
            me + heads,
        )

    def down_copy(index):
        return remote(
            down_out.at[index],
            down_in.at[index],
            chain_send.at[1, index],
            chain_recv.at[1, index],
            me - heads,
        )

    def send_up(index):
        @pl.when(quad == 0)
        def _():
            up_out[index] = own_part(rows_of(index)).astype(BF16)
            up_copy(index).start()

        @pl.when((quad > 0) & (quad < index))
        def _():
            up_copy(index).wait_recv()
            up_out[index] = (own_part(rows_of(index)) + up_in[index].astype(F32)).astype(BF16)
            up_copy(index).start()

    def send_down(index):
        @pl.when(quad == quads - 1)
        def _():
            down_out[index] = own_part(rows_of(index)).astype(BF16)
            down_copy(index).start()

        @pl.when((quad < quads - 1) & (quad > index))
        def _():
            down_copy(index).wait_recv()
            down_out[index] = (own_part(rows_of(index)) + down_in[index].astype(F32)).astype(BF16)
            down_copy(index).start()

    @pl.when(2 * quad < quads)
    def _():
        for turn in range(quads - 1):
            send_up(quads - 1 - turn)
            send_down(turn)

    @pl.when(2 * quad >= quads)
    def _():
        for turn in range(quads - 1):
            send_down(turn)
            send_up(quads - 1 - turn)

    mine = pl.ds(pl.multiple_of(quad * piece, piece), piece)
    grad[mine, :] = own_part(mine)

    @pl.when(quad > 0)
    def _():
        up_copy(quad).wait_recv()
        grad[mine, :] += up_in[quad].astype(F32)

    @pl.when(quad < quads - 1)
    def _():
        down_copy(quad).wait_recv()
        grad[mine, :] += down_in[quad].astype(F32)

    total = grad[mine, :]
    scaled = total * lax.rsqrt(jnp.mean(total * total, axis=-1, keepdims=True) + EPS)
    first = quad * piece
    block = math.gcd(piece, width)
    for part in range(piece // block):
        start = first + part * block
        old = weights_ref[
            head, start // width, pl.ds(pl.multiple_of(start % width, block), block), :
        ]
        fresh_ref[quad, part * block : (part + 1) * block, :] = (
            old.astype(F32) - steps_ref[head] * scaled[part * block : (part + 1) * block, :]
        ).astype(BF16)

    def spread_copy(way, index):
        return remote(
            fresh_ref.at[index],
            fresh_ref.at[index],
            spread_send.at[way, index],
            spread_recv.at[index],
            me + heads if way == 0 else me - heads,
        )

    @pl.when(quad < quads - 1)
    def _():
        spread_copy(0, quad).start()

    @pl.when(quad > 0)
    def _():
        spread_copy(1, quad).start()

    for step in range(1, n):
        meta_copy(step).wait()
        block_copy(step).wait()
    lane_source, lane_view, lane_slot = (lanes_ref[i : i + 1, :] for i in range(3))
    lane_count = lanes_ref.shape[1]
    counts = got_meta_ref[:, 0, :].astype(BF16)
    sources = lax.broadcasted_iota(jnp.int32, (n, lane_count), 0)
    over_source = (((0,), (0,)), ((), ()))
    same = (sources == lane_source).astype(F32).astype(BF16)
    lower = (sources < lane_source).astype(F32).astype(BF16)
    owners = lax.broadcasted_iota(jnp.int32, (meta_ref.shape[1], lane_count), 0)
    wanted = owners == lane_view + quad * heads

    def lane_sum(table):
        found = lax.dot_general(counts, table, over_source, preferred_element_type=F32)
        return jnp.sum(jnp.where(wanted, found, 0.0), axis=0, keepdims=True).astype(jnp.int32)

    place_at = jnp.where(
        lane_slot < lane_sum(same), lane_view * rows + lane_sum(lower) + lane_slot, -1
    )
    place = (
        lax.broadcasted_iota(jnp.int32, (heads * rows, lane_count), 0) == place_at
    ).astype(F32).astype(BF16)
    arranged = [
        jnp.dot(
            place, got_ref[:, i].reshape(lane_count, width), preferred_element_type=F32
        ).astype(BF16)
        for i in range(3)
    ]
    for view in range(heads):
        part = slice(view * rows, (view + 1) * rows)
        scores = lax.dot_general(
            arranged[0][part], arranged[1][part], (((1,), (1,)), ((), ())),
            preferred_element_type=F32,
        ) * width ** (-0.5)
        powers = jnp.exp(scores - jnp.max(scores, axis=-1, keepdims=True))
        probs = (powers / jnp.sum(powers, axis=-1, keepdims=True)).astype(BF16)
        attended[part] = jnp.dot(probs, arranged[2][part], preferred_element_type=F32)
    query_rows[...] = arranged[0]

    for hop in range(1, quads):

        @pl.when(quad - hop >= 0)
        def _():
            index = quad - hop
            spread_copy(0, index).wait_recv()

            @pl.when(quad < quads - 1)
            def _():
                spread_copy(0, index).start()

        @pl.when(quad + hop < quads)
        def _():
            index = quad + hop
            spread_copy(1, index).wait_recv()

            @pl.when(quad > 0)
            def _():
                spread_copy(1, index).start()

    fresh = fresh_ref[...].reshape(3 * width, width)
    pre_gate = jnp.dot(query_rows[...], fresh[0:width], preferred_element_type=F32)
    pre_up = jnp.dot(query_rows[...], fresh[width : 2 * width], preferred_element_type=F32)
    target_hidden = (pre_gate * jax.nn.sigmoid(pre_gate) * pre_up).astype(BF16)
    fast_out = jnp.dot(target_hidden, fresh[2 * width :], preferred_element_type=F32)
    normed = fast_out * lax.rsqrt(jnp.mean(fast_out * fast_out, axis=-1, keepdims=True) + EPS)
    mixed[...] = (normed + attended[...]).astype(BF16).reshape(mixed.shape)
    own_columns = pl.ds(pl.multiple_of(head * width, width), width)

    def out_copy(step):
        view = (head + step) % heads
        return remote(
            mixed.at[view],
            out_ref.at[:, own_columns],
            out_send.at[step],
            out_recv.at[step],
            quad * heads + view,
        )

    for step in range(1, heads):
        out_copy(step).start()
    out_ref[:, own_columns] = mixed[head]
    for step in range(1, heads):
        out_copy(step).wait()

    core_copy(0).wait_send()
    core_copy(1).wait_send()
    side_copy.wait_send()
    for index in range(quads):

        @pl.when(quad < index)
        def _():
            up_copy(index).wait_send()

        @pl.when(quad > index)
        def _():
            down_copy(index).wait_send()

        @pl.when((index <= quad) & (quad < quads - 1))
        def _():
            spread_copy(0, index).wait_send()

        @pl.when((index >= quad) & (quad > 0))
        def _():
            spread_copy(1, index).wait_send()


def exchange(keys, values, rates, weights, steps, queries, view_keys, view_values, views):
    n = lax.axis_size("tokens")
    heads = weights.shape[0]
    width = weights.shape[-1]
    rows = queries.shape[0]
    quads = n // heads
    piece = 3 * width // quads
    capacity = 2 * rows // n
    slots = heads * capacity
    owner_lanes = -(-n // 128) * 128
    lane = np.arange(n * slots)
    lanes = np.zeros((8, n * slots), np.int32)
    lanes[0] = lane // slots
    lanes[1] = lane % slots // capacity
    lanes[2] = lane % capacity
    vmem = pl.BlockSpec(memory_space=pltpu.VMEM)
    smem = pl.BlockSpec(memory_space=pltpu.SMEM)
    dma = pltpu.SemaphoreType.DMA
    whole = (3 * width, width)
    parts = (quads, piece, width)
    return pl.pallas_call(
        functools.partial(exchange_kernel, n, heads),
        out_shape=jax.ShapeDtypeStruct((rows, heads * width), BF16),
        in_specs=[vmem, vmem, vmem, vmem, smem] + [vmem] * 5,
        out_specs=vmem,
        scratch_shapes=[
            pltpu.VMEM((3, n * capacity, heads * width), BF16),
            pltpu.VMEM((8, owner_lanes), F32),
            pltpu.VMEM(parts, BF16),
            pltpu.VMEM((n, 3, slots, width), BF16),
            pltpu.VMEM((n, 8, owner_lanes), F32),
            pltpu.VMEM((heads * rows, width), BF16),
            pltpu.VMEM((heads * rows, width), F32),
            pltpu.VMEM((heads, rows, width), BF16),
            pltpu.VMEM(whole, F32),
            pltpu.VMEM((2,) + whole, BF16),
            pltpu.VMEM((2,) + whole, BF16),
            pltpu.VMEM(whole, BF16),
            pltpu.VMEM(whole, BF16),
            pltpu.VMEM(parts, BF16),
            pltpu.VMEM(parts, BF16),
            pltpu.VMEM(parts, BF16),
            pltpu.VMEM(parts, BF16),
            dma((n,)),
            dma((n,)),
            dma((n,)),
            dma((n,)),
            dma((3,)),
            dma((3,)),
            dma((2, quads)),
            dma((2, quads)),
            dma((2, quads)),
            dma((quads,)),
            dma((heads,)),
            dma((heads,)),
        ],
        compiler_params=pltpu.CompilerParams(
            collective_id=0, has_side_effects=True, vmem_limit_bytes=63 * 1024 * 1024
        ),
    )(keys, values, rates, weights, steps, queries, view_keys, view_values, views, jnp.asarray(lanes))


def scene_kernel(
    n,
    heads,
    keys_ref,
    values_ref,
    rates_ref,
    mask_ref,
    weights_ref,
    steps_ref,
    queries_ref,
    view_keys_ref,
    view_values_ref,
    views_ref,
    out_ref,
    key_buf,
    value_buf,
    weight_buf,
    target_grad,
    hidden,
    grad_gate,
    grad_up,
    grad,
    core_out,
    core_in,
    side_out,
    side_in,
    own,
    chain_out,
    chain_in,
    fresh_ref,
    got_q,
    got_kv,
    views_out,
    got_views,
    rank_q,
    rank_kv,
    counts,
    place_q,
    place_kv,
    arranged_q,
    arranged_kv,
    powers,
    attended,
    part_out,
    part_in,
    stats_out,
    stats_in,
    mixed,
    normed,
    load_sem,
    local_sem,
    z_send,
    z_recv,
    y_send,
    y_recv,
    c_send,
    c_recv,
    cy_send,
    cy_recv,
    core_send,
    core_recv,
    side_send,
    side_recv,
    chain_send,
    chain_recv,
    fresh_send,
    fresh_recv,
    part_send,
    part_recv,
    out_send,
    out_recv,
):
    width = out_ref.shape[1] // heads
    rows = out_ref.shape[0]
    planes = n // heads
    piece = 3 * width // heads
    me = lax.axis_index("tokens")
    z, p = me // heads, me % heads
    y, c = p // 2, p % 2
    core_peer = me + 1 - 2 * c
    side_peer = me + 2 - 4 * y
    low = 2 * z < planes
    ahead = jnp.where(low, me + heads, me - heads)
    behind = jnp.where(low, me - heads, me + heads)
    is_end = (z == 0) | (z == planes - 1)

    def plane_of(step):
        return (z + step) % planes

    barrier = pltpu.get_barrier_semaphore()
    for peer in [core_peer, side_peer] + [
        plane_of(step) * heads + p for step in range(1, planes)
    ]:
        pl.semaphore_signal(barrier, inc=1, device_id={"tokens": peer}, device_id_type=MESH)

    def head_at(turn):
        at_mid = jnp.where(turn == 0, 3, jnp.where(turn == 1, 0, 4 - turn))
        place = jnp.where(is_end, 3 - turn, at_mid)
        return jnp.where(low, place, 3 - place)

    def columns(head):
        return pl.ds(pl.multiple_of(head * width, width), width)

    def loads(turn):
        head = head_at(turn)
        return (
            pltpu.make_async_copy(keys_ref.at[:, columns(head)], key_buf.at[turn], load_sem.at[0, turn]),
            pltpu.make_async_copy(weights_ref.at[head], weight_buf.at[turn], load_sem.at[1, turn]),
            pltpu.make_async_copy(values_ref.at[:, columns(head)], value_buf.at[turn], load_sem.at[2, turn]),
        )

    for turn in range(heads):
        for load in loads(turn):
            load.start()

    views_out[...] = jnp.broadcast_to(views_ref[...], views_out.shape)
    here = p * planes + z
    kv_here = c * planes + z
    locals_ = (
        pltpu.make_async_copy(queries_ref.at[:, columns(z)], got_q.at[here], local_sem.at[0]),
        pltpu.make_async_copy(view_keys_ref.at[:, columns(z)], got_kv.at[0, kv_here], local_sem.at[1]),
        pltpu.make_async_copy(view_values_ref.at[:, columns(z)], got_kv.at[1, kv_here], local_sem.at[2]),
    )
    for copy in locals_:
        copy.start()
    got_views[here] = views_out[...]

    pl.semaphore_wait(barrier, planes + 1)

    def z_copy(turn, index):
        plane = head_at(turn)
        source, target = (
            (queries_ref.at[:, columns(plane)], got_q.at[here]),
            (view_keys_ref.at[:, columns(plane)], got_kv.at[0, kv_here]),
            (view_values_ref.at[:, columns(plane)], got_kv.at[1, kv_here]),
            (views_out, got_views.at[here]),
        )[index]
        return remote(
            source, target, z_send.at[index, turn], z_recv.at[index, z], plane * heads + p
        )

    def z_arrived(step, index):
        source, target = ((queries_ref.at[:, columns(z)], got_q.at[here]), (views_out, got_views.at[here]))[
            index == 3
        ]
        remote(
            source, target, z_send.at[index, 0], z_recv.at[index, plane_of(step)], core_peer
        ).wait_recv()

    def y_copy(step, index):
        slot = p * planes + plane_of(step)
        if index == 0:
            source = queries_ref.at[:, columns(z)] if step == 0 else got_q.at[slot]
            target = got_q.at[slot]
        else:
            source = views_out if step == 0 else got_views.at[slot]
            target = got_views.at[slot]
        return remote(source, target, y_send.at[index, step], y_recv.at[index, step], side_peer)

    def c_copy(step, index):
        slot = p * planes + plane_of(step)
        kv_slot = c * planes + plane_of(step)
        target = (
            got_q.at[slot], got_kv.at[0, kv_slot], got_kv.at[1, kv_slot], got_views.at[slot]
        )[index]
        if step == 0:
            source = (
                queries_ref.at[:, columns(z)],
                view_keys_ref.at[:, columns(z)],
                view_values_ref.at[:, columns(z)],
                views_out,
            )[index]
        else:
            source = target
        return remote(source, target, c_send.at[index, step], c_recv.at[index, step], core_peer)

    def cy_copy(step, index):
        slot = (2 * (1 - y) + c) * planes + plane_of(step)
        target = got_q.at[slot] if index == 0 else got_views.at[slot]
        return remote(target, target, cy_send.at[index, step], cy_recv.at[index, step], core_peer)

    for index in (3, 0, 1):
        for turn in (1, 0, 2):
            z_copy(turn, index).start()


    for index in (1, 0):
        y_copy(0, index).start()
    for index in (3, 0, 1, 2):
        c_copy(0, index).start()

    def core_copy(turn):
        return remote(
            core_out.at[turn], core_in.at[turn], core_send.at[turn], core_recv.at[turn], core_peer
        )

    chunk = math.gcd(piece, width)
    chunks = piece // chunk

    def chunk_rows(index):
        return slice(index * chunk, (index + 1) * chunk)

    def side_copy(turn, index):
        at = chunk_rows(index)
        return remote(
            side_out.at[turn, at],
            side_in.at[turn, at],
            side_send.at[turn, index],
            side_recv.at[turn, index],
            side_peer,
        )

    def quarter(at_y, at_c):
        return pl.ds(pl.multiple_of((2 * at_y + at_c) * piece, piece), piece)

    def take_core(turn):
        core_copy(turn).wait_recv()
        side_out[turn] = (
            grad[quarter(1 - y, c), :] + core_in[turn, 1 - y].astype(F32)
        ).astype(BF16)
        for index in range(chunks):
            side_copy(turn, index).start()
        own[turn] = grad[quarter(y, c), :] + core_in[turn, y].astype(F32)

    eye = lax.broadcasted_iota(jnp.int32, (rows, rows), 0) == lax.broadcasted_iota(
        jnp.int32, (rows, rows), 1
    )

    def to_column(row):
        parts = [
            jnp.sum(jnp.where(eye, row[:, at : at + rows], 0.0), axis=1, keepdims=True)
            for at in range(0, row.shape[1], rows)
        ]
        return parts[0] if len(parts) == 1 else jnp.concatenate(parts, axis=0)

    def to_row(column):
        return jnp.sum(jnp.where(eye, column, 0.0), axis=0, keepdims=True)

    over_rows = (((0,), (0,)), ((), ()))
    over_last = (((1,), (1,)), ((), ()))

    def is_early(step):
        return is_end & (plane_of(step) * heads + p == ahead)

    def hand_on(step):
        z_arrived(step, 0)
        y_copy(step, 0).start()
        c_copy(step, 0).start()

    def one_head(turn, carry):
        for load in loads(turn):
            load.wait()
        rate = to_column(rates_ref[pl.ds(head_at(turn), 1), :] * mask_ref[...].astype(F32))
        key_rows = key_buf[turn]
        target_grad[...] = (-rate * value_buf[turn].astype(F32)).astype(BF16)
        pre_gate = jnp.dot(key_rows, weight_buf[turn, 0], preferred_element_type=F32)
        pre_up = jnp.dot(key_rows, weight_buf[turn, 1], preferred_element_type=F32)
        back = lax.dot_general(
            target_grad[...], weight_buf[turn, 2], over_last, preferred_element_type=F32
        )
        sigma = jax.nn.sigmoid(pre_gate)
        activated = pre_gate * sigma
        hidden[...] = (activated * pre_up).astype(BF16)
        grad_gate[...] = (back * pre_up * sigma * (1.0 + pre_gate * (1.0 - sigma))).astype(BF16)
        grad_up[...] = (back * activated).astype(BF16)

        for step in (1, planes - 1):

            @pl.when((turn == 1) & is_early(step))
            def _():
                hand_on(step)

        @pl.when(turn > 0)
        def _():
            take_core(turn - 1)

        grad[0:width] = lax.dot_general(
            key_buf[turn], grad_gate[...], over_rows, preferred_element_type=F32
        )
        grad[width : 2 * width] = lax.dot_general(
            key_buf[turn], grad_up[...], over_rows, preferred_element_type=F32
        )
        grad[2 * width : 3 * width] = lax.dot_general(
            hidden[...], target_grad[...], over_rows, preferred_element_type=F32
        )
        for at_y in range(2):
            core_out[turn, at_y] = grad[quarter(at_y, 1 - c), :].astype(BF16)
        core_copy(turn).start()

        @pl.when(turn == 1)
        def _():
            for step in range(1, planes):
                z_arrived(step, 3)
                y_copy(step, 1).start()
                c_copy(step, 3).start()

        @pl.when((turn == 1) & jnp.logical_not(is_end))
        def _():
            for to in (2, 0, 1):
                z_copy(to, 2).start()

        @pl.when(turn == 2)
        def _():
            for step in range(1, planes):

                @pl.when(jnp.logical_not(is_early(step)))
                def _():
                    hand_on(step)

        return carry

    lax.fori_loop(0, heads, one_head, 0)
    take_core(heads - 1)

    def chain_copy(out_slot, in_slot, index, peer):
        at = chunk_rows(index)
        return remote(
            chain_out.at[out_slot, at],
            chain_in.at[in_slot, at],
            chain_send.at[out_slot, index],
            chain_recv.at[in_slot, index],
            peer,
        )

    hops = ((0, 3, ahead), (3, 5, behind), (1, 4, ahead))

    def pass_on(turn, index):
        side_copy(turn, index).wait_recv()
        at = chunk_rows(index)

        @pl.when(is_end)
        def _():
            chain_out[turn, at] = (own[turn, at] + side_in[turn, at].astype(F32)).astype(BF16)
            chain_copy(turn, turn, index, ahead).start()

        @pl.when(jnp.logical_not(is_end))
        def _():
            taken, given, peer = hops[turn]
            chain_copy(turn, taken, index, peer).wait_recv()
            chain_out[turn, at] = (
                own[turn, at] + side_in[turn, at].astype(F32) + chain_in[taken, at].astype(F32)
            ).astype(BF16)
            chain_copy(turn, given, index, peer).start()

    views = 2 * planes
    def ones(where):
        return where.astype(F32).astype(BF16)

    def rank_rows():
        square = (n * views, n * views)
        low_axis = lax.broadcasted_iota(jnp.int32, square, 0)
        high_axis = lax.broadcasted_iota(jnp.int32, square, 1)

        def order(index):
            slot = index // views
            return slot % planes * heads + slot // planes

        listed = low_axis % views
        side_of = jnp.where(listed < planes, y, 1 - y)
        wanted = listed % planes * heads + 2 * side_of + c
        is_hit = got_views[...].reshape(n * views, rows) == wanted[:, :rows]
        hits = ones(is_hit)
        within = jnp.dot(
            hits,
            ones(
                lax.broadcasted_iota(jnp.int32, (rows, rows), 0)
                < lax.broadcasted_iota(jnp.int32, (rows, rows), 1)
            ),
            preferred_element_type=F32,
        )
        before = (low_axis % views == high_axis % views) & (order(high_axis) < order(low_axis))
        in_column = high_axis // (views * n // 2) == y

        def earlier(table):
            found = jnp.dot(ones(table), hits, preferred_element_type=F32)
            return jnp.sum(found, axis=1, keepdims=True)

        rank_q[...] = jnp.where(is_hit, earlier(before) + within, -1.0).reshape(rank_q.shape)
        rank_kv[...] = jnp.where(is_hit, earlier(before & in_column) + within, -1.0).reshape(
            rank_kv.shape
        )
        counts[...] = jnp.broadcast_to(
            earlier(((low_axis % views == high_axis % views) & in_column)[0:views]), counts.shape
        )

    def spots(ranks, first, sources, view):
        row = jnp.concatenate(
            [ranks[first + source, view : view + 1, :] for source in range(sources)], axis=1
        )
        at = lax.broadcasted_iota(jnp.int32, (rows, sources * rows), 0).astype(F32)
        return ones(at == row)

    def spot_q(group):
        for view in range(planes):
            place_q[group, view * rows : (view + 1) * rows] = spots(
                rank_q, 0, n, group * planes + view
            )

    def arrange_q(group):
        arranged_q[group] = jnp.dot(
            place_q[group], got_q[...].reshape(n * rows, width), preferred_element_type=F32
        ).astype(BF16)

    def spot_kv(group):
        for view in range(planes):
            place_kv[group, view * rows : (view + 1) * rows] = spots(
                rank_kv, y * (n // 2), n // 2, group * planes + view
            )

    def arrange_kv(group, index):
        arranged_kv[group, index] = jnp.dot(
            place_kv[group],
            got_kv[index].reshape(n // 2 * rows, width),
            preferred_element_type=F32,
        ).astype(BF16)

    def view_rows(view):
        return pl.ds(pl.multiple_of(view * rows, rows), rows)

    def weigh(group, turn):
        view = head_at(turn)
        part = view_rows(view)
        scores = lax.dot_general(
            arranged_q[group, part], arranged_kv[group, 0, part], over_last, preferred_element_type=F32
        ) * width ** (-0.5)
        at = group * planes + view
        real = lax.broadcasted_iota(jnp.int32, (rows, rows), 1).astype(F32) < counts[pl.ds(at, 1), :]
        top = jnp.max(jnp.where(real, scores, LOWEST), axis=-1, keepdims=True)
        exps = jnp.where(real, jnp.exp(jnp.where(real, scores - top, 0.0)), 0.0)
        powers[group, turn] = exps.astype(BF16)
        return top, jnp.sum(exps, axis=-1, keepdims=True)

    def attend(group, turn):
        return jnp.dot(
            powers[group, turn],
            arranged_kv[group, 1, view_rows(head_at(turn))],
            preferred_element_type=F32,
        )

    def part_copy(turn, index):
        view = head_at(turn)
        source, target = ((part_out, part_in), (stats_out, stats_in))[index]
        return remote(
            source.at[view],
            target.at[view],
            part_send.at[index, turn],
            part_recv.at[index, turn],
            side_peer,
        )

    for index in range(chunks):
        pass_on(0, index)
    for step in range(planes):
        y_copy(step, 1).wait_recv()
        cy_copy(step, 1).start()
    for step in range(planes):
        cy_copy(step, 1).wait_recv()
        c_copy(step, 3).wait_recv()
    rank_rows()
    spot_q(1)
    pass_on(1, 0)
    spot_q(0)
    pass_on(1, 1)
    spot_kv(1)
    pass_on(1, 2)

    @pl.when(is_end)
    def _():
        for turn in (1, 2):
            z_copy(turn, 2).start()

    spot_kv(0)
    for copy in locals_:
        copy.wait()
    for step in range(1, planes):
        z_arrived(step, 1)
        c_copy(step, 1).start()
    for step in range(planes):
        y_copy(step, 0).wait_recv()
        cy_copy(step, 0).start()
    for step in range(planes):
        c_copy(step, 1).wait_recv()
    arrange_kv(1, 0)
    pass_on(2, 0)
    arrange_kv(0, 0)
    for step in range(planes):
        cy_copy(step, 0).wait_recv()
        c_copy(step, 0).wait_recv()
    arrange_q(1)
    pass_on(2, 1)
    arrange_q(0)
    pass_on(2, 2)

    @pl.when(is_end)
    def _():
        for turn in (0,):
            z_copy(turn, 2).start()

    for turn in range(heads):
        view = head_at(turn)
        top, total = weigh(1, turn)
        stats_out[view, 0:1, :] = to_row(top)
        stats_out[view, 1:2, :] = to_row(total)
        part_copy(turn, 1).start()

    last = heads - 1

    def fresh_copy(way, index):
        slot = 2 * (1 - y) + c if way == 2 else p
        at = chunk_rows(index)
        return remote(
            fresh_ref.at[slot, at],
            fresh_ref.at[slot, at],
            fresh_send.at[way, index],
            fresh_recv.at[way, index],
            side_peer if way == 0 else core_peer,
        )

    for index in range(chunks):
        at = chunk_rows(index)
        side_copy(last, index).wait_recv()
        own[last, at] += side_in[last, at].astype(F32)

        @pl.when(is_end)
        def _():
            chain_copy(0, 5, index, ahead).wait_recv()
            own[last, at] += chain_in[5, at].astype(F32)

        @pl.when(jnp.logical_not(is_end))
        def _():
            for slot in (2, 4):
                chain_copy(0, slot, index, ahead).wait_recv()
            own[last, at] += chain_in[2, at].astype(F32) + chain_in[4, at].astype(F32)

        gradient = own[last, at]
        scaled = gradient * lax.rsqrt(jnp.mean(gradient * gradient, axis=-1, keepdims=True) + EPS)
        start = p * piece + index * chunk
        old = weight_buf[
            last, start // width, pl.ds(pl.multiple_of(start % width, chunk), chunk), :
        ]
        fresh_ref[p, at, :] = (old.astype(F32) - steps_ref[z] * scaled).astype(BF16)
        fresh_copy(0, index).start()
        fresh_copy(1, index).start()

    tops, totals = [], []
    for turn in range(heads):
        top, total = weigh(0, turn)
        tops.append(top)
        totals.append(total)

    for step in range(1, planes):
        z_arrived(step, 2)
        c_copy(step, 2).start()
    for step in range(planes):
        c_copy(step, 2).wait_recv()
    arrange_kv(1, 1)
    for turn in range(heads):
        part_out[head_at(turn)] = attend(1, turn).astype(BF16)
        part_copy(turn, 0).start()
    for index in range(chunks):
        fresh_copy(0, index).wait_recv()
        fresh_copy(2, index).start()
    arrange_kv(0, 1)
    for turn in range(heads):
        attended[turn] = attend(0, turn)

    for index in range(chunks):
        fresh_copy(1, index).wait_recv()
        fresh_copy(2, index).wait_recv()

    fresh = fresh_ref[...].reshape(3 * width, width)
    query_rows = arranged_q[0]
    pre_gate = jnp.dot(query_rows, fresh[0:width], preferred_element_type=F32)
    pre_up = jnp.dot(query_rows, fresh[width : 2 * width], preferred_element_type=F32)
    target_hidden = (pre_gate * jax.nn.sigmoid(pre_gate) * pre_up).astype(BF16)
    fast_out = jnp.dot(target_hidden, fresh[2 * width :], preferred_element_type=F32)
    normed[...] = fast_out * lax.rsqrt(
        jnp.mean(fast_out * fast_out, axis=-1, keepdims=True) + EPS
    )

    def out_copy(turn, plane, source):
        return remote(
            mixed.at[turn],
            out_ref.at[:, columns(source)],
            out_send.at[turn],
            out_recv.at[source],
            plane * heads + p,
        )

    for turn in range(heads):
        view = head_at(turn)
        for index in range(2):
            part_copy(turn, index).wait_recv()
        other_top = to_column(stats_in[view, 0:1, :])
        other_total = to_column(stats_in[view, 1:2, :])
        top = jnp.maximum(tops[turn], other_top)
        scale, other_scale = jnp.exp(tops[turn] - top), jnp.exp(other_top - top)
        weight = 1.0 / (scale * totals[turn] + other_scale * other_total)
        result = (
            normed[pl.ds(pl.multiple_of(view * rows, rows), rows)]
            + attended[turn] * (scale * weight)
            + part_in[view].astype(F32) * (other_scale * weight)
        ).astype(BF16)
        if turn < last:
            mixed[turn] = result
            out_copy(turn, view, z).start()
        else:
            out_ref[:, columns(z)] = result

    for step in range(1, planes):
        out_copy(0, z, plane_of(step)).wait_recv()
    for turn in range(last):
        out_copy(turn, z, z).wait_send()
        for index in range(chunks):
            chain_copy(turn, 0, index, ahead).wait_send()
            fresh_copy(turn, index).wait_send()
    for turn in range(heads):
        core_copy(turn).wait_send()
        for index in range(2):
            part_copy(turn, index).wait_send()
        for index in range(chunks):
            side_copy(turn, index).wait_send()
    for step in range(planes):
        for index in range(4):
            c_copy(step, index).wait_send()
            if step < last:
                z_copy(step, index).wait_send()
        for index in range(2):
            y_copy(step, index).wait_send()
            cy_copy(step, index).wait_send()


def scene(keys, values, rates, mask, weights, steps, queries, view_keys, view_values, views):
    n = lax.axis_size("tokens")
    heads, _, _, width = weights.shape
    rows = queries.shape[0]
    depth = keys.shape[0]
    planes = n // heads
    piece = 3 * width // heads
    chunks = piece // math.gcd(piece, width)
    slots = 2 * planes
    vmem = pl.BlockSpec(memory_space=pltpu.VMEM)
    smem = pl.BlockSpec(memory_space=pltpu.SMEM)
    hbm = pl.BlockSpec(memory_space=pl.ANY)
    dma = pltpu.SemaphoreType.DMA

    def half(*shape):
        return pltpu.VMEM(shape, BF16)

    def single(*shape):
        return pltpu.VMEM(shape, F32)

    return pl.pallas_call(
        functools.partial(scene_kernel, n, heads),
        out_shape=jax.ShapeDtypeStruct((rows, heads * width), BF16),
        in_specs=[hbm, hbm, vmem, vmem, hbm, smem, hbm, hbm, hbm, vmem],
        out_specs=vmem,
        scratch_shapes=[
            half(heads, depth, width),
            half(heads, depth, width),
            half(heads, 3, width, width),
            half(depth, width),
            half(depth, width),
            half(depth, width),
            half(depth, width),
            single(3 * width, width),
            half(heads, 2, piece, width),
            half(heads, 2, piece, width),
            half(heads, piece, width),
            half(heads, piece, width),
            single(heads, piece, width),
            half(3, piece, width),
            half(6, piece, width),
            half(heads, piece, width),
            half(n, rows, width),
            half(2, n // 2, rows, width),
            pltpu.VMEM((slots, rows), jnp.int32),
            pltpu.VMEM((n, slots, rows), jnp.int32),
            single(n, slots, rows),
            single(n, slots, rows),
            single(slots, rows),
            half(2, planes * rows, n * rows),
            half(2, planes * rows, n // 2 * rows),
            half(2, planes * rows, width),
            half(2, 2, planes * rows, width),
            half(2, heads, rows, rows),
            single(planes, rows, width),
            half(planes, rows, width),
            half(planes, rows, width),
            single(planes, 8, rows),
            single(planes, 8, rows),
            half(planes - 1, rows, width),
            single(planes * rows, width),
            dma((3, heads)),
            dma((3,)),
            dma((4, planes)),
            dma((4, planes)),
            dma((2, planes)),
            dma((2, planes)),
            dma((4, planes)),
            dma((4, planes)),
            dma((2, planes)),
            dma((2, planes)),
            dma((heads,)),
            dma((heads,)),
            dma((heads, chunks)),
            dma((heads, chunks)),
            dma((3, chunks)),
            dma((6, chunks)),
            dma((3, chunks)),
            dma((3, chunks)),
            dma((2, heads)),
            dma((2, heads)),
            dma((planes - 1,)),
            dma((planes,)),
        ],
        compiler_params=pltpu.CompilerParams(
            collective_id=1, has_side_effects=True, vmem_limit_bytes=63 * 1024 * 1024
        ),
    )(keys, values, rates, mask, weights, steps, queries, view_keys, view_values, views)


def on_device(
    update_keys,
    update_values,
    update_rates,
    update_mask,
    fast_weights,
    step_sizes,
    target_queries,
    target_keys,
    target_values,
    target_views,
):
    n = lax.axis_size("tokens")
    heads = fast_weights.shape[0]
    if heads == 4 and n == heads * heads:
        return scene(
            update_keys,
            update_values,
            update_rates.T,
            update_mask[None, :],
            fast_weights,
            step_sizes,
            target_queries,
            target_keys,
            target_values,
            target_views[None, :],
        )
    rates = update_rates * update_mask.astype(F32)[:, None]
    return exchange(
        update_keys,
        update_values,
        rates,
        fast_weights,
        step_sizes,
        target_queries,
        target_keys,
        target_values,
        target_views[None, :],
    )


def solution(mesh):
    rows = P(("groups", "tokens"), None)
    flat = P(("groups", "tokens"))
    return jax.shard_map(
        on_device,
        mesh=mesh,
        in_specs=(rows, rows, rows, flat, P(), P(), rows, rows, rows, flat),
        out_specs=rows,
        check_vma=False,
    )
```
